32 devices in a mesh: group: 4 (over x, core), replica: 8 (over z, y).
Axes of the slice: x: 2, y: 2, z: 4, core: 2. Of those that a mesh axis runs over, the one named last changes fastest.
Arguments:
- activations: float32 [16, 1024, 768], P('replica', 'group'), may hold values from -6 to 6
- out_grad: float32 [16, 1024, 768], P('replica', 'group'), may hold values from -6 to 6
- picture_ids: int32 [16, 1024], P('replica'), may hold values from -1 to 9, as said below
- ln1_gain: float32 [768], P('group'), may hold values from 0.5 to 1.5
- ln1_bias: float32 [768], P('group'), may hold values from -3 to 3
- w_query: float32 [768, 768], P(None, 'group'), may hold values from -0.3125 to 0.3125
- q_bias: float32 [768], P('group'), may hold values from -3 to 3
- w_key: float32 [768, 768], P(None, 'group'), may hold values from -0.3125 to 0.3125
- w_value: float32 [768, 768], P(None, 'group'), may hold values from -0.21875 to 0.21875
- v_bias: float32 [768], P('group'), may hold values from -3 to 3
- w_out: float32 [768, 768], P('group'), may hold values from -1.75 to 1.75
- out_bias: float32 [768], P('group'), may hold values from -3 to 3
- ln2_gain: float32 [768], P('group'), may hold values from 0.5 to 1.5
- ln2_bias: float32 [768], P('group'), may hold values from -3 to 3
- w_fc1: float32 [768, 3072], P(None, 'group'), may hold values from -0.21875 to 0.21875
- fc1_bias: float32 [3072], P('group'), may hold values from -3 to 3
- w_fc2: float32 [3072, 768], P('group'), may hold values from -0.109375 to 0.109375
- fc2_bias: float32 [768], P('group'), may hold values from -3 to 3
Outputs:
- output: float32 [16, 1024, 768], P('replica', 'group')
- grad_input: float32 [16, 1024, 768], P('replica', 'group')
- grad_ln1_gain: float32 [768], P('group')
- grad_ln1_bias: float32 [768], P('group')
- grad_w_query: float32 [768, 768], P(None, 'group')
- grad_q_bias: float32 [768], P('group')
- grad_w_key: float32 [768, 768], P(None, 'group')
- grad_w_value: float32 [768, 768], P(None, 'group')
- grad_v_bias: float32 [768], P('group')
- grad_w_out: float32 [768, 768], P('group')
- grad_out_bias: float32 [768], P('group')
- grad_ln2_gain: float32 [768], P('group')
- grad_ln2_bias: float32 [768], P('group')
- grad_w_fc1: float32 [768, 3072], P(None, 'group')
- grad_fc1_bias: float32 [3072], P('group')
- grad_w_fc2: float32 [3072, 768], P('group')
- grad_fc2_bias: float32 [768], P('group')
The draws below stay inside these ranges and needn't reach their ends.
Inputs may be any that keep to these rules, and one draw needn't show every extreme that they name: `picture_ids`: each row holds whole pictures numbered 0, 1, 2 and so on from its start, each of 100 to 1024 patches, followed by padding marked -1.
All inputs are finite; a program needn't handle non-finite values.
Results may differ from the reference program's by a relative error of at most 0.04.
Values may be sent and summed in bfloat16 or wider, within the bound.
No kernel may reach another device: no remote copies, remote signals or barrier semaphores. Data moves between devices by JAX's collectives and lax.ppermute only.
A program may use at most 256 MiB of HBM per device.

```python
import math
import jax
import jax.numpy as jnp
from jax import lax

D = 768
HEADS = 12
HEAD_DIM = 64
FF = 3072
ROW_LEN = 1024
MIN_PIC = 100
ROW_COUNT = 16


def draw_picture_ids(key, part):
    seeded = jax.random.fold_in(key, 11)
    first_key, second_key = jax.random.split(seeded)
    pictures = ROW_LEN // MIN_PIC
    first_len = jax.random.randint(first_key, (ROW_COUNT, pictures), MIN_PIC, ROW_LEN + 1)
    second_len = jax.random.randint(second_key, (ROW_COUNT, pictures), MIN_PIC, ROW_LEN + 1)
    lengths = jnp.minimum(first_len, second_len)
    row_index = jnp.arange(ROW_COUNT)[:, None]
    column = jnp.arange(pictures)[None, :]
    lengths = jnp.where(row_index == 0, jnp.where(column == 0, ROW_LEN, MIN_PIC), lengths)
    lengths = jnp.where(row_index == ROW_COUNT - 1, MIN_PIC, lengths)
    ends = jnp.cumsum(lengths, axis=1)
    kept = ends <= ROW_LEN
    position = jnp.arange(ROW_LEN)[None, :, None]
    finished = jnp.sum((kept[:, None, :] & (position >= ends[:, None, :])).astype(jnp.int32), axis=2)
    filled = jnp.sum(jnp.where(kept, lengths, 0), axis=1)
    inside = jnp.arange(ROW_LEN)[None, :] < filled[:, None]
    return jnp.where(inside, finished, -1).astype(jnp.int32)


def block_levels(key, extent, cuts, low, high):
    loudness, own = 1.0, jax.random.fold_in(key, 6)
    for dim, blocks in cuts:
        steps = jnp.exp(jax.random.uniform(jax.random.fold_in(own, dim), (blocks,), jnp.float32, low / len(cuts), high / len(cuts)))
        loudness = loudness * jnp.repeat(steps, extent[dim] // blocks).reshape([-1 if axis == dim else 1 for axis in range(len(extent))])
    return loudness


def scatter_about(own_key, extent, width, most, cuts=(), held_as=jnp.bfloat16):
    entries = jax.random.normal(own_key, extent, jnp.float32) * width
    if len(cuts) > 0:
        entries = block_levels(own_key, extent, cuts, -0.22, 0.18) * entries
    return jnp.clip(entries, min=-most, max=most).astype(held_as)


def setup_inputs(seed: int = 0) -> dict:
    key_list = jax.random.split(jax.random.key(seed), 19)
    activations = scatter_about(key_list[0], (ROW_COUNT, ROW_LEN, D), 1.0, 6.0, ((0, 8), (1, 4)), jnp.float32)
    out_grad = scatter_about(key_list[1], (ROW_COUNT, ROW_LEN, D), 1.0, 6.0, ((0, 8), (1, 4)), jnp.float32)
    picture_ids = draw_picture_ids(jax.random.fold_in(key_list[18], 71), 0)
    ln1_gain = jnp.clip(1.0 + 0.1 * jax.random.normal(key_list[3], (D,), jnp.float32), 0.5, 1.5)
    ln1_bias = scatter_about(key_list[4], (D,), 0.3, 3.0, ((0, 4),), jnp.float32)
    w_query = scatter_about(key_list[5], (D, D), (D // 2) ** -0.5, 0.3125, ((1, 4),), jnp.float32)
    q_bias = scatter_about(key_list[6], (D,), 0.3, 3.0, ((0, 4),), jnp.float32)
    w_key = scatter_about(key_list[7], (D, D), (D // 2) ** -0.5, 0.3125, ((1, 4),), jnp.float32)
    w_value = scatter_about(key_list[8], (D, D), D ** -0.5, 0.21875, ((1, 4),), jnp.float32)
    v_bias = scatter_about(key_list[9], (D,), 0.3, 3.0, ((0, 4),), jnp.float32)
    w_out = scatter_about(key_list[10], (D, D), (max(D // 64, 8)) ** -0.5, 1.75, ((0, 4),), jnp.float32)
    out_bias = scatter_about(key_list[11], (D,), 0.3, 3.0, ((0, 4),), jnp.float32)
    ln2_gain = jnp.clip(1.0 + 0.1 * jax.random.normal(key_list[12], (D,), jnp.float32), 0.5, 1.5)
    ln2_bias = scatter_about(key_list[13], (D,), 0.3, 3.0, ((0, 4),), jnp.float32)
    w_fc1 = scatter_about(key_list[14], (D, FF), D ** -0.5, 0.21875, ((1, 4),), jnp.float32)
    fc1_bias = scatter_about(key_list[15], (FF,), 0.3, 3.0, ((0, 4),), jnp.float32)
    w_fc2 = scatter_about(key_list[16], (FF, D), FF ** -0.5, 0.109375, ((0, 4),), jnp.float32)
    fc2_bias = scatter_about(key_list[17], (D,), 0.3, 3.0, ((0, 4),), jnp.float32)
    return dict(activations=activations, out_grad=out_grad, picture_ids=picture_ids, ln1_gain=ln1_gain, ln1_bias=ln1_bias, w_query=w_query, q_bias=q_bias, w_key=w_key, w_value=w_value, v_bias=v_bias, w_out=w_out, out_bias=out_bias, ln2_gain=ln2_gain, ln2_bias=ln2_bias, w_fc1=w_fc1, fc1_bias=fc1_bias, w_fc2=w_fc2, fc2_bias=fc2_bias)


@jax.custom_vjp
def low(v):
    return lax.optimization_barrier(v.astype(jnp.bfloat16)).astype(jnp.float32)

@jax.custom_vjp
def low_back(v):
    return v

def low_keep(v):
    return (low(v), None)

def low_pass(kept, grad):
    return (grad,)

def back_keep(v):
    return (v, None)

def back_low(kept, grad):
    return (low(grad),)
low.defvjp(low_keep, low_pass)
low_back.defvjp(back_keep, back_low)
EPS = 1e-06
MASKED = -1e+30
PRECISE = lax.Precision.HIGHEST

def project(left, right):
    return jnp.einsum('...d,de->...e', left, right, precision=PRECISE, preferred_element_type=jnp.float32)

def normalize(values, gain, shift):
    centred = values - lax.optimization_barrier(jnp.mean(values, axis=-1, keepdims=True))
    variance = lax.optimization_barrier(jnp.mean(centred * centred, axis=-1, keepdims=True))
    return centred * lax.rsqrt(variance + EPS) * gain + shift

def block_rows(params, inputs, picture_rows):
    gain_one, shift_one, w_query, q_bias, w_key, w_value, v_bias, w_out, out_bias, gain_two, shift_two, w_fc1, fc1_bias, w_fc2, fc2_bias = params
    row_block = inputs.shape[0]
    head_shape = (row_block, ROW_LEN, HEADS, HEAD_DIM)
    normed_one = low(normalize(inputs, gain_one, shift_one))
    queries = low(low_back(project(normed_one, w_query) + q_bias))
    keys_new = low(low_back(project(normed_one, w_key)))
    values_new = low(low_back(project(normed_one, w_value) + v_bias))
    scores = jnp.einsum('rqhe,rkhe->rhqk', queries.reshape(head_shape), keys_new.reshape(head_shape), precision=PRECISE, preferred_element_type=jnp.float32) * HEAD_DIM ** (-0.5)
    scores = low_back(scores)
    allowed = picture_rows[:, None, :, None] == picture_rows[:, None, None, :]
    scores = jnp.where(allowed, scores, MASKED)
    row_top = lax.optimization_barrier(jnp.max(scores, axis=-1, keepdims=True))
    exponent = jnp.exp(scores - row_top)
    probability = low(exponent / lax.optimization_barrier(jnp.sum(exponent, axis=-1, keepdims=True)))
    attended = jnp.einsum('rhqk,rkhe->rqhe', probability, values_new.reshape(head_shape), precision=PRECISE, preferred_element_type=jnp.float32)
    attended = low(low_back(attended.reshape(row_block, ROW_LEN, D)))
    middle = inputs + low_back(project(attended, w_out) + out_bias)
    normed_two = low(normalize(middle, gain_two, shift_two))
    hidden = low_back(project(normed_two, w_fc1) + fc1_bias)
    activated = low(jax.nn.gelu(hidden, approximate=True))
    return middle + low_back(project(activated, w_fc2) + fc2_bias)

def forward(inputs, params, picture_ids):
    rounded = tuple((low(item) for item in params))
    block_size = math.gcd(ROW_COUNT, 4)
    step_count = ROW_COUNT // block_size
    checked = jax.checkpoint(block_rows)

    def one_step(carry, pieces):
        return (carry, checked(rounded, pieces[0], pieces[1]))
    carry_out, outputs = lax.scan(one_step, jnp.zeros((), jnp.float32), (inputs.reshape(step_count, block_size, ROW_LEN, D), picture_ids.reshape(step_count, block_size, ROW_LEN)))
    return outputs.reshape(ROW_COUNT, ROW_LEN, D)

def reference(activations, out_grad, picture_ids, ln1_gain, ln1_bias, w_query, q_bias, w_key, w_value, v_bias, w_out, out_bias, ln2_gain, ln2_bias, w_fc1, fc1_bias, w_fc2, fc2_bias):
    params = (ln1_gain, ln1_bias, w_query, q_bias, w_key, w_value, v_bias, w_out, out_bias, ln2_gain, ln2_bias, w_fc1, fc1_bias, w_fc2, fc2_bias)

    def run_layer(inputs, weights):
        return forward(inputs, weights, picture_ids)
    output, pullback = jax.vjp(run_layer, activations, params)
    valid_rows = (picture_ids >= 0).astype(jnp.float32)
    grad_input, grads = pullback(out_grad * valid_rows[:, :, None])
    return (output, grad_input, grads[0], grads[1], grads[2], grads[3], grads[4], grads[5], grads[6], grads[7], grads[8], grads[9], grads[10], grads[11], grads[12], grads[13], grads[14])
```

```python
import jax
import jax.numpy as jnp
from jax import lax
from jax.experimental import pallas as pl
from jax.experimental.pallas import tpu as pltpu
from jax.sharding import PartitionSpec as P

HEADS = 12
HEAD_DIM = 64
EPS = 1e-06
MASKED = -1e30
BF = jnp.bfloat16
F32 = jnp.float32
PAIR = 2 * HEAD_DIM
Q_BLOCK = 256


def to_float(values):
    return values.astype(F32)


def normalize(values):
    centred = values - jnp.mean(values, axis=-1, keepdims=True)
    inverse = lax.rsqrt(jnp.mean(centred * centred, axis=-1, keepdims=True) + EPS)
    return (centred * inverse, inverse)


def norm_back(grad_hat, normed_hat, inverse):
    return inverse * (
        grad_hat
        - jnp.mean(grad_hat, axis=-1, keepdims=True)
        - normed_hat * jnp.mean(grad_hat * normed_hat, axis=-1, keepdims=True)
    )


def gelu_tanh(values):
    return jax.nn.gelu(values, approximate=True)


def dot_nn(left, right):
    return jnp.dot(left, right, preferred_element_type=F32)


def dot_nt(left, right):
    return lax.dot_general(left, right, (((1,), (1,)), ((), ())), preferred_element_type=F32)


def dot_tn(left, right):
    return lax.dot_general(left, right, (((0,), (0,)), ((), ())), preferred_element_type=F32)


def attend_kernel(q_ref, k_ref, v_ref, iq_ref, ik_ref, out_ref, prob_ref):
    first = lax.broadcasted_iota(jnp.int32, (1, PAIR), 1) < HEAD_DIM
    queries = q_ref[...] * jnp.asarray(HEAD_DIM**-0.5, BF)
    allowed = iq_ref[...] == ik_ref[...]
    parts = []
    for head in range(2):
        lanes = first if head == 0 else ~first
        scores = dot_nt(jnp.where(lanes, queries, jnp.zeros_like(queries)), k_ref[...])
        scores = jnp.where(allowed, scores, MASKED)
        exponent = jnp.exp(scores - jnp.max(scores, axis=1, keepdims=True))
        scale = 1.0 / jnp.sum(exponent, axis=1, keepdims=True)
        probability = (exponent * scale).astype(BF)
        prob_ref[head] = probability
        parts.append(dot_nn(probability, v_ref[...]))
    out_ref[...] = jnp.where(first, parts[0], parts[1]).astype(BF)


def attend(queries, keys, values, ids):
    length, width = queries.shape
    pairs = width // PAIR
    query_spec = pl.BlockSpec((Q_BLOCK, PAIR), lambda p, i: (i, p))
    key_spec = pl.BlockSpec((length, PAIR), lambda p, i: (0, p))
    return pl.pallas_call(
        attend_kernel,
        grid=(pairs, length // Q_BLOCK),
        in_specs=[
            query_spec,
            key_spec,
            key_spec,
            pl.BlockSpec((Q_BLOCK, 1), lambda p, i: (i, 0)),
            pl.BlockSpec((1, length), lambda p, i: (0, 0)),
        ],
        out_specs=[query_spec, pl.BlockSpec((2, Q_BLOCK, length), lambda p, i: (p, i, 0))],
        out_shape=[
            jax.ShapeDtypeStruct((length, width), BF),
            jax.ShapeDtypeStruct((2 * pairs, length, length), BF),
        ],
        compiler_params=pltpu.CompilerParams(vmem_limit_bytes=40 << 20),
        name="attend",
    )(queries, keys, values, ids[:, None], ids[None, :])


def attend_back_kernel(
    q_ref, k_ref, v_ref, out_ref, grad_ref, prob_ref, dq_ref, dk_ref, dv_ref, key_sum, value_sum
):
    step = pl.program_id(1)
    first = lax.broadcasted_iota(jnp.int32, (1, PAIR), 1) < HEAD_DIM
    queries, keys, grad = q_ref[...], k_ref[...], grad_ref[...]
    product = to_float(grad) * to_float(out_ref[...])

    @pl.when(step == 0)
    def _():
        key_sum[...] = jnp.zeros_like(key_sum)
        value_sum[...] = jnp.zeros_like(value_sum)

    grad_queries = None
    for head in range(2):
        lanes = first if head == 0 else ~first
        grad_head = jnp.where(lanes, grad, jnp.zeros_like(grad))
        query_head = jnp.where(lanes, queries, jnp.zeros_like(queries))
        key_head = jnp.where(lanes, keys, jnp.zeros_like(keys))
        centre = jnp.sum(jnp.where(lanes, product, 0.0), axis=1, keepdims=True)
        probability = prob_ref[head]
        grad_probs = dot_nt(grad_head, v_ref[...])
        grad_scores = (to_float(probability) * (grad_probs - centre)).astype(BF)
        part = dot_nn(grad_scores, key_head)
        grad_queries = part if head == 0 else grad_queries + part
        key_sum[...] += dot_tn(grad_scores, query_head)
        value_sum[...] += dot_tn(probability, grad_head)
    dq_ref[...] = (grad_queries * HEAD_DIM**-0.5).astype(BF)

    @pl.when(step == pl.num_programs(1) - 1)
    def _():
        dk_ref[...] = (key_sum[...] * HEAD_DIM**-0.5).astype(BF)
        dv_ref[...] = value_sum[...].astype(BF)


def attend_back(queries, keys, values, attended, grad_attended, probability):
    length, width = queries.shape
    query_spec = pl.BlockSpec((Q_BLOCK, PAIR), lambda p, i: (i, p))
    key_spec = pl.BlockSpec((length, PAIR), lambda p, i: (0, p))
    return pl.pallas_call(
        attend_back_kernel,
        grid=(width // PAIR, length // Q_BLOCK),
        in_specs=[
            query_spec,
            key_spec,
            key_spec,
            query_spec,
            query_spec,
            pl.BlockSpec((2, Q_BLOCK, length), lambda p, i: (p, i, 0)),
        ],
        out_specs=[query_spec, key_spec, key_spec],
        out_shape=[jax.ShapeDtypeStruct((length, width), BF)] * 3,
        scratch_shapes=[pltpu.VMEM((length, PAIR), F32)] * 2,
        compiler_params=pltpu.CompilerParams(vmem_limit_bytes=40 << 20),
        name="attend_back",
    )(queries, keys, values, attended, grad_attended, probability)


def swap(values, axis, size, bit):
    return lax.ppermute(values, axis, [(i, i ^ bit) for i in range(size)])


def core_swap(values):
    return swap(values, "group", 4, 1)


def chip_swap(values):
    return swap(values, "group", 4, 2)


def replica_sum(rows, size):
    index = lax.axis_index("replica")
    bits = []
    bit = 1
    while bit < size:
        bits.append(bit)
        bit *= 2
    for bit in bits:
        half = rows.shape[0] // 2
        mine = (index // bit) % 2
        sent = lax.dynamic_slice_in_dim(rows, (1 - mine) * half, half, 0)
        kept = lax.dynamic_slice_in_dim(rows, mine * half, half, 0)
        rows = (to_float(kept) + to_float(swap(sent, "replica", size, bit))).astype(BF)
    for bit in reversed(bits):
        mine = (index // bit) % 2
        other = swap(rows, "replica", size, bit)
        rows = jnp.concatenate(
            [jnp.where(mine == 0, rows, other), jnp.where(mine == 0, other, rows)], axis=0
        )
    return rows


def per_device(
    replicas,
    activations,
    out_grad,
    picture_ids,
    ln1_gain,
    ln1_bias,
    w_query,
    q_bias,
    w_key,
    w_value,
    v_bias,
    w_out,
    out_bias,
    ln2_gain,
    ln2_bias,
    w_fc1,
    fc1_bias,
    w_fc2,
    fc2_bias,
):
    row_block, quarter, width = activations.shape
    assert row_block == 2
    shard = w_query.shape[1]
    half = 2 * quarter
    group = lax.axis_index("group")
    core = group % 2

    def own_row(values):
        return lax.dynamic_index_in_dim(values, core, 0, keepdims=False)

    def other_row(values):
        return lax.dynamic_index_in_dim(values, 1 - core, 0, keepdims=False)

    def home(values):
        kept, sent = values[:quarter], values[quarter:]
        got = core_swap(sent)
        return jnp.stack([jnp.where(core == 0, kept, got), jnp.where(core == 0, got, kept)])

    small = jnp.concatenate(
        [ln1_gain, ln1_bias, out_bias, ln2_gain, ln2_bias, fc2_bias, q_bias, v_bias, fc1_bias]
    ).astype(BF)
    small_chip = chip_swap(small)
    both = jnp.stack([small, small_chip])
    both_core = core_swap(both)
    shards = [both[0], both_core[0], both[1], both_core[1]]

    def full(position):
        part = jnp.stack([s[position * shard : (position + 1) * shard] for s in shards])
        return jnp.concatenate(
            [lax.dynamic_index_in_dim(part, group ^ i, 0) for i in range(4)], axis=0
        ).reshape(-1)

    gain_one, shift_one, bias_out, gain_two, shift_two, bias_fc2 = [
        to_float(full(i)) for i in range(6)
    ]

    def pair(start, size):
        return to_float(
            jnp.concatenate([shards[0][start : start + size], shards[1][start : start + size]])
        )

    bias_query = pair(6 * shard, shard)
    bias_value = pair(7 * shard, shard)
    bias_fc1 = pair(8 * shard, fc1_bias.shape[0])

    inputs = jnp.concatenate([own_row(activations), core_swap(other_row(activations))], axis=0)
    own_ids = lax.dynamic_slice_in_dim(picture_ids, group * quarter, quarter, 1)
    grad_home = out_grad * (own_ids >= 0).astype(F32)[..., None]
    grad_out = jnp.concatenate([own_row(grad_home), core_swap(other_row(grad_home))], axis=0)
    row_ids = own_row(picture_ids).reshape(4, quarter)
    ids = jnp.concatenate(
        [lax.dynamic_index_in_dim(row_ids, group ^ i, 0, keepdims=False) for i in range(4)]
    )

    hat_one, inverse_one = normalize(inputs)
    normed_own = (hat_one * gain_one + shift_one).astype(BF)
    normed_one = jnp.concatenate([normed_own, chip_swap(normed_own)], axis=0)
    grad_mlp_own = grad_out.astype(BF)
    grad_mlp = jnp.concatenate([grad_mlp_own, chip_swap(grad_mlp_own)], axis=0)

    projections = jnp.stack([w_query, w_key, w_value]).astype(BF)
    partner = core_swap(projections)
    w_qkv = jnp.concatenate(
        [part for i in range(3) for part in (projections[i], partner[i])], axis=1
    )
    down = jnp.concatenate([w_out, w_fc2], axis=0).astype(BF)
    down_partner = core_swap(down)
    out_full = jnp.concatenate([down[:shard], down_partner[:shard]], axis=0)
    fc2_full = jnp.concatenate([down[shard:], down_partner[shard:]], axis=0)
    up = w_fc1.astype(BF)
    fc1_full = jnp.concatenate([up, core_swap(up)], axis=1)

    bias_qkv = jnp.concatenate([bias_query, jnp.zeros_like(bias_query), bias_value])
    qkv = (dot_nn(normed_one, w_qkv) + bias_qkv).astype(BF)
    span = 2 * shard
    queries, keys, values = qkv[:, :span], qkv[:, span : 2 * span], qkv[:, 2 * span :]
    attended, probability = attend(queries, keys, values, ids)
    branch = dot_nn(attended, out_full)
    branch_other = chip_swap(branch[half:].astype(BF))
    middle = inputs + (branch[:half] + to_float(branch_other) + bias_out)

    hat_two, inverse_two = normalize(middle)
    normed_two_own = (hat_two * gain_two + shift_two).astype(BF)
    normed_two = jnp.concatenate([normed_two_own, chip_swap(normed_two_own)], axis=0)
    hidden = dot_nn(normed_two, fc1_full) + bias_fc1
    gelu_value, gelu_pull = jax.vjp(gelu_tanh, hidden)
    activated = gelu_value.astype(BF)
    grad_hidden = gelu_pull(dot_nt(grad_mlp, fc2_full))[0].astype(BF)
    grad_normed = dot_nt(grad_hidden, fc1_full)
    grad_normed_other = chip_swap(grad_normed[half:].astype(BF))
    grad_normed_two = grad_normed[:half] + to_float(grad_normed_other)
    mlp = dot_nn(activated, fc2_full)
    mlp_other = chip_swap(mlp[half:].astype(BF))
    output = home(middle + (mlp[:half] + to_float(mlp_other) + bias_fc2))

    grad_middle = grad_out + norm_back(grad_normed_two * gain_two, hat_two, inverse_two)
    grad_branch_own = grad_middle.astype(BF)
    grad_branch = jnp.concatenate([grad_branch_own, chip_swap(grad_branch_own)], axis=0)

    grad_fc1 = dot_tn(normed_two, grad_hidden).astype(BF)
    grad_fc2 = dot_tn(activated, grad_mlp).astype(BF)
    wide = fc1_full.shape[1] // 2
    fc_kept = jnp.concatenate([grad_fc1[:, :wide], grad_fc2[:wide]], axis=0)
    fc_sent = jnp.concatenate([grad_fc1[:, wide:], grad_fc2[wide:]], axis=0)
    fc_rows = (to_float(fc_kept) + to_float(core_swap(fc_sent))).astype(BF)
    fc_rows = replica_sum(fc_rows, replicas)
    grad_w_fc1 = to_float(fc_rows[:width])
    grad_w_fc2 = to_float(fc_rows[width:])

    grad_attended = dot_nt(grad_branch, out_full).astype(BF)
    grad_queries, grad_keys, grad_values = attend_back(
        queries, keys, values, attended, grad_attended, probability
    )
    grad_qkv = jnp.concatenate([grad_queries, grad_keys, grad_values], axis=1)
    grad_first = dot_nt(grad_qkv, w_qkv)
    grad_first_other = chip_swap(grad_first[half:].astype(BF))
    grad_normed_one = grad_first[:half] + to_float(grad_first_other)
    grad_input = home(
        grad_middle + norm_back(grad_normed_one * gain_one, hat_one, inverse_one)
    )

    grad_w_qkv = dot_tn(grad_qkv, normed_one).astype(BF)
    grad_w_out = dot_tn(attended, grad_branch).astype(BF)

    def total(values):
        return jnp.sum(to_float(values), axis=0)

    wide_sums = jnp.stack(
        [
            jnp.sum(grad_normed_one * hat_one, axis=0),
            jnp.sum(grad_normed_one, axis=0),
            total(grad_branch_own),
            jnp.sum(grad_normed_two * hat_two, axis=0),
            jnp.sum(grad_normed_two, axis=0),
            total(grad_mlp_own),
        ]
    ).astype(BF)
    by_shard = jnp.transpose(wide_sums.reshape(6, 4, shard), (1, 0, 2))

    def shard_of(i):
        return lax.dynamic_index_in_dim(by_shard, group ^ i, 0, keepdims=False)

    chip_part = chip_swap(jnp.stack([shard_of(2), shard_of(3)]))
    small_own = to_float(shard_of(0)) + to_float(chip_part[0])
    small_core = to_float(shard_of(1)) + to_float(chip_part[1])
    bias_sums = total(grad_queries), total(grad_values), total(grad_hidden)

    def side(index):
        return [
            s[index * (s.shape[0] // 2) : (index + 1) * (s.shape[0] // 2)] for s in bias_sums
        ]

    kept_small = jnp.concatenate([small_own.reshape(-1)] + side(0))
    sent_small = jnp.concatenate([small_core.reshape(-1)] + side(1)).astype(BF)
    small_rows = kept_small.shape[0] // width
    padding = -small_rows % replicas

    def padded(values):
        return jnp.pad(values.reshape(small_rows, width), ((0, padding), (0, 0)))

    def arranged(index, vector):
        rows = [grad_w_out[index * shard : (index + 1) * shard]]
        for i in range(3):
            start = i * span + index * shard
            rows.append(grad_w_qkv[start : start + shard])
        rows.append(padded(vector).astype(BF))
        return jnp.concatenate(rows, axis=0)

    attention_rows = (
        to_float(arranged(0, kept_small)) + to_float(core_swap(arranged(1, sent_small)))
    ).astype(BF)
    attention_rows = replica_sum(attention_rows, replicas)
    sums = to_float(attention_rows[4 * shard : 4 * shard + small_rows]).reshape(-1)

    def vector(position):
        return sums[position * shard : (position + 1) * shard]

    def weight(index):
        return to_float(attention_rows[index * shard : (index + 1) * shard])

    return (
        output,
        grad_input,
        vector(0),
        vector(1),
        weight(1).T,
        vector(6),
        weight(2).T,
        weight(3).T,
        vector(7),
        weight(0),
        vector(2),
        vector(3),
        vector(4),
        grad_w_fc1,
        sums[8 * shard :],
        grad_w_fc2,
        vector(5),
    )


def solution(mesh):
    replicas = mesh.shape["replica"]
    assert mesh.shape["group"] == 4
    patches = P("replica", "group", None)
    vector = P("group")
    columns = P(None, "group")
    rows = P("group", None)

    def program(*arguments):
        return per_device(replicas, *arguments)

    return jax.shard_map(
        program,
        mesh=mesh,
        in_specs=(
            patches,
            patches,
            P("replica", None),
            vector,
            vector,
            columns,
            vector,
            columns,
            columns,
            vector,
            rows,
            vector,
            vector,
            vector,
            columns,
            vector,
            rows,
            vector,
        ),
        out_specs=(
            patches,
            patches,
            vector,
            vector,
            columns,
            vector,
            columns,
            columns,
            vector,
            rows,
            vector,
            vector,
            vector,
            columns,
            vector,
            rows,
            vector,
        ),
        check_vma=False,
    )
```

```python
import jax
import jax.numpy as jnp
from jax import lax
from jax.experimental import pallas as pl
from jax.experimental.pallas import tpu as pltpu
from jax.sharding import PartitionSpec as P

HEAD_DIM = 64
EPS = 1e-06
MASKED = -1e30
BF = jnp.bfloat16
F32 = jnp.float32
LANES = 128
LOG2_E = 1.4426950408889634
GELU_A = 0.7978845608028654
GELU_B = 0.044715
BLOCK = 256


def to_float(values):
    return values.astype(F32)


def dot_nn(left, right):
    return jnp.dot(left, right, preferred_element_type=F32)


def dot_nt(left, right):
    return lax.dot_general(left, right, (((1,), (1,)), ((), ())), preferred_element_type=F32)


def dot_tn(left, right):
    return lax.dot_general(left, right, (((0,), (0,)), ((), ())), preferred_element_type=F32)


def normalize(values):
    centred = values - jnp.mean(values, axis=-1, keepdims=True)
    inverse = lax.rsqrt(jnp.mean(centred * centred, axis=-1, keepdims=True) + EPS)
    return (centred * inverse, inverse)


def norm_back(grad_hat, normed_hat, inverse):
    return inverse * (
        grad_hat
        - jnp.mean(grad_hat, axis=-1, keepdims=True)
        - normed_hat * jnp.mean(grad_hat * normed_hat, axis=-1, keepdims=True)
    )


def column_sum(values):
    return jnp.sum(to_float(values), axis=0, keepdims=True)


def shape(dims, dtype):
    return jax.ShapeDtypeStruct(dims, dtype)


IN_VMEM = pl.BlockSpec(memory_space=pltpu.VMEM)


def launch(body, name, ins, outs, grid=(1,), scratch=(), flops=0, exps=0, scalar=None, limit=12):
    in_specs = [IN_VMEM if spec is None else spec for _, spec in ins]
    out_specs = [IN_VMEM if spec is None else spec for _, spec in outs]
    arrays = [
        a if spec is None else pltpu.with_memory_space_constraint(a, pltpu.HBM) for a, spec in ins
    ]
    moved = sum(a.size * a.dtype.itemsize for a in arrays)
    moved += sum(o.size * o.dtype.itemsize for o, _ in outs)
    count = 0
    if scalar is not None:
        arrays, count = [scalar] + arrays, 1
    return pl.pallas_call(
        body,
        grid_spec=pltpu.PrefetchScalarGridSpec(
            num_scalar_prefetch=count,
            grid=grid,
            in_specs=in_specs,
            out_specs=out_specs,
            scratch_shapes=list(scratch),
        ),
        out_shape=[o if spec is None else pltpu.HBM(o.shape, o.dtype) for o, spec in outs],
        cost_estimate=pl.CostEstimate(flops=flops, transcendentals=exps, bytes_accessed=moved),
        compiler_params=pltpu.CompilerParams(vmem_limit_bytes=limit << 20),
        name=name,
    )(*arrays)


def step_rows(size=BLOCK):
    return pl.ds(pl.multiple_of(pl.program_id(0) * size, size), size)


def held(*dims):
    return pl.BlockSpec(dims, lambda *_: (0,) * len(dims), pipeline_mode=pl.Buffered(1))


def by_step(*dims):
    return pl.BlockSpec(dims, lambda i, *_: (i,) + (0,) * (len(dims) - 1))


def row_spec(quarter, width, other):
    return pl.BlockSpec(
        (None, quarter, width), lambda i, c: ((1 - c[0]) if other else c[0], 0, 0)
    )


def split_inputs(activations, small, position, shard, padded):
    _, quarter, width = activations.shape
    extra = 16

    def body(at_ref, own_in, other_ref, small_ref, chip_ref, diagonal_ref, partner_ref, mine_ref):
        lane = lax.broadcasted_iota(jnp.int32, (1, width), 1)
        low = at_ref[1] * shard
        inside = (lane >= low) & (lane < low + shard)
        wide = jnp.concatenate([small_ref[0:6]] * (width // shard), axis=1)
        placed = jnp.where(inside, wide, 0.0).astype(BF)
        gap = jnp.zeros((1, padded - shard), F32)
        query_value = jnp.concatenate(
            [small_ref[6:7], gap, jnp.zeros((1, padded), F32), small_ref[7:8], gap], axis=1
        )
        hidden = jnp.concatenate([small_ref[8 + i : 9 + i] for i in range(4)], axis=1)
        rest = jnp.zeros((extra - 8, width), F32)
        mine = jnp.concatenate([to_float(placed), query_value, hidden, rest], axis=0)
        mine = to_float(mine.astype(BF))
        mine_ref[...] = mine
        chip_ref[:quarter] = own_in[...].astype(BF)
        chip_ref[quarter:] = mine.astype(BF)
        diagonal_ref[:quarter] = other_ref[...].astype(BF)
        diagonal_ref[quarter:] = mine.astype(BF)
        partner_ref[:quarter] = other_ref[...]
        partner_ref[quarter:] = mine

    dims = (quarter + extra, width)
    return launch(
        body,
        "split_inputs",
        [
            (activations, row_spec(quarter, width, False)),
            (activations, row_spec(quarter, width, True)),
            (small, None),
        ],
        [(shape(dims, BF), None)] * 2
        + [(shape(dims, F32), None), (shape((extra, width), F32), None)],
        scalar=position,
    )


def split_grads(out_grad, ids, core):
    _, quarter, width = out_grad.shape

    def body(core_ref, own, other, own_id, other_id, keep_ref, partner_ref):
        keep_ref[...] = jnp.where(own_id[...] >= 0, own[...], 0.0)
        partner_ref[...] = jnp.where(other_id[...] >= 0, other[...], 0.0)

    return launch(
        body,
        "split_grads",
        [
            (out_grad, row_spec(quarter, width, False)),
            (out_grad, row_spec(quarter, width, True)),
            (ids, row_spec(quarter, 1, False)),
            (ids, row_spec(quarter, 1, True)),
        ],
        [(shape((quarter, width), F32), held(quarter, width)), (shape((quarter, width), F32), None)],
        scalar=core,
    )


def join_grads(first, second):
    quarter, width = first.shape

    def body(first_ref, second_ref, out_ref):
        out_ref[:quarter] = first_ref[...].astype(BF)
        out_ref[quarter:] = second_ref[...].astype(BF)

    return launch(
        body,
        "join_grads",
        [(first, held(quarter, width)), (second, None)],
        [(shape((2 * quarter, width), BF), None)],
    )[0]


def pack_attention(w_query, w_key, w_value, w_out):
    shard, width = w_out.shape
    padded = -(-shard // LANES) * LANES

    def body(q_ref, k_ref, v_ref, o_ref, out_ref):
        for i, ref in enumerate((q_ref, k_ref, v_ref, o_ref)):
            out_ref[i * padded : i * padded + shard] = ref[...].astype(BF)
            out_ref[i * padded + shard : (i + 1) * padded] = jnp.zeros((padded - shard, width), BF)

    full = pl.BlockSpec((shard, width), lambda i: (0, 0))
    return launch(
        body,
        "pack_attention",
        [(w_query.T, full), (w_key.T, full), (w_value.T, full), (w_out, full)],
        [(shape((4 * padded, width), BF), None)],
    )[0]


def pack_mlp(w_fc1, w_fc2):
    rows, columns = w_fc1.shape

    def body(up_ref, down_ref, up_out, down_out):
        at = step_rows(rows // 4)
        up_out[at] = up_ref[...].astype(BF)
        down_out[at] = down_ref[...].astype(BF)

    block = pl.BlockSpec((rows // 4, columns), lambda i: (i, 0))
    return launch(
        body,
        "pack_mlp",
        [(w_fc1, block), (w_fc2, block)],
        [(shape((rows, columns), BF), None)] * 2,
        grid=(4,),
    )


def project(activations, mine, pieces, weights, padded, core):
    _, quarter, width = activations.shape
    length = 4 * quarter
    columns = 3 * padded

    def body(core_ref, own, mine_ref, second, third, fourth, w_m, w_p, *outs):
        normed_ref, hat_ref, m_ref, p_ref, vec_ref, bias_ref, values = outs
        step = pl.program_id(0)
        pieces = (second, third, fourth)

        @pl.when(step == 0)
        def _():
            vec_ref[...] = mine_ref[0:6] + sum(
                to_float(ref[quarter : quarter + 6]) for ref in pieces
            )
            bias_ref[0:2] = mine_ref[6:8]
            bias_ref[2:4] = second[quarter + 6 : quarter + 8]
            values[...] = own[...]

        for i, piece in enumerate(pieces):

            @pl.when(step == i + 1)
            def _():
                values[...] = to_float(piece[:quarter])

        rows = step_rows(quarter)
        hat, _ = normalize(values[...])
        normed = (hat * vec_ref[0:1] + vec_ref[1:2]).astype(BF)
        normed_ref[...] = normed
        hat_ref[...] = hat.astype(BF)
        m_ref[rows] = (dot_nt(normed, w_m[:columns]) + bias_ref[0:1]).astype(BF)
        p_ref[rows] = (dot_nt(normed, w_p[:columns]) + bias_ref[2:3]).astype(BF)

    return launch(
        body,
        "project",
        [(activations, row_spec(quarter, width, False))]
        + [(a, None) for a in (mine, *pieces, *weights)],
        [(shape((length, width), BF), by_step(quarter, width))] * 2
        + [(shape((length, columns), BF), None)] * 2
        + [(shape((6, width), F32), None), (shape((4, width), F32), None)],
        grid=(4,),
        scratch=[pltpu.VMEM((quarter, width), F32)],
        scalar=core,
        flops=2 * length * width * 2 * columns,
    )


def lane_half():
    return lax.broadcasted_iota(jnp.int32, (1, LANES), 1) < HEAD_DIM


def head_place(head, first):
    block = slice((head // 2) * LANES, (head // 2 + 1) * LANES)
    return block, (first if head % 2 == 0 else ~first)


def attend(side_m, side_p, marks, weights, half_index, heads, dtype):
    length, columns = side_m.shape
    padded = columns // 3
    width = weights[0].shape[1]
    half = length // 2

    def body(side_m, side_p, marks, w_m, w_p, *outs):
        att_refs, inv_refs, e_ref, branch_ref = outs[0:2], outs[2:4], outs[4], outs[5]
        first = lane_half()
        here = step_rows()
        start = half_index * half + pl.program_id(0) * BLOCK
        rows = pl.ds(pl.multiple_of(start, BLOCK), BLOCK)
        mark_q = marks[rows, :LANES]
        mark_k = marks[:, LANES:]
        branch = None
        for side, (ref, w_ref) in enumerate(((side_m, w_m), (side_p, w_p))):
            att = [jnp.zeros((BLOCK, LANES), F32)] * (padded // LANES)
            inv = list(att)
            for head in range(heads):
                block, lanes = head_place(head, first)
                scaled = to_float(ref[rows, block]) * (HEAD_DIM**-0.5 * LOG2_E)
                high = scaled.astype(BF)
                low = (scaled - to_float(high)).astype(BF)
                keys = ref[:, padded + block.start : padded + block.stop]
                left = jnp.concatenate(
                    [jnp.where(lanes, high, mark_q), jnp.where(lanes, low, jnp.zeros_like(low))],
                    axis=1,
                )
                right = jnp.concatenate([jnp.where(lanes, keys, mark_k), keys], axis=1)
                scores = dot_nt(left, right)
                exponent = jnp.exp2(scores - jnp.max(scores, axis=1, keepdims=True)).astype(BF)
                e_ref[side * heads + head] = exponent
                values = ref[:, 2 * padded + block.start : 2 * padded + block.stop]
                both = dot_nn(exponent, jnp.concatenate([values, jnp.ones_like(values)], axis=1))
                inverse = 1.0 / both[:, LANES:]
                index = head // 2
                att[index] = jnp.where(lanes, both[:, :LANES] * inverse, att[index])
                inv[index] = jnp.where(lanes, inverse, inv[index])
            attended = jnp.concatenate(att, axis=1).astype(BF)
            att_refs[side][...] = attended
            inv_refs[side][...] = jnp.concatenate(inv, axis=1)
            part = dot_nn(attended, w_ref[columns:])
            branch = part if branch is None else branch + part
        branch_ref[here] = branch.astype(dtype)

    return launch(
        body,
        f"attend_{half_index}",
        [(a, None) for a in (side_m, side_p, marks, *weights)],
        [(shape((half, padded), BF), by_step(BLOCK, padded))] * 2
        + [(shape((half, padded), F32), by_step(BLOCK, padded))] * 2
        + [
            (
                shape((2 * heads, half, length), BF),
                pl.BlockSpec((2 * heads, BLOCK, length), lambda i: (0, i, 0)),
            ),
            (shape((half, width), dtype), None),
        ],
        grid=(half // BLOCK,),
        flops=8 * 2 * heads * half * length * 256,
        exps=2 * heads * half * length,
        limit=14,
    )


def second_norm(activations, core_piece, branch, received, vectors, core):
    half, width = branch.shape
    quarter = half // 2

    def body(core_ref, own, core_piece, branch_ref, recv_ref, vec, middle_ref, normed_ref):
        for i, piece in enumerate((own, core_piece)):
            rows = slice(i * quarter, (i + 1) * quarter)
            middle = piece[:quarter] + (branch_ref[rows] + to_float(recv_ref[rows]) + vec[2:3])
            middle_ref[rows] = middle
            hat, _ = normalize(middle)
            normed_ref[rows] = (hat * vec[3:4] + vec[4:5]).astype(BF)

    return launch(
        body,
        "second_norm",
        [(activations, row_spec(quarter, width, False))]
        + [(a, None) for a in (core_piece, branch, received, vectors)],
        [(shape((half, width), F32), held(half, width)), (shape((half, width), BF), None)],
        scalar=core,
    )


def mlp(normed, grad, ups, downs, bias, name, dtype):
    rows, width = normed.shape
    hidden_size = ups[0].shape[1]

    def body(n_ref, g_ref, up_m, up_p, down_m, down_p, bias, *outs):
        act_refs, grad_refs, out_ref, grad_ref, sum_ref = outs[0:2], outs[2:4], *outs[4:]

        @pl.when(pl.program_id(0) == 0)
        def _():
            sum_ref[...] = jnp.zeros_like(sum_ref)

        here = step_rows()
        normed_rows, grad_rows = n_ref[here], g_ref[here]
        out = grad_in = None
        for side, (up, down) in enumerate(((up_m, down_m), (up_p, down_p))):
            hidden = dot_nn(normed_rows, up[...]) + bias[2 * side + 1 : 2 * side + 2]
            grad_act = dot_nt(grad_rows, down[...])
            square = hidden * hidden
            th = jnp.tanh(hidden * (GELU_A + GELU_A * GELU_B * square))
            gate = 0.5 + 0.5 * th
            act = (hidden * gate).astype(BF)
            slope = gate + (0.5 * hidden) * (1.0 - th * th) * (
                GELU_A + 3.0 * GELU_A * GELU_B * square
            )
            grad_hidden = (grad_act * slope).astype(BF)
            act_refs[side][here] = act
            grad_refs[side][here] = grad_hidden
            sum_ref[side : side + 1] += column_sum(grad_hidden)
            part = dot_nn(act, down[...])
            out = part if out is None else out + part
            part = dot_nt(grad_hidden, up[...])
            grad_in = part if grad_in is None else grad_in + part
        at = slice(None) if dtype == F32 else here
        out_ref[at] = out.astype(dtype)
        grad_ref[at] = grad_in.astype(dtype)

    return launch(
        body,
        name,
        [(a, None) for a in (normed, grad, *ups, *downs, bias)],
        [(shape((rows, hidden_size), BF), None)] * 4
        + [(shape((rows, width), dtype), by_step(BLOCK, width) if dtype == F32 else None)] * 2
        + [(shape((2, hidden_size), F32), None)],
        grid=(rows // BLOCK,),
        flops=8 * rows * width * 2 * hidden_size,
        exps=rows * 2 * hidden_size,
        limit=12,
    )


def second_norm_back(middle, grad, received, grad_own, grad_partner, vectors):
    quarter, width = grad_own.shape

    def body(middle_ref, grad_ref, recv_ref, own, core_piece, vec, out_ref, branch_ref, sum_ref):
        sums = None
        for i, piece in enumerate((own, core_piece)):
            rows = slice(i * quarter, (i + 1) * quarter)
            hat, inverse = normalize(middle_ref[rows])
            incoming = grad_ref[rows] + to_float(recv_ref[rows])
            out = piece[...] + norm_back(incoming * vec[3:4], hat, inverse)
            branch = out.astype(BF)
            out_ref[rows] = out
            branch_ref[rows] = branch
            part = [
                column_sum(incoming * hat),
                column_sum(incoming),
                column_sum(branch),
                column_sum(piece[...].astype(BF)),
            ]
            sums = part if sums is None else [a + b for a, b in zip(sums, part)]
        sum_ref[...] = jnp.concatenate(sums, axis=0)

    dims = (2 * quarter, width)
    return launch(
        body,
        "second_norm_back",
        [(middle, held(*dims)), (grad, held(*dims)), (received, None)]
        + [(grad_own, held(quarter, width)), (grad_partner, None), (vectors, None)],
        [(shape(dims, F32), held(*dims)), (shape(dims, BF), None), (shape((4, width), F32), None)],
    )


def weight_grad(lefts, rights, name):
    rows, left_size = lefts[0].shape
    right_size = rights[0].shape[1]

    def body(left_0, left_1, right_0, right_1, out_ref):
        total = dot_tn(left_0[...], right_0[...]) + dot_tn(left_1[...], right_1[...])
        out_ref[...] = total.astype(BF)

    return launch(
        body,
        name,
        [(a, None) for a in (*lefts, *rights)],
        [(shape((left_size, right_size), BF), None)],
        flops=4 * rows * left_size * right_size,
    )[0]


def attend_back(grad, weights, attended, inverse, exponent, side_m, side_p, half_index, heads, previous):
    length, columns = side_m.shape
    padded = columns // 3
    half, width = grad.shape
    last = previous is not None
    steps = half // BLOCK

    def body(*refs):
        grad_ref, w_m, w_p, at_m, at_p, inv_m, inv_p, side_m, side_p, e_ref = refs[:10]
        rest = refs[10:]
        if last:
            sum_in, rest = rest[:4], rest[4:]
        dq_refs, sums = rest[0:2], rest[2:6]
        if last:
            sums, sum_out = rest[6:10], rest[2:6]
        step = pl.program_id(0)
        here = step_rows()
        rows = pl.ds(pl.multiple_of(half_index * half + step * BLOCK, BLOCK), BLOCK)

        @pl.when(step == 0)
        def _():
            for i in range(4):
                sums[i][...] = sum_in[i][...] if last else jnp.zeros_like(sums[i])

        first = lane_half()
        lane = lax.broadcasted_iota(jnp.int32, (1, LANES), 1)
        zero = jnp.zeros((), BF)
        for side, (w_ref, at_ref, inv_ref, ref) in enumerate(
            ((w_m, at_m, inv_m, side_m), (w_p, at_p, inv_p, side_p))
        ):
            dk_sum, dv_sum = sums[2 * side], sums[2 * side + 1]
            grad_att = to_float(dot_nt(grad_ref[here], w_ref[columns:]).astype(BF))
            scaled = (grad_att * inv_ref[...]).astype(BF)
            product = to_float(scaled) * to_float(at_ref[...])
            dq = [None] * (padded // LANES)
            for head in range(heads):
                block, lanes = head_place(head, first)
                keys = ref[:, padded + block.start : padded + block.stop]
                values = ref[:, 2 * padded + block.start : 2 * padded + block.stop]
                grad_head = jnp.where(lanes, scaled[:, block], zero)
                centre = -jnp.sum(jnp.where(lanes, product[:, block], 0.0), axis=1, keepdims=True)
                high = centre.astype(BF)
                low = (centre - to_float(high)).astype(BF)
                extra = jnp.where(lane == 0, high, jnp.where(lane == 1, low, zero))
                grad_probs = dot_nt(
                    jnp.concatenate([grad_head, extra], axis=1),
                    jnp.concatenate([values, jnp.ones_like(values)], axis=1),
                )
                probs = e_ref[side * heads + head]
                grad_scores = (to_float(probs) * grad_probs).astype(BF)
                part = dot_nn(grad_scores, jnp.where(lanes, keys, zero))
                index = head // 2
                dq[index] = part if dq[index] is None else dq[index] + part
                dk_sum[:, block] += dot_tn(grad_scores, jnp.where(lanes, ref[rows, block], zero))
                dv_sum[:, block] += dot_tn(probs, grad_head)
            dq_refs[side][here] = (jnp.concatenate(dq, axis=1) * HEAD_DIM**-0.5).astype(BF)

        if last:

            @pl.when(step == steps - 1)
            def _():
                for i in range(4):
                    scale = HEAD_DIM**-0.5 if i % 2 == 0 else 1.0
                    sum_out[i][...] = (sums[i][...] * scale).astype(BF)

    ins = [(a, None) for a in (grad, *weights)]
    ins += [(a, by_step(BLOCK, padded)) for a in (*attended, *inverse)]
    ins += [(side_m, None), (side_p, None)]
    ins += [(exponent, pl.BlockSpec((2 * heads, BLOCK, length), lambda i: (0, i, 0)))]
    if last:
        ins += [(a, None) for a in previous]
    sum_dtype = BF if last else F32
    return launch(
        body,
        f"attend_back_{half_index}",
        ins,
        [(shape((half, padded), BF), None)] * 2 + [(shape((length, padded), sum_dtype), None)] * 4,
        grid=(steps,),
        scratch=[pltpu.VMEM((length, padded), F32)] * 4 if last else [],
        flops=16 * 2 * heads * half * length * 256,
        limit=18,
    )


def input_grad(queries, keys, values, weights, hat, half_index, dtype, sums):
    half, padded = queries[0].shape
    width = hat.shape[1]

    def body(qm, qp, km, kp, vm, vp, w_m, w_p, hat_ref, *rest):
        out_ref, sum_ref = rest[-2:]
        rows = slice(half_index * half, (half_index + 1) * half)
        total = None
        for w_ref, refs in ((w_m, (qm[...], km[rows], vm[rows])), (w_p, (qp[...], kp[rows], vp[rows]))):
            part = dot_nn(jnp.concatenate(refs, axis=1), w_ref[: 3 * padded])
            total = part if total is None else total + part
        out_ref[...] = total.astype(dtype)
        norm = [column_sum(total * to_float(hat_ref[...])), column_sum(total)]
        norm = jnp.concatenate(norm, axis=0)
        if sums:
            first, late = rest[:2]
            norm = jnp.concatenate([norm + first[...], late[...]], axis=0).astype(BF)
        sum_ref[...] = norm

    sum_shape = shape((6, width), BF) if sums else shape((2, width), F32)
    return launch(
        body,
        f"input_grad_{half_index}",
        [(a, None) for a in (*queries, *keys, *values, *weights)]
        + [(hat, pl.BlockSpec((half, width), lambda i: (half_index, 0)))]
        + [(a, None) for a in sums],
        [
            (shape((half, width), dtype), held(half, width) if dtype == F32 else None),
            (sum_shape, None),
        ],
        flops=2 * half * 6 * padded * width,
    )


def attention_weight_grad(attended, grads, queries, key, value, normed, sums, up_sums, side, shard, rows, name):
    half, padded = queries[0].shape
    width = normed.shape[1]

    def body(at_0, at_1, g_0, g_1, q_0, q_1, k_ref, v_ref, n_ref, sum_0, sum_1, up_0, up_1, out_ref):
        def halves(left_0, left_1, right_0, right_1):
            return dot_tn(left_0, right_0) + dot_tn(left_1, right_1)

        n_0, n_1 = n_ref[:half], n_ref[half:]
        products = [
            halves(at_0[...], at_1[...], g_0[...], g_1[...]),
            halves(q_0[...], q_1[...], n_0, n_1),
            dot_tn(k_ref[...], n_ref[...]),
            dot_tn(v_ref[...], n_ref[...]),
        ]
        for i, part in enumerate(products):
            out_ref[i * shard : (i + 1) * shard] = part[:shard].astype(BF)
        bias = [
            column_sum(q_0[...]) + column_sum(q_1[...]),
            column_sum(v_ref[...]),
            jnp.zeros((1, width - 2 * padded), F32),
        ]
        small = jnp.concatenate(
            [
                to_float(sum_0[...]) + to_float(sum_1[...]),
                jnp.concatenate(bias, axis=1),
                up_0[side : side + 1] + up_1[side : side + 1],
            ],
            axis=0,
        )
        out_ref[4 * shard : 4 * shard + 8] = small.astype(BF)
        out_ref[4 * shard + 8 :] = jnp.zeros((rows - 4 * shard - 8, width), BF)

    return launch(
        body,
        name,
        [(a, held(*a.shape)) for a in attended]
        + [(a, None) for a in (*grads, *queries, key, value)]
        + [(normed, held(*normed.shape))]
        + [(a, None) for a in (*sums, *up_sums)],
        [(shape((rows, width), BF), None)],
        flops=2 * 2 * half * 4 * padded * width,
        limit=12,
    )[0]


def home_spec(quarter, width):
    return pl.BlockSpec((None, quarter, width), lambda i, c: (c[0], 0, 0))


def first_norm_back(activations, core_piece, grad_middle, grad, received, vectors, core):
    half, width = grad.shape
    quarter = half // 2

    def body(core_ref, own, core_piece, middle_ref, grad_ref, recv_ref, vec, home_ref, sent_ref):
        for i, piece in enumerate((own, core_piece)):
            rows = slice(i * quarter, (i + 1) * quarter)
            hat, inverse = normalize(piece[:quarter])
            incoming = grad_ref[rows] + to_float(recv_ref[rows])
            out = middle_ref[rows] + norm_back(incoming * vec[0:1], hat, inverse)
            (home_ref, sent_ref)[i][...] = out

    return launch(
        body,
        "first_norm_back",
        [(activations, row_spec(quarter, width, False)), (core_piece, None)]
        + [(grad_middle, held(half, width)), (grad, held(half, width))]
        + [(received, None), (vectors, None)],
        [
            (shape((2, quarter, width), F32), home_spec(quarter, width)),
            (shape((quarter, width), F32), None),
        ],
        scalar=core,
    )


def finish_output(middle, out, received, vectors, core):
    half, width = middle.shape
    quarter = half // 2

    def body(core_ref, middle_ref, out_ref, recv_ref, vec, home_ref, sent_ref):
        total = middle_ref[...] + (out_ref[...] + to_float(recv_ref[...]) + vec[5:6])
        home_ref[...] = total[:quarter]
        sent_ref[...] = total[quarter:]

    return launch(
        body,
        "finish_output",
        [(middle, held(half, width)), (out, held(half, width)), (received, None), (vectors, None)],
        [
            (shape((2, quarter, width), F32), home_spec(quarter, width)),
            (shape((quarter, width), F32), None),
        ],
        scalar=core,
    )


def swap(values, axis, size, bit):
    return lax.ppermute(values, axis, [(i, i ^ bit) for i in range(size)])


def core_swap(values):
    return swap(values, "group", 4, 1)


def chip_swap(values):
    return swap(values, "group", 4, 2)


def diagonal_swap(values):
    return swap(values, "group", 4, 3)


def divide(kept, received, mine, count):
    rows, width = kept.shape
    part = rows // count
    total = len(received)

    def body(mine_ref, kept_ref, *refs):
        recv_refs, out_refs = refs[:total], refs[total:]
        for k in range(count):
            at = pl.ds(pl.multiple_of((mine_ref[0] ^ k) * part, 8), part)
            value = to_float(kept_ref[at])
            for ref in recv_refs:
                value = value + to_float(ref[at])
            out_refs[k][...] = value.astype(BF)

    return launch(
        body,
        "divide",
        [(kept, held(rows, width))] + [(a, None) for a in received],
        [(shape((part, width), BF), held(part, width))] + [(shape((part, width), BF), None)] * (count - 1),
        scalar=mine,
    )


def add_all(kept, received):
    rows, width = kept.shape

    def body(kept_ref, *refs):
        value = to_float(kept_ref[...])
        for ref in refs[:-1]:
            value = value + to_float(ref[...])
        refs[-1][...] = value.astype(BF)

    return launch(
        body,
        "add_all",
        [(kept, held(rows, width))] + [(a, None) for a in received],
        [(shape((rows, width), BF), None)],
    )[0]


def join(parts, mine, dtype):
    part, width = parts[0].shape
    count = len(parts)

    def body(mine_ref, *refs):
        for k in range(count):
            at = pl.ds(pl.multiple_of((mine_ref[0] ^ k) * part, 8), part)
            refs[-1][at] = refs[k][...].astype(dtype)

    dims = (count * part, width)
    return launch(
        body,
        "join",
        [(a, None) for a in parts],
        [(shape(dims, dtype), held(*dims) if dtype == F32 else None)],
        scalar=mine,
    )[0]


def join_weights(parts, mine, shard):
    part, width = parts[0].shape
    count = len(parts)

    def body(mine_ref, *refs):
        rows, outs = refs[-1], refs[count : count + 5]
        for k in range(count):
            at = pl.ds(pl.multiple_of((mine_ref[0] ^ k) * part, 8), part)
            rows[at] = to_float(refs[k][...])
        for i in range(4):
            outs[i][...] = rows[i * shard : (i + 1) * shard]
        outs[4][...] = rows[4 * shard : 4 * shard + 8]

    return launch(
        body,
        "join_weights",
        [(a, None) for a in parts],
        [(shape((shard, width), F32), held(shard, width))] * 4 + [(shape((8, width), F32), None)],
        scratch=[pltpu.VMEM((count * part, width), F32)],
        scalar=mine,
    )


class ReplicaSum:
    def __init__(self, kept, received, size, first, others):
        self.kept, self.received, self.size = kept, [received], size
        self.groups, bit, bits = [], 1, size.bit_length() - 1
        while bit < size:
            take = min(first if bit == 1 else others, bits)
            self.groups.append((bit, 1 << take))
            bit, bits = bit << take, bits - take
        self.at = 0

    def mine(self):
        bit, count = self.groups[self.at]
        return (lax.axis_index("replica") // bit) % count

    def exchange(self, values, k):
        bit, _ = self.groups[self.at]
        return swap(values, "replica", self.size, k * bit)

    def divide(self):
        _, count = self.groups[self.at]
        mine = self.mine().astype(jnp.int32)
        part = self.kept.shape[0] // count
        if part % 8 == 0:
            parts = divide(self.kept, self.received, mine.reshape(1), count)
        else:
            value = to_float(self.kept)
            for received in self.received:
                value = value + to_float(received)
            parts = [
                lax.dynamic_slice_in_dim(value, (mine ^ k) * part, part, 0).astype(BF)
                for k in range(count)
            ]
        self.kept, self.sent = parts[0], parts[1:]

    def send(self):
        self.received = [self.exchange(a, k + 1) for k, a in enumerate(self.sent)]
        self.at += 1

    def scatter(self):
        self.divide()
        self.send()

    def total(self):
        while self.at < len(self.groups):
            self.scatter()
        self.rows = add_all(self.kept, self.received)

    def collect(self):
        self.at -= 1
        _, count = self.groups[self.at]
        self.parts = [self.rows] + [self.exchange(self.rows, k) for k in range(1, count)]

    def combine(self, final=join):
        mine = self.mine().astype(jnp.int32)
        dtype = F32 if self.at == 0 else BF
        part = self.parts[0].shape[0]
        if part % 8 == 0:
            self.rows = (final if self.at == 0 else join)(self.parts, mine.reshape(1), dtype)
            return
        value = jnp.zeros((len(self.parts) * part, self.parts[0].shape[1]), dtype)
        for k, a in enumerate(self.parts):
            value = lax.dynamic_update_slice(value, a.astype(dtype), ((mine ^ k) * part, 0))
        self.rows = value


def after(value, *others):
    return lax.optimization_barrier((value, *others))[0]


def per_device(
    replicas,
    activations,
    out_grad,
    picture_ids,
    ln1_gain,
    ln1_bias,
    w_query,
    q_bias,
    w_key,
    w_value,
    v_bias,
    w_out,
    out_bias,
    ln2_gain,
    ln2_bias,
    w_fc1,
    fc1_bias,
    w_fc2,
    fc2_bias,
):
    row_block, quarter, width = activations.shape
    assert row_block == 2
    shard = w_query.shape[1]
    heads = shard // HEAD_DIM
    padded = -(-shard // LANES) * LANES
    half = 2 * quarter
    group = lax.axis_index("group")
    core_index = group % 2
    core = core_index.astype(jnp.int32).reshape(1)

    small = jnp.concatenate(
        [ln1_gain, ln1_bias, out_bias, ln2_gain, ln2_bias, fc2_bias, q_bias, v_bias, fc1_bias]
    ).reshape(-1, shard)
    position = jnp.stack([core_index, group]).astype(jnp.int32)
    to_chip, to_diagonal, to_core, mine = split_inputs(
        activations, small, position, shard, padded
    )
    from_chip, from_diagonal = chip_swap(to_chip), diagonal_swap(to_diagonal)
    core_piece = core_swap(to_core)

    packed = pack_attention(after(w_query, core_piece), w_key, w_value, w_out)
    w_att = packed, core_swap(packed)

    own_ids = lax.dynamic_slice_in_dim(picture_ids, group * quarter, quarter, 1)[..., None]
    grad_own, grad_to_core = split_grads(after(out_grad, core_piece), own_ids, core)
    grad_core = core_swap(grad_to_core)
    grad_own_rows = join_grads(grad_own, grad_core)
    up_own, down_own = pack_mlp(after(w_fc1, core_piece), w_fc2)

    row_ids = lax.dynamic_index_in_dim(picture_ids, core_index, 0, keepdims=False)
    row_ids = row_ids.reshape(4, quarter)
    ids = jnp.concatenate(
        [lax.dynamic_index_in_dim(row_ids, group ^ i, 0, keepdims=False) for i in range(4)]
    )
    lane = jnp.arange(2 * LANES)
    same = ids[:, None] == (lane % HEAD_DIM - 1)[None, :]
    marks = jnp.where(
        lane[None, :] < LANES, jnp.where(same, 0.0, 1.0), jnp.where(same, MASKED, 0.0)
    ).astype(BF)

    mine = after(mine, up_own, down_own, grad_own_rows, marks)
    normed_one, hat_one, side_m, side_p, vectors, bias = project(
        activations, mine, (core_piece, from_chip, from_diagonal), w_att, padded, core
    )
    ups = up_own, core_swap(up_own)
    downs = down_own, core_swap(down_own)
    grad_mlp = grad_own_rows, chip_swap(grad_own_rows)
    attend_1 = attend(side_m, side_p, marks, w_att, 1, heads, BF)
    branch_received = chip_swap(attend_1[5])
    attend_0 = attend(side_m, after(side_p, grad_mlp[1]), marks, w_att, 0, heads, F32)
    middle, normed_own = second_norm(
        activations, core_piece, attend_0[5], branch_received, vectors, core
    )
    normed_two = normed_own, chip_swap(normed_own)

    mlp_0 = mlp(normed_two[0], grad_mlp[0], ups, downs, bias, "mlp_0", F32)
    mlp_1 = mlp(normed_two[1], grad_mlp[1], ups, downs, bias, "mlp_1", BF)
    grad_received = chip_swap(mlp_1[5])
    out_received = chip_swap(mlp_1[4])

    fc2_sum = ReplicaSum(
        weight_grad((mlp_0[0], mlp_1[0]), grad_mlp, "fc2_kept"),
        core_swap(weight_grad((mlp_0[1], mlp_1[1]), grad_mlp, "fc2_sent")),
        replicas,
        1,
        2,
    )
    fc2_sum.divide()
    normed_back = after(normed_two[1], fc2_sum.sent[0])
    fc2_sum.send()
    fc1_sum = ReplicaSum(
        weight_grad((normed_two[0], normed_back), (mlp_0[2], mlp_1[2]), "fc1_kept"),
        core_swap(weight_grad((normed_two[0], normed_back), (mlp_0[3], mlp_1[3]), "fc1_sent")),
        replicas,
        1,
        2,
    )
    fc1_sum.scatter()
    fc2_sum.received[0] = after(fc2_sum.received[0], *fc1_sum.sent)
    fc2_sum.scatter()

    grad_middle, grad_branch_own, late_sums = second_norm_back(
        middle, mlp_0[5], after(grad_received, *fc2_sum.sent), grad_own, grad_core, vectors
    )
    grad_branch_other = chip_swap(grad_branch_own)
    fc1_sum.received[0] = after(fc1_sum.received[0], grad_branch_own)
    fc1_sum.scatter()

    back_0 = attend_back(
        after(grad_branch_own, out_received, *fc1_sum.sent),
        w_att, attend_0[0:2], attend_0[2:4], attend_0[4], side_m, side_p, 0, heads, None,
    )
    fc2_sum.received[0] = after(fc2_sum.received[0], back_0[0])
    fc2_sum.total()
    fc2_sum.collect()
    output_home, output_sent = finish_output(
        middle, mlp_0[4], after(out_received, fc2_sum.rows), vectors, core
    )
    grad_branch = grad_branch_own, after(grad_branch_other, fc2_sum.rows, output_sent)
    back_1 = attend_back(
        grad_branch[1], w_att, attend_1[0:2], attend_1[2:4], attend_1[4], side_m, side_p, 1, heads,
        back_0[2:6],
    )
    keys, values = (back_1[2], back_1[4]), (back_1[3], back_1[5])
    first_1, norm_sums_1 = input_grad(back_1[0:2], keys, values, w_att, hat_one, 1, BF, ())
    first_received = chip_swap(first_1)
    fc1_sum.received[0] = after(fc1_sum.received[0], first_1)
    fc1_sum.total()
    fc1_sum.collect()
    fc2_sum.parts[1] = after(fc2_sum.parts[1], fc1_sum.rows)
    fc2_sum.combine()
    fc2_sum.collect()
    first_0, wide = input_grad(
        (after(back_0[0], fc2_sum.rows), back_0[1]), keys, values, w_att, hat_one, 0, F32, (norm_sums_1, late_sums)
    )
    wide_received = chip_swap(wide)
    rows = 4 * shard + 8
    rows += -rows % (8 * replicas)

    def attention_grads(side, name, order):
        return attention_weight_grad(
            (attend_0[side], attend_1[side]),
            grad_branch,
            (back_0[side], back_1[side]),
            keys[side],
            after(values[side], *order),
            normed_one,
            (wide, wide_received),
            (mlp_0[6], mlp_1[6]),
            side,
            shard,
            rows,
            name,
        )

    attention_sent = attention_grads(1, "attention_sent", (first_0,))
    attention_kept = attention_grads(0, "attention_kept", (attention_sent,))
    attention_sum = ReplicaSum(attention_kept, core_swap(attention_sent), replicas, 1, 2)
    attention_sum.scatter()
    fc1_sum.parts[1] = after(fc1_sum.parts[1], *attention_sum.sent)
    fc1_sum.combine()
    fc1_sum.collect()
    input_home, input_sent = first_norm_back(
        activations, core_piece, grad_middle, first_0, after(first_received, fc1_sum.rows), vectors, core
    )
    attention_sum.total()
    while attention_sum.at > 0:
        attention_sum.collect()
        attention_sum.combine(lambda parts, mine, _: join_weights(parts, mine, shard))
    for pending in (fc2_sum, fc1_sum):
        pending.combine()
        while pending.at > 0:
            pending.collect()
            pending.combine()
    weights = attention_sum.rows

    def place(home, sent):
        return lax.dynamic_update_slice(home, core_swap(sent)[None], (1 - core_index, 0, 0))

    small = weights[4]
    mine = lax.dynamic_slice_in_dim(small[:6], group * shard, shard, 1)

    return (
        place(output_home, output_sent),
        place(input_home, input_sent),
        mine[0],
        mine[1],
        weights[1].T,
        small[6, :shard],
        weights[2].T,
        weights[3].T,
        small[6, padded : padded + shard],
        weights[0],
        mine[4],
        mine[2],
        mine[3],
        fc1_sum.rows,
        small[7],
        fc2_sum.rows,
        mine[5],
    )


def solution(mesh):
    replicas = mesh.shape["replica"]
    assert mesh.shape["group"] == 4
    patches = P("replica", "group", None)
    vector = P("group")
    columns = P(None, "group")
    rows = P("group", None)
    parameters = (vector, vector, columns, vector, columns, columns, vector, rows)
    parameters += (vector, vector, vector, columns, vector, rows, vector)

    def program(*arguments):
        return per_device(replicas, *arguments)

    return jax.shard_map(
        program,
        mesh=mesh,
        in_specs=(patches, patches, P("replica", None)) + parameters,
        out_specs=(patches, patches) + parameters,
        check_vma=False,
    )
```

```python
import jax
import jax.numpy as jnp
from jax import lax
from jax.experimental import pallas as pl
from jax.experimental.pallas import tpu as pltpu
from jax.sharding import PartitionSpec as P

HEAD_DIM = 64
EPS = 1e-06
MASKED = -1e30
BF = jnp.bfloat16
F32 = jnp.float32
LANES = 128
LOG2_E = 1.4426950408889634
GELU_A = 0.7978845608028654
GELU_B = 0.044715
BLOCK = 256


def to_float(values):
    return values.astype(F32)


def dot_nn(left, right):
    return jnp.dot(left, right, preferred_element_type=F32)


def dot_nt(left, right):
    return lax.dot_general(left, right, (((1,), (1,)), ((), ())), preferred_element_type=F32)


def dot_tn(left, right):
    return lax.dot_general(left, right, (((0,), (0,)), ((), ())), preferred_element_type=F32)


def normalize(values):
    centred = values - jnp.mean(values, axis=-1, keepdims=True)
    inverse = lax.rsqrt(jnp.mean(centred * centred, axis=-1, keepdims=True) + EPS)
    return (centred * inverse, inverse)


def norm_back(grad_hat, normed_hat, inverse):
    return inverse * (
        grad_hat
        - jnp.mean(grad_hat, axis=-1, keepdims=True)
        - normed_hat * jnp.mean(grad_hat * normed_hat, axis=-1, keepdims=True)
    )


def column_sum(values):
    return jnp.sum(to_float(values), axis=0, keepdims=True)


def shape(dims, dtype):
    return jax.ShapeDtypeStruct(dims, dtype)


def after(value, *others):
    return lax.optimization_barrier((value, *others))[0]


SEQUENCE = (
    "W1", "R", "W0", "m", "N", "B0", "m", "B1", "m", "A1",
    "A0", "a", "m", "I1", "I0", "G", "m", "F", "C", "U",
    "a", "m", "a", "L",
)
COSTS = {
    "project": 8000000000,
    "attend_1": 8000000000,
    "attend_0": 8000000000,
    "mlp_0": 8000000000,
    "mlp_1": 8000000000,
    "mlp_kept": 6000000000,
    "attend_back_0": 6000000000,
}
MLP_GROUPS = (1, 1)
ATT_GROUPS = (1, 1)
RS4_EARLY = True
ORDER = []
IN_VMEM = pl.BlockSpec(memory_space=pltpu.VMEM)


def launch(body, name, ins, outs, grid=(1,), scratch=(), aliases=None, flops=0, exps=0, scalar=None, limit=12):
    ins = list(ins)
    if ORDER:
        sizes = [(a.size if spec is None else a.size * 1024, i) for i, (a, spec) in enumerate(ins)]
        at = min(sizes)[1]
        ins[at] = (after(ins[at][0], ORDER[0]), ins[at][1])
    in_specs = [IN_VMEM if spec is None else spec for _, spec in ins]
    out_specs = [IN_VMEM if spec is None else spec for _, spec in outs]
    arrays = [
        a if spec is None else pltpu.with_memory_space_constraint(a, pltpu.HBM) for a, spec in ins
    ]
    count = 0
    if scalar is not None:
        arrays, count = [scalar] + arrays, 1
    results = pl.pallas_call(
        body,
        grid_spec=pltpu.PrefetchScalarGridSpec(
            num_scalar_prefetch=count,
            grid=grid,
            in_specs=in_specs,
            out_specs=out_specs,
            scratch_shapes=list(scratch),
        ),
        input_output_aliases=aliases or {},
        out_shape=[o if spec is None else pltpu.HBM(o.shape, o.dtype) for o, spec in outs],
        cost_estimate=pl.CostEstimate(
            flops=COSTS.get(name, 1), transcendentals=0, bytes_accessed=1
        ),
        compiler_params=pltpu.CompilerParams(vmem_limit_bytes=limit << 20),
        name=name,
    )(*arrays)
    ORDER[:] = [min(results, key=lambda a: a.size)]
    return results


def step_rows(size=BLOCK):
    return pl.ds(pl.multiple_of(pl.program_id(0) * size, size), size)


def held(*dims):
    return pl.BlockSpec(dims, lambda *_: (0,) * len(dims), pipeline_mode=pl.Buffered(1))


def by_step(*dims):
    return pl.BlockSpec(dims, lambda i, *_: (i,) + (0,) * (len(dims) - 1))


def row_spec(quarter, width, other):
    return pl.BlockSpec(
        (None, quarter, width), lambda i, c: ((1 - c[0]) if other else c[0], 0, 0)
    )


def split_inputs(activations, small, position, shard, padded):
    _, quarter, width = activations.shape
    extra = 16

    def body(at_ref, own_in, other_ref, small_ref, chip_ref, diagonal_ref, partner_ref, mine_ref):
        lane = lax.broadcasted_iota(jnp.int32, (1, width), 1)
        low = at_ref[1] * shard
        inside = (lane >= low) & (lane < low + shard)
        wide = jnp.concatenate([small_ref[0:6]] * (width // shard), axis=1)
        placed = jnp.where(inside, wide, 0.0).astype(BF)
        gap = jnp.zeros((1, padded - shard), F32)
        query_value = jnp.concatenate(
            [small_ref[6:7], gap, jnp.zeros((1, padded), F32), small_ref[7:8], gap], axis=1
        )
        hidden = jnp.concatenate([small_ref[8 + i : 9 + i] for i in range(4)], axis=1)
        rest = jnp.zeros((extra - 8, width), F32)
        mine = jnp.concatenate([to_float(placed), query_value, hidden, rest], axis=0)
        mine = to_float(mine.astype(BF))
        mine_ref[...] = mine
        chip_ref[:quarter] = own_in[...].astype(BF)
        chip_ref[quarter:] = mine.astype(BF)
        diagonal_ref[:quarter] = other_ref[...].astype(BF)
        diagonal_ref[quarter:] = mine.astype(BF)
        partner_ref[:quarter] = other_ref[...]
        partner_ref[quarter:] = mine

    dims = (quarter + extra, width)
    return launch(
        body,
        "split_inputs",
        [
            (activations, row_spec(quarter, width, False)),
            (activations, row_spec(quarter, width, True)),
            (small, None),
        ],
        [(shape(dims, BF), None)] * 2
        + [(shape(dims, F32), None), (shape((extra, width), F32), None)],
        scalar=position,
    )


def split_grads(out_grad, ids, core):
    _, quarter, width = out_grad.shape

    def body(core_ref, own_in, other_in, own_id, other_id, chip, diagonal, keep_ref, partner_ref):
        own = jnp.where(own_id[...] >= 0, own_in[...], 0.0)
        other = jnp.where(other_id[...] >= 0, other_in[...], 0.0)
        chip[...] = own.astype(BF)
        diagonal[...] = other.astype(BF)
        keep_ref[...] = own
        partner_ref[...] = other

    return launch(
        body,
        "split_grads",
        [
            (out_grad, row_spec(quarter, width, False)),
            (out_grad, row_spec(quarter, width, True)),
            (ids, row_spec(quarter, 1, False)),
            (ids, row_spec(quarter, 1, True)),
        ],
        [(shape((quarter, width), BF), None)] * 2
        + [(shape((quarter, width), F32), held(quarter, width)), (shape((quarter, width), F32), None)],
        scalar=core,
    )


def pack_attention(w_query, w_key, w_value, w_out):
    shard, width = w_out.shape
    padded = -(-shard // LANES) * LANES

    def body(q_ref, k_ref, v_ref, o_ref, out_ref):
        for i, ref in enumerate((q_ref, k_ref, v_ref, o_ref)):
            out_ref[i * padded : i * padded + shard] = ref[...].astype(BF)
            out_ref[i * padded + shard : (i + 1) * padded] = jnp.zeros((padded - shard, width), BF)

    full = pl.BlockSpec((shard, width), lambda i: (0, 0))
    return launch(
        body,
        "pack_attention",
        [(w_query.T, full), (w_key.T, full), (w_value.T, full), (w_out, full)],
        [(shape((4 * padded, width), BF), None)],
    )[0]


def pack_mlp(w_fc1, w_fc2):
    rows, columns = w_fc1.shape

    def body(up_ref, down_ref, up_out, down_out):
        at = step_rows(rows // 4)
        up_out[at] = up_ref[...].astype(BF)
        down_out[at] = down_ref[...].astype(BF)

    block = pl.BlockSpec((rows // 4, columns), lambda i: (i, 0))
    return launch(
        body,
        "pack_mlp",
        [(w_fc1, block), (w_fc2, block)],
        [(shape((rows, columns), BF), None)] * 2,
        grid=(4,),
    )


def project(activations, mine, pieces, weights, padded, core):
    _, quarter, width = activations.shape
    length = 4 * quarter
    columns = 3 * padded

    def body(core_ref, own, mine_ref, second, third, fourth, w_0, w_1, *outs):
        normed_ref, hat_ref, sides_ref, out_w, vec_ref, bias_ref, values = outs
        step = pl.program_id(0)
        pieces = (second, third, fourth)

        @pl.when(step == 0)
        def _():
            vec_ref[...] = mine_ref[0:6] + sum(
                to_float(ref[quarter : quarter + 6]) for ref in pieces
            )
            bias_ref[0:2] = mine_ref[6:8]
            bias_ref[2:4] = second[quarter + 6 : quarter + 8]
            out_w[0] = w_0[columns:]
            out_w[1] = w_1[columns:]
            values[...] = own[...]

        for i, piece in enumerate(pieces):

            @pl.when(step == i + 1)
            def _():
                values[...] = to_float(piece[:quarter])

        rows = step_rows(quarter)
        hat, _ = normalize(values[...])
        normed = (hat * vec_ref[0:1] + vec_ref[1:2]).astype(BF)
        normed_ref[...] = normed
        hat_ref[...] = hat.astype(BF)
        for side, w_ref in enumerate((w_0, w_1)):
            bias = bias_ref[2 * side : 2 * side + 1]
            sides_ref[side, rows] = (dot_nt(normed, w_ref[:columns]) + bias).astype(BF)

    return launch(
        body,
        "project",
        [(activations, row_spec(quarter, width, False))]
        + [(a, None) for a in (mine, *pieces, *weights)],
        [(shape((length, width), BF), by_step(quarter, width))] * 2
        + [(shape((2, length, columns), BF), None), (shape((2, padded, width), BF), None)]
        + [(shape((6, width), F32), None), (shape((4, width), F32), None)],
        grid=(4,),
        scratch=[pltpu.VMEM((quarter, width), F32)],
        scalar=core,
        flops=2 * length * width * 2 * columns,
    )


def lane_half():
    return lax.broadcasted_iota(jnp.int32, (1, LANES), 1) < HEAD_DIM


def head_place(head, first):
    block = slice((head // 2) * LANES, (head // 2 + 1) * LANES)
    return block, (first if head % 2 == 0 else ~first)


def attend(sides, marks, out_w, half_index, heads, dtype):
    _, length, columns = sides.shape
    padded, width = out_w.shape[1:]
    half = length // 2

    def body(sides, marks, w_ref, att_ref, inv_ref, e_ref, branch_ref, total_ref):
        side = pl.program_id(1)
        first = lane_half()
        here = step_rows()
        start = half_index * half + pl.program_id(0) * BLOCK
        rows = pl.ds(pl.multiple_of(start, BLOCK), BLOCK)
        mark_q = marks[rows, :LANES]
        mark_k = marks[:, LANES:]
        att = [jnp.zeros((BLOCK, LANES), F32)] * (padded // LANES)
        inv = list(att)
        for head in range(heads):
            block, lanes = head_place(head, first)
            scaled = to_float(sides[side, rows, block]) * (HEAD_DIM**-0.5 * LOG2_E)
            high = scaled.astype(BF)
            low = (scaled - to_float(high)).astype(BF)
            keys = sides[side, :, padded + block.start : padded + block.stop]
            left = jnp.concatenate(
                [jnp.where(lanes, high, mark_q), jnp.where(lanes, low, jnp.zeros_like(low))],
                axis=1,
            )
            right = jnp.concatenate([jnp.where(lanes, keys, mark_k), keys], axis=1)
            scores = dot_nt(left, right)
            exponent = jnp.exp2(scores - jnp.max(scores, axis=1, keepdims=True)).astype(BF)
            e_ref[head] = exponent
            values = sides[side, :, 2 * padded + block.start : 2 * padded + block.stop]
            both = dot_nn(exponent, jnp.concatenate([values, jnp.ones_like(values)], axis=1))
            inverse = 1.0 / both[:, LANES:]
            index = head // 2
            att[index] = jnp.where(lanes, both[:, :LANES] * inverse, att[index])
            inv[index] = jnp.where(lanes, inverse, inv[index])
        attended = jnp.concatenate(att, axis=1).astype(BF)
        att_ref[...] = attended
        inv_ref[...] = jnp.concatenate(inv, axis=1)
        part = dot_nn(attended, w_ref[side])

        @pl.when(side == 0)
        def _():
            total_ref[...] = part

        @pl.when(side == 1)
        def _():
            branch_ref[here] = (total_ref[...] + part).astype(dtype)

    block = pl.BlockSpec((None, BLOCK, padded), lambda i, j: (j, i, 0))
    return launch(
        body,
        f"attend_{half_index}",
        [(a, None) for a in (sides, marks, out_w)],
        [
            (shape((2, half, padded), BF), block),
            (shape((2, half, padded), F32), block),
            (
                shape((2 * heads, half, length), BF),
                pl.BlockSpec((heads, BLOCK, length), lambda i, j: (j, i, 0)),
            ),
            (shape((half, width), dtype), None),
        ],
        grid=(half // BLOCK, 2),
        scratch=[pltpu.VMEM((BLOCK, width), F32)],
        flops=8 * 2 * heads * half * length * 256,
        exps=2 * heads * half * length,
        limit=16,
    )


def second_norm(activations, core_piece, branch, received, vectors, core):
    half, width = branch.shape
    quarter = half // 2
    size = quarter // 2

    def body(core_ref, own, core_piece, branch_ref, recv_ref, vec, middle_ref, normed_ref, values):
        step = pl.program_id(0)
        here = step_rows(size)

        @pl.when(step < 2)
        def _():
            values[...] = own[...]

        @pl.when(step >= 2)
        def _():
            values[...] = core_piece[pl.ds(pl.multiple_of((step - 2) * size, size), size)]

        middle = values[...] + (branch_ref[here] + to_float(recv_ref[here]) + vec[2:3])
        middle_ref[...] = middle
        hat, _ = normalize(middle)
        normed_ref[here] = (hat * vec[3:4] + vec[4:5]).astype(BF)

    own_spec = pl.BlockSpec((None, size, width), lambda i, c: (c[0], jnp.minimum(i, 1), 0))
    return launch(
        body,
        "second_norm",
        [(activations, own_spec)] + [(a, None) for a in (core_piece, branch, received, vectors)],
        [(shape((half, width), F32), by_step(size, width)), (shape((half, width), BF), None)],
        grid=(4,),
        scratch=[pltpu.VMEM((size, width), F32)],
        scalar=core,
    )


def stack_weights(own, partner):
    def body(*refs):
        refs[4][0], refs[4][1] = refs[0][...], refs[1][...]
        refs[5][0], refs[5][1] = refs[2][...], refs[3][...]

    return launch(
        body,
        "stack_weights",
        [(a, None) for pair in zip(own, partner) for a in pair],
        [(shape((2, *a.shape), BF), None) for a in own],
    )


def mlp(normed, grad, ups, downs, bias, half_index, dtype, previous):
    rows, width = normed.shape
    hidden_size = ups.shape[2]

    def body(n_ref, g_0, g_1, up, down, bias, *rest):
        act_ref, hid_ref, out_ref, grad_ref, sum_ref, *totals = rest[len(previous) :]
        side = pl.program_id(1)
        start = half_index * rows + pl.program_id(0) * BLOCK
        shared = pl.ds(pl.multiple_of(start, BLOCK), BLOCK)

        @pl.when((pl.program_id(0) == 0) & (side == 0))
        def _():
            sum_ref[...] = jnp.zeros_like(sum_ref)

        here = step_rows()
        grad_rows = jnp.where(pl.program_id(0) == 0, g_0[...].astype(BF), g_1[...].astype(BF))
        normed_rows = n_ref[here]
        hidden = dot_nn(normed_rows, up[side]) + jnp.where(side == 0, bias[1:2], bias[3:4])
        grad_act = dot_nt(grad_rows, down[side])
        square = hidden * hidden
        th = jnp.tanh(hidden * (GELU_A + GELU_A * GELU_B * square))
        gate = 0.5 + 0.5 * th
        act = (hidden * gate).astype(BF)
        slope = gate + (0.5 * hidden) * (1.0 - th * th) * (GELU_A + 3.0 * GELU_A * GELU_B * square)
        grad_hidden = (grad_act * slope).astype(BF)
        act_ref[side, shared] = act
        hid_ref[side, shared] = grad_hidden
        sum_ref[side] += column_sum(grad_hidden)
        out = dot_nn(act, down[side])
        grad_in = dot_nt(grad_hidden, up[side])

        if dtype == F32:

            @pl.when(side == 0)
            def _():
                out_ref[...] = out
                grad_ref[...] = grad_in

            @pl.when(side == 1)
            def _():
                out_ref[...] += out
                grad_ref[...] += grad_in

        else:

            @pl.when(side == 0)
            def _():
                totals[0][...] = out
                totals[1][...] = grad_in

            @pl.when(side == 1)
            def _():
                out_ref[here] = (totals[0][...] + out).astype(dtype)
                grad_ref[here] = (totals[1][...] + grad_in).astype(dtype)

    return launch(
        body,
        f"mlp_{half_index}",
        [(a, None) for a in (normed, *grad, ups, downs, bias, *previous)],
        [(shape((2, 2 * rows, hidden_size), BF), None)] * 2
        + [(shape((rows, width), dtype), by_step(BLOCK, width) if dtype == F32 else None)] * 2
        + [(shape((2, 1, hidden_size), F32), None)],
        grid=(rows // BLOCK, 2),
        scratch=[] if dtype == F32 else [pltpu.VMEM((BLOCK, width), F32)] * 2,
        aliases={6 + i: i for i in range(len(previous))},
        flops=8 * rows * width * 2 * hidden_size,
        exps=rows * 2 * hidden_size,
        limit=12,
    )


def second_norm_back(middle, grad, received, grad_own, grad_partner, vectors):
    quarter, width = grad_own.shape
    size = quarter // 2

    def body(
        middle_ref, grad_ref, recv_ref, own, partner, vec, out_ref, branch_ref, sum_ref, values
    ):
        step = pl.program_id(0)
        here = step_rows(size)

        @pl.when(step < 2)
        def _():
            values[...] = own[...]

        @pl.when(step >= 2)
        def _():
            values[...] = partner[pl.ds(pl.multiple_of((step - 2) * size, size), size)]

        hat, inverse = normalize(middle_ref[...])
        incoming = grad_ref[...] + to_float(recv_ref[here])
        out = values[...] + norm_back(incoming * vec[3:4], hat, inverse)
        branch = out.astype(BF)
        out_ref[...] = out
        branch_ref[here] = branch
        sums = jnp.concatenate(
            [
                column_sum(incoming * hat),
                column_sum(incoming),
                column_sum(branch),
                column_sum(values[...].astype(BF)),
            ],
            axis=0,
        )

        @pl.when(step == 0)
        def _():
            sum_ref[...] = sums

        @pl.when(step > 0)
        def _():
            sum_ref[...] += sums

    dims = (2 * quarter, width)
    own_spec = pl.BlockSpec((size, width), lambda i: (jnp.minimum(i, 1), 0))
    return launch(
        body,
        "second_norm_back",
        [(middle, by_step(size, width)), (grad, by_step(size, width)), (received, None)]
        + [(grad_own, own_spec), (grad_partner, None), (vectors, None)],
        [
            (shape(dims, F32), by_step(size, width)),
            (shape(dims, BF), None),
            (shape((4, width), F32), None),
        ],
        grid=(4,),
        scratch=[pltpu.VMEM((size, width), F32)],
    )


def mlp_weight_grad(normed, grads, activated, hidden, side):
    rows, width = normed[0].shape
    size = hidden.shape[2]

    def body(n_0, n_1, g_0, g_1, g_2, g_3, act_ref, hid_ref, out_ref):
        first, second = slice(0, rows), slice(rows, 2 * rows)
        up = dot_tn(n_0[...], hid_ref[side, first]) + dot_tn(n_1[...], hid_ref[side, second])
        out_ref[:width] = up.astype(BF)
        down, at = None, rows // 2
        for i, ref in enumerate((g_0, g_1, g_2, g_3)):
            part = dot_tn(act_ref[side, i * at : (i + 1) * at], ref[...].astype(BF))
            down = part if down is None else down + part
        out_ref[width:] = down.astype(BF)

    dims = (width + size, width)
    return launch(
        body,
        ("mlp_kept", "mlp_sent")[side],
        [(a, None) for a in (*normed, *grads, activated, hidden)],
        [(shape(dims, BF), None)],
        flops=8 * rows * width * size,
        limit=14,
    )[0]


def attend_back(grad, out_w, attended, inverse, exponent, sides, half_index, heads, previous, only=None):
    _, length, columns = sides.shape
    padded = columns // 3
    half, width = grad.shape
    last = previous is not None
    steps = half // BLOCK

    def body(grad_ref, w_ref, at_ref, inv_ref, sides, e_ref, *rest):
        if last:
            dk_in, dv_in, dq_ref, dk_out, dv_out, dk_sum, dv_sum = rest
        else:
            dq_ref, dk_sum, dv_sum = rest
        step = pl.program_id(0)
        side = pl.program_id(1) if only is None else only
        slot = side if only is None else 0
        here = step_rows()
        rows = pl.ds(pl.multiple_of(half_index * half + step * BLOCK, BLOCK), BLOCK)

        @pl.when(step == 0)
        def _():
            dk_sum[slot] = dk_in[side] if last else jnp.zeros((length, padded), F32)
            dv_sum[slot] = dv_in[side] if last else jnp.zeros((length, padded), F32)

        first = lane_half()
        lane = lax.broadcasted_iota(jnp.int32, (1, LANES), 1)
        zero = jnp.zeros((), BF)
        grad_att = to_float(dot_nt(grad_ref[here], w_ref[side]).astype(BF))
        scaled = (grad_att * inv_ref[...]).astype(BF)
        product = to_float(scaled) * to_float(at_ref[...])
        dq = [None] * (padded // LANES)
        for head in range(heads):
            block, lanes = head_place(head, first)
            keys = sides[side, :, padded + block.start : padded + block.stop]
            values = sides[side, :, 2 * padded + block.start : 2 * padded + block.stop]
            grad_head = jnp.where(lanes, scaled[:, block], zero)
            centre = -jnp.sum(jnp.where(lanes, product[:, block], 0.0), axis=1, keepdims=True)
            high = centre.astype(BF)
            low = (centre - to_float(high)).astype(BF)
            extra = jnp.where(lane == 0, high, jnp.where(lane == 1, low, zero))
            grad_probs = dot_nt(
                jnp.concatenate([grad_head, extra], axis=1),
                jnp.concatenate([values, jnp.ones_like(values)], axis=1),
            )
            probs = e_ref[head]
            grad_scores = (to_float(probs) * grad_probs).astype(BF)
            part = dot_nn(grad_scores, jnp.where(lanes, keys, zero))
            index = head // 2
            dq[index] = part if dq[index] is None else dq[index] + part
            queries = jnp.where(lanes, sides[side, rows, block], zero)
            dk_sum[slot, :, block] += dot_tn(grad_scores, queries)
            dv_sum[slot, :, block] += dot_tn(probs, grad_head)
        dq_ref[slot, here] = (jnp.concatenate(dq, axis=1) * HEAD_DIM**-0.5).astype(BF)

        if last:

            @pl.when(step == steps - 1)
            def _():
                dk_out[slot] = (dk_sum[slot] * HEAD_DIM**-0.5).astype(BF)
                dv_out[slot] = dv_sum[slot].astype(BF)

    count = 2 if only is None else 1
    block = pl.BlockSpec((None, BLOCK, padded), lambda i, j: (j if only is None else only, i, 0))
    ins = [(grad, None), (out_w, None), (attended, block), (inverse, block), (sides, None)]
    ins += [(exponent, pl.BlockSpec((heads, BLOCK, length), lambda i, j: (j if only is None else only, i, 0)))]
    if last:
        ins += [(a, None) for a in previous]
    sum_dtype = BF if last else F32
    return launch(
        body,
        f"attend_back_{half_index}" + ("" if only is None else f"_{only}"),
        ins,
        [(shape((count, half, padded), BF), None)]
        + [(shape((count, length, padded), sum_dtype), None)] * 2,
        grid=(steps, count),
        scratch=[pltpu.VMEM((count, length, padded), F32)] * 2 if last else [],
        flops=16 * 2 * heads * half * length * 256,
        limit=20,
    )


def input_grad(queries, keys, values, weights, hat, half_index, dtype):
    half, padded = queries[0].shape
    width = hat.shape[1]

    def body(q_0, q_1, k_0, k_1, v_0, v_1, w_0, w_1, hat_ref, out_ref, sum_ref):
        rows = slice(half_index * half, (half_index + 1) * half)
        total = None
        for w_ref, q_ref, k_ref, v_ref in ((w_0, q_0, k_0, v_0), (w_1, q_1, k_1, v_1)):
            left = jnp.concatenate([q_ref[...], k_ref[rows], v_ref[rows]], axis=1)
            part = dot_nn(left, w_ref[: 3 * padded])
            total = part if total is None else total + part
        out_ref[...] = total.astype(dtype)
        sums = [column_sum(total * to_float(hat_ref[...])), column_sum(total)]
        sum_ref[...] = jnp.concatenate(sums, axis=0)

    return launch(
        body,
        f"input_grad_{half_index}",
        [(a, None) for a in (*queries, *keys, *values, *weights)]
        + [(hat, pl.BlockSpec((half, width), lambda i: (half_index, 0)))],
        [
            (shape((half, width), dtype), held(half, width) if dtype == F32 else None),
            (shape((2, width), F32), None),
        ],
        flops=2 * half * 6 * padded * width,
    )


def attention_weight_grad(attended, grads, queries, keys, values, normed, shard, side):
    half, padded = queries[0].shape
    width = normed.shape[1]

    def body(at_0, at_1, g_0, g_1, q_0, q_1, k_ref, v_ref, n_ref, out_ref):
        n_0, n_1 = n_ref[:half], n_ref[half:]
        products = [
            dot_tn(at_0[...], g_0[...]) + dot_tn(at_1[...], g_1[...]),
            dot_tn(q_0[...], n_0) + dot_tn(q_1[...], n_1),
            dot_tn(k_ref[...], n_ref[...]),
            dot_tn(v_ref[...], n_ref[...]),
        ]
        for i, part in enumerate(products):
            out_ref[i * shard : (i + 1) * shard] = part[:shard].astype(BF)

    at_spec = pl.BlockSpec((None, half, padded), lambda i: (side, 0, 0))
    dims = (4 * shard, width)
    return launch(
        body,
        ("attention_kept", "attention_sent")[side],
        [(a, at_spec) for a in attended]
        + [(a, None) for a in (*grads, *queries, keys, values)]
        + [(normed, held(*normed.shape))],
        [(shape(dims, BF), None)],
        flops=2 * 2 * half * 4 * padded * width,
        limit=14,
    )[0]


def small_grads(norm_0, norm_1, late, queries, values, up_0, up_1):
    width = late.shape[1]
    padded = values[0].shape[1]

    def body(norm_0, norm_1, late, *rest):
        queries, values, (up_0, up_1, wide_ref, bias_ref) = rest[:4], rest[4:6], rest[6:]
        wide_ref[...] = jnp.concatenate([norm_0[...] + norm_1[...], late[...]], axis=0).astype(BF)
        for side in range(2):
            bias = [
                column_sum(queries[side][...]) + column_sum(queries[2 + side][...]),
                column_sum(values[side][...]),
                jnp.zeros((1, width - 2 * padded), F32),
            ]
            both = [jnp.concatenate(bias, axis=1), up_0[side] + up_1[side]]
            bias_ref[2 * side : 2 * side + 2] = jnp.concatenate(both, axis=0)

    return launch(
        body,
        "small_grads",
        [(a, None) for a in (norm_0, norm_1, late, *queries, *values, up_0, up_1)],
        [(shape((6, width), BF), None), (shape((4, width), F32), None)],
    )


def small_chip(wide, received, bias):
    width = wide.shape[1]

    def body(wide_ref, recv_ref, bias_ref, own_ref, sent_ref):
        total = to_float(wide_ref[...]) + to_float(recv_ref[...])
        own_ref[...] = jnp.concatenate([total, bias_ref[0:2]], axis=0)
        sent_ref[...] = jnp.concatenate([total, bias_ref[2:4]], axis=0)

    return launch(
        body,
        "small_chip",
        [(wide, None), (received, None), (bias, None)],
        [(shape((8, width), F32), None)] * 2,
    )


def small_sum(own, received):
    def body(own_ref, recv_ref, out_ref):
        out_ref[...] = (own_ref[...] + recv_ref[...]).astype(BF)

    return launch(
        body, "small_sum", [(own, None), (received, None)], [(shape(own.shape, BF), None)]
    )[0]


def home_spec(quarter, width):
    return pl.BlockSpec((None, quarter, width), lambda i, c: (c[0], 0, 0))


def first_norm_back(activations, core_piece, grad_middle, grad, received, vectors, core):
    half, width = grad.shape
    quarter = half // 2

    def body(core_ref, own, core_piece, middle_ref, grad_ref, recv_ref, vec, home_ref, sent_ref):
        for i, piece in enumerate((own, core_piece)):
            rows = slice(i * quarter, (i + 1) * quarter)
            hat, inverse = normalize(piece[:quarter])
            incoming = grad_ref[rows] + to_float(recv_ref[rows])
            out = middle_ref[rows] + norm_back(incoming * vec[0:1], hat, inverse)
            (home_ref, sent_ref)[i][...] = out

    return launch(
        body,
        "first_norm_back",
        [(activations, row_spec(quarter, width, False)), (core_piece, None)]
        + [(grad_middle, held(half, width)), (grad, held(half, width))]
        + [(received, None), (vectors, None)],
        [
            (shape((2, quarter, width), F32), home_spec(quarter, width)),
            (shape((quarter, width), F32), None),
        ],
        scalar=core,
    )


def finish_output(middle, out, received, vectors, core):
    half, width = middle.shape
    quarter = half // 2

    def body(core_ref, middle_ref, out_ref, recv_ref, vec, home_ref, sent_ref):
        total = middle_ref[...] + (out_ref[...] + to_float(recv_ref[...]) + vec[5:6])
        home_ref[...] = total[:quarter]
        sent_ref[...] = total[quarter:]

    return launch(
        body,
        "finish_output",
        [(middle, held(half, width)), (out, held(half, width)), (received, None), (vectors, None)],
        [
            (shape((2, quarter, width), F32), home_spec(quarter, width)),
            (shape((quarter, width), F32), None),
        ],
        scalar=core,
    )


def swap(values, axis, size, bit):
    return lax.ppermute(values, axis, [(i, i ^ bit) for i in range(size)])


def core_swap(values):
    return swap(values, "group", 4, 1)


def chip_swap(values):
    return swap(values, "group", 4, 2)


def diagonal_swap(values):
    return swap(values, "group", 4, 3)


def divide(kept, received, mine, count, fresh):
    rows, width = kept.shape
    part = rows // count
    total = len(received)

    def body(mine_ref, kept_ref, *refs):
        recv_refs, out_refs = refs[:total], refs[total:]
        for k in range(count):
            at = pl.ds(pl.multiple_of((mine_ref[0] ^ k) * part, 8), part)
            value = to_float(kept_ref[at])
            for ref in recv_refs:
                value = value + to_float(ref[at])
            out_refs[k][...] = value.astype(BF)

    return launch(
        body,
        "divide",
        [(kept, None if fresh else held(rows, width))] + [(a, None) for a in received],
        [(shape((part, width), BF), held(part, width))] + [(shape((part, width), BF), None)] * (count - 1),
        scalar=mine,
    )


def add_all(kept, received, extra):
    rows, width = kept.shape
    below = extra.shape[0] if extra is not None else 0

    def body(kept_ref, *refs):
        out_ref = refs[-1]
        value = to_float(kept_ref[...])
        for ref in refs[: len(received)]:
            value = value + to_float(ref[...])
        out_ref[:rows] = value.astype(BF)
        if below:
            out_ref[rows:] = refs[-2][...]

    return launch(
        body,
        "add_all",
        [(kept, held(rows, width))]
        + [(a, None) for a in received]
        + ([(extra, None)] if below else []),
        [(shape((rows + below, width), BF), None)],
    )[0]


def join(parts, mine, extra):
    rows, width = parts[0].shape
    part, count = rows - extra, len(parts)

    def body(mine_ref, *refs):
        out_ref = refs[-1]
        for k in range(count):
            at = pl.ds(pl.multiple_of((mine_ref[0] ^ k) * part, 8), part)
            out_ref[at] = refs[k][:part]
        if extra:
            out_ref[count * part :] = sum(to_float(ref[part:]) for ref in refs[:-1]).astype(BF)

    return launch(
        body,
        "join",
        [(a, None) for a in parts],
        [(shape((count * part + extra, width), BF), None)],
        scalar=mine,
    )[0]


def join_weights(parts, mine, shard, extra):
    rows, width = parts[0].shape
    part, count = rows - extra, len(parts)

    def body(mine_ref, *refs):
        total, outs = refs[-1], refs[count : count + 5]
        for k in range(count):
            at = pl.ds(pl.multiple_of((mine_ref[0] ^ k) * part, 8), part)
            total[at] = to_float(refs[k][:part])
        for i in range(4):
            outs[i][...] = total[i * shard : (i + 1) * shard]
        outs[4][...] = sum(to_float(ref[part:]) for ref in refs[:count])

    return launch(
        body,
        "join_weights",
        [(a, None) for a in parts],
        [(shape((shard, width), F32), held(shard, width))] * 4 + [(shape((extra, width), F32), None)],
        scratch=[pltpu.VMEM((count * part, width), F32)],
        scalar=mine,
    )


def join_mlp(parts, mine):
    def body(mine_ref, first_ref, second_ref, up_ref, down_ref):
        for ref, which in ((first_ref, mine_ref[0]), (second_ref, 1 - mine_ref[0])):
            for index, out_ref in enumerate((up_ref, down_ref)):

                @pl.when(which == index)
                def _():
                    out_ref[...] = to_float(ref[...])

    dims = parts[0].shape
    return launch(
        body,
        "join_mlp",
        [(a, None) for a in parts],
        [(shape(dims, F32), held(*dims))] * 2,
        scalar=mine,
    )


class ReplicaSum:
    def __init__(self, kept, received, size, first, others):
        self.kept, self.received, self.size = kept, [received], size
        self.groups, bit, bits = [], 1, size.bit_length() - 1
        while bit < size:
            take = min(first if bit == 1 else others, bits)
            self.groups.append((bit, 1 << take))
            bit, bits = bit << take, bits - take
        self.at, self.rows = 0, None

    def mine(self):
        bit, count = self.groups[self.at]
        return (lax.axis_index("replica") // bit) % count

    def exchange(self, values, k):
        bit, _ = self.groups[self.at]
        return swap(values, "replica", self.size, k * bit)

    def divide(self):
        _, count = self.groups[self.at]
        mine = self.mine().astype(jnp.int32)
        part = self.kept.shape[0] // count
        if part % 8 == 0:
            parts = divide(self.kept, self.received, mine.reshape(1), count, self.at == 0)
        else:
            value = to_float(self.kept)
            for received in self.received:
                value = value + to_float(received)
            parts = [
                lax.dynamic_slice_in_dim(value, (mine ^ k) * part, part, 0).astype(BF)
                for k in range(count)
            ]
        self.kept, self.sent = parts[0], parts[1:]

    def send(self):
        self.received = [self.exchange(a, k + 1) for k, a in enumerate(self.sent)]
        self.at += 1

    def scatter(self):
        self.divide()
        self.send()

    def total(self, extra=None):
        while self.at < len(self.groups):
            self.scatter()
        self.extra = 0 if extra is None else extra.shape[0]
        self.rows = add_all(self.kept, self.received, extra)

    def collect(self):
        self.at -= 1
        _, count = self.groups[self.at]
        self.parts = [self.rows] + [self.exchange(self.rows, k) for k in range(1, count)]

    def combine(self, final=None):
        mine = self.mine().astype(jnp.int32)
        part = self.parts[0].shape[0] - self.extra
        if final is not None:
            self.rows = final(self.parts, mine.reshape(1))
            return
        if part % 8 == 0:
            self.rows = join(self.parts, mine.reshape(1), self.extra)
            return
        width = self.parts[0].shape[1]
        value = jnp.zeros((len(self.parts) * part, width), BF)
        for k, a in enumerate(self.parts):
            value = lax.dynamic_update_slice(value, a[:part], ((mine ^ k) * part, 0))
        below = sum(to_float(a[part:]) for a in self.parts).astype(BF)
        self.rows = jnp.concatenate([value, below], axis=0)


def per_device(
    replicas,
    activations,
    out_grad,
    picture_ids,
    ln1_gain,
    ln1_bias,
    w_query,
    q_bias,
    w_key,
    w_value,
    v_bias,
    w_out,
    out_bias,
    ln2_gain,
    ln2_bias,
    w_fc1,
    fc1_bias,
    w_fc2,
    fc2_bias,
):
    ORDER.clear()
    row_block, quarter, width = activations.shape
    assert row_block == 2
    shard = w_query.shape[1]
    heads = shard // HEAD_DIM
    padded = -(-shard // LANES) * LANES
    half = 2 * quarter
    group = lax.axis_index("group")
    core_index = group % 2
    core = core_index.astype(jnp.int32).reshape(1)

    small = jnp.concatenate(
        [ln1_gain, ln1_bias, out_bias, ln2_gain, ln2_bias, fc2_bias, q_bias, v_bias, fc1_bias]
    ).reshape(-1, shard)
    position = jnp.stack([core_index, group]).astype(jnp.int32)
    to_chip, to_diagonal, to_core, mine = split_inputs(
        activations, small, position, shard, padded
    )
    from_chip, from_diagonal = chip_swap(to_chip), diagonal_swap(to_diagonal)
    core_piece = core_swap(to_core)

    packed = pack_attention(w_query, w_key, w_value, w_out)
    w_att = packed, core_swap(packed)
    own_ids = lax.dynamic_slice_in_dim(picture_ids, group * quarter, quarter, 1)[..., None]
    grad_to_chip, grad_to_diagonal, grad_own, grad_to_core = split_grads(out_grad, own_ids, core)
    grad_core = core_swap(grad_to_core)
    grad_far = chip_swap(grad_to_chip), diagonal_swap(grad_to_diagonal)
    grad_near = grad_to_chip, grad_core
    up_own, down_own = pack_mlp(w_fc1, w_fc2)
    up_core, down_core = core_swap(up_own), core_swap(down_own)

    row_ids = lax.dynamic_index_in_dim(picture_ids, core_index, 0, keepdims=False)
    row_ids = row_ids.reshape(4, quarter)
    ids = jnp.concatenate(
        [lax.dynamic_index_in_dim(row_ids, group ^ i, 0, keepdims=False) for i in range(4)]
    )
    lane = jnp.arange(2 * LANES)
    same = ids[:, None] == (lane % HEAD_DIM - 1)[None, :]
    marks = jnp.where(
        lane[None, :] < LANES, jnp.where(same, 0.0, 1.0), jnp.where(same, MASKED, 0.0)
    ).astype(BF)

    normed_one, hat_one, sides, out_w, vectors, bias = project(
        activations, mine, (core_piece, from_chip, from_diagonal), w_att, padded, core
    )
    att_1, inv_1, exp_1, branch_1 = attend(sides, marks, out_w, 1, heads, BF)
    branch_received = chip_swap(branch_1)
    att_0, inv_0, exp_0, branch_0 = attend(sides, after(marks, *grad_far), out_w, 0, heads, F32)
    ups, downs = stack_weights((up_own, down_own), (up_core, down_core))
    middle, normed_own = second_norm(
        activations, core_piece, branch_0, branch_received, vectors, core
    )
    normed_two = normed_own, chip_swap(normed_own)

    activated, hidden, mlp_0, back_0, up_sum_0 = mlp(
        normed_two[0], grad_near, ups, downs, bias, 0, F32, ()
    )
    activated, hidden, mlp_1, back_1, up_sum_1 = mlp(
        normed_two[1], grad_far, ups, downs, bias, 1, BF, (activated, hidden)
    )
    grad_received = chip_swap(back_1)

    state = {}

    def advance(name):
        pending = state[name]
        if pending.rows is None and pending.at < len(pending.groups):
            pending.scatter()
        elif pending.rows is None:
            pending.total(state["small"] if name == "a" else None)
            pending.collect()
        elif pending.at > 0:
            pending.combine()
            pending.collect()

    def attention_grads(side):
        return attention_weight_grad(
            (att_0, att_1),
            state["branch"],
            (state["dq_0"][side], state["dq_1"][side]),
            state["dk"][side],
            state["dv"][side],
            normed_one,
            shard,
            side,
        )

    def first_grad(half_index, dtype):
        return input_grad(
            state[f"dq_{half_index}"], state["dk"], state["dv"], w_att, hat_one, half_index, dtype
        )

    for token in SEQUENCE:
        if token == "W1":
            state["sent"] = core_swap(mlp_weight_grad(normed_two, grad_near + grad_far, activated, hidden, 1))
        elif token == "R":
            state["out"] = chip_swap(after(mlp_1, ORDER[0]))
        elif token == "W0":
            kept = mlp_weight_grad(normed_two, grad_near + grad_far, activated, hidden, 0)
            state["m"] = ReplicaSum(kept, state["sent"], replicas, *MLP_GROUPS)
        elif token == "N":
            grad_middle, branch_own, late_sums = second_norm_back(
                middle, back_0, grad_received, grad_own, grad_core, vectors
            )
            state["branch"] = branch_own, chip_swap(branch_own)
        elif token == "B0":
            dq, dk_0, dv_0 = attend_back(
                state["branch"][0], out_w, att_0, inv_0, exp_0, sides, 0, heads, None
            )
            state["dq_0"] = dq[0], dq[1]
        elif token == "B1":
            dq, dk, dv = attend_back(
                state["branch"][1], out_w, att_1, inv_1, exp_1, sides, 1, heads, (dk_0, dv_0)
            )
            state["dq_1"], state["dk"], state["dv"] = [(a[0], a[1]) for a in (dq, dk, dv)]
        elif token in ("B11", "B10"):
            side = int(token[2])
            parts = attend_back(
                state["branch"][1], out_w, att_1, inv_1, exp_1, sides, 1, heads, (dk_0, dv_0), side
            )
            for key, part in zip(("dq_1", "dk", "dv"), parts):
                state.setdefault(key, {})[side] = part[0]
        elif token == "A1":
            state["sent"] = core_swap(attention_grads(1))
        elif token == "A0":
            state["a"] = ReplicaSum(attention_grads(0), state["sent"], replicas, *ATT_GROUPS)
        elif token == "I1":
            for key in ("dq_1", "dk", "dv"):
                state[key] = state[key][0], state[key][1]
            first_1, norm_1 = first_grad(1, BF)
            if RS4_EARLY:
                first_received = chip_swap(first_1)
        elif token == "I0":
            first_0, norm_0 = first_grad(0, F32)
        elif token == "G":
            wide, bias_sums = small_grads(
                norm_0, norm_1, late_sums, (*state["dq_0"], *state["dq_1"]), state["dv"],
                up_sum_0, up_sum_1,
            )
            wide_received = chip_swap(wide)
            if not RS4_EARLY:
                first_received = chip_swap(after(first_1, wide))
        elif token == "F":
            output_home, output_sent = finish_output(middle, mlp_0, state["out"], vectors, core)
            output_received = core_swap(output_sent)
        elif token == "C":
            small_own, small_sent = small_chip(wide, wide_received, bias_sums)
            small_core = core_swap(small_sent)
        elif token == "U":
            state["small"] = small_sum(small_own, small_core)
        elif token == "L":
            input_home, input_sent = first_norm_back(
                activations, core_piece, grad_middle, first_0, first_received, vectors, core
            )
            input_received = core_swap(input_sent)
        else:
            advance(token)
    for name in ("m", "a"):
        while state[name].rows is None or state[name].at > 0:
            advance(name)
    state["m"].combine(join_mlp)
    state["a"].combine(lambda parts, mine: join_weights(parts, mine, shard, 8))
    weights, small = state["a"].rows[:4], state["a"].rows[4]
    mlp_sum = state["m"]

    def place(home, received):
        return lax.dynamic_update_slice(home, received[None], (1 - core_index, 0, 0))

    mine = lax.dynamic_slice_in_dim(small[:6], group * shard, shard, 1)

    return (
        place(output_home, output_received),
        place(input_home, input_received),
        mine[0],
        mine[1],
        weights[1].T,
        small[6, :shard],
        weights[2].T,
        weights[3].T,
        small[6, padded : padded + shard],
        weights[0],
        mine[4],
        mine[2],
        mine[3],
        mlp_sum.rows[0],
        small[7],
        mlp_sum.rows[1],
        mine[5],
    )


def solution(mesh):
    replicas = mesh.shape["replica"]
    assert mesh.shape["group"] == 4
    patches = P("replica", "group", None)
    vector = P("group")
    columns = P(None, "group")
    rows = P("group", None)
    parameters = (vector, vector, columns, vector, columns, columns, vector, rows)
    parameters += (vector, vector, vector, columns, vector, rows, vector)

    def program(*arguments):
        return per_device(replicas, *arguments)

    return jax.shard_map(
        program,
        mesh=mesh,
        in_specs=(patches, patches, P("replica", None)) + parameters,
        out_specs=(patches, patches) + parameters,
        check_vma=False,
    )
```

```python
import jax
import jax.numpy as jnp
from jax import lax
from jax.experimental import pallas as pl
from jax.experimental.pallas import tpu as pltpu
from jax.sharding import PartitionSpec as P

HEAD_DIM = 64
EPS = 1e-06
MASKED = -1e30
BF = jnp.bfloat16
F32 = jnp.float32
LANES = 128
LOG2_E = 1.4426950408889634
GELU_A = 0.7978845608028654
GELU_B = 0.044715
BLOCK = 256


def to_float(values):
    return values.astype(F32)


def dot_nn(left, right):
    return jnp.dot(left, right, preferred_element_type=F32)


def dot_nt(left, right):
    return lax.dot_general(left, right, (((1,), (1,)), ((), ())), preferred_element_type=F32)


def dot_tn(left, right):
    return lax.dot_general(left, right, (((0,), (0,)), ((), ())), preferred_element_type=F32)


def normalize(values):
    centred = values - jnp.mean(values, axis=-1, keepdims=True)
    inverse = lax.rsqrt(jnp.mean(centred * centred, axis=-1, keepdims=True) + EPS)
    return (centred * inverse, inverse)


def norm_back(grad_hat, normed_hat, inverse):
    return inverse * (
        grad_hat
        - jnp.mean(grad_hat, axis=-1, keepdims=True)
        - normed_hat * jnp.mean(grad_hat * normed_hat, axis=-1, keepdims=True)
    )


def column_sum(values):
    return jnp.sum(to_float(values), axis=0, keepdims=True)


def shape(dims, dtype):
    return jax.ShapeDtypeStruct(dims, dtype)


def after(value, *others):
    return lax.optimization_barrier((value, *others))[0]


SEQUENCE = (
    "W", "m", "R", "N", "B0", "B2", "m", "B3", "A1", "m",
    "A0", "a", "m", "I1", "I0", "F", "m", "G", "C", "a",
    "U", "m", "a", "a", "L", "J",
)
COSTS = {
    "project": 8000000000,
    "attend_1": 8000000000,
    "attend_0": 8000000000,
    "mlp_0": 8000000000,
    "mlp_1": 8000000000,
    "attend_back_0": 14000000000,
    "attend_back_3": 8000000000,
}
MLP_GROUPS = (1, 1)
ATT_GROUPS = (1, 1)
RS4_EARLY = True
ORDER = []
IN_VMEM = pl.BlockSpec(memory_space=pltpu.VMEM)


def launch(body, name, ins, outs, grid=(1,), scratch=(), aliases=None, flops=0, exps=0, scalar=None, limit=12):
    ins = list(ins)
    if ORDER:
        sizes = [(a.size if spec is None else a.size * 1024, i) for i, (a, spec) in enumerate(ins)]
        at = min(sizes)[1]
        ins[at] = (after(ins[at][0], ORDER[0]), ins[at][1])
    in_specs = [IN_VMEM if spec is None else spec for _, spec in ins]
    out_specs = [IN_VMEM if spec is None else spec for _, spec in outs]
    arrays = [
        a if spec is None else pltpu.with_memory_space_constraint(a, pltpu.HBM) for a, spec in ins
    ]
    count = 0
    if scalar is not None:
        arrays, count = [scalar] + arrays, 1
    results = pl.pallas_call(
        body,
        grid_spec=pltpu.PrefetchScalarGridSpec(
            num_scalar_prefetch=count,
            grid=grid,
            in_specs=in_specs,
            out_specs=out_specs,
            scratch_shapes=list(scratch),
        ),
        input_output_aliases=aliases or {},
        out_shape=[o if spec is None else pltpu.HBM(o.shape, o.dtype) for o, spec in outs],
        cost_estimate=pl.CostEstimate(
            flops=COSTS.get(name, 1), transcendentals=0, bytes_accessed=1
        ),
        compiler_params=pltpu.CompilerParams(vmem_limit_bytes=limit << 20),
        name=name,
    )(*arrays)
    ORDER[:] = [min(results, key=lambda a: a.size)]
    return results


def step_rows(size=BLOCK):
    return pl.ds(pl.multiple_of(pl.program_id(0) * size, size), size)


def held(*dims):
    return pl.BlockSpec(dims, lambda *_: (0,) * len(dims), pipeline_mode=pl.Buffered(1))


def by_step(*dims):
    return pl.BlockSpec(dims, lambda i, *_: (i,) + (0,) * (len(dims) - 1))


def row_spec(quarter, width, other):
    return pl.BlockSpec(
        (None, quarter, width), lambda i, c: ((1 - c[0]) if other else c[0], 0, 0)
    )


def split_inputs(activations, small, position, shard, padded):
    _, quarter, width = activations.shape
    extra = 16

    def body(at_ref, own_in, other_ref, small_ref, chip_ref, diagonal_ref, partner_ref, mine_ref):
        lane = lax.broadcasted_iota(jnp.int32, (1, width), 1)
        low = at_ref[1] * shard
        inside = (lane >= low) & (lane < low + shard)
        wide = jnp.concatenate([small_ref[0:6]] * (width // shard), axis=1)
        placed = jnp.where(inside, wide, 0.0).astype(BF)
        gap = jnp.zeros((1, padded - shard), F32)
        query_value = jnp.concatenate(
            [small_ref[6:7], gap, jnp.zeros((1, padded), F32), small_ref[7:8], gap], axis=1
        )
        hidden = jnp.concatenate([small_ref[8 + i : 9 + i] for i in range(4)], axis=1)
        rest = jnp.zeros((extra - 8, width), F32)
        mine = jnp.concatenate([to_float(placed), query_value, hidden, rest], axis=0)
        mine = to_float(mine.astype(BF))
        mine_ref[...] = mine
        chip_ref[:quarter] = own_in[...].astype(BF)
        chip_ref[quarter:] = mine.astype(BF)
        diagonal_ref[:quarter] = other_ref[...].astype(BF)
        diagonal_ref[quarter:] = mine.astype(BF)
        partner_ref[:quarter] = other_ref[...]
        partner_ref[quarter:] = mine

    dims = (quarter + extra, width)
    return launch(
        body,
        "split_inputs",
        [
            (activations, row_spec(quarter, width, False)),
            (activations, row_spec(quarter, width, True)),
            (small, None),
        ],
        [(shape(dims, BF), None)] * 2
        + [(shape(dims, F32), None), (shape((extra, width), F32), None)],
        scalar=position,
    )


def split_grads(out_grad, ids, core):
    _, quarter, width = out_grad.shape

    def body(core_ref, own_in, other_in, own_id, other_id, chip, diagonal, keep_ref, partner_ref):
        own = jnp.where(own_id[...] >= 0, own_in[...], 0.0)
        other = jnp.where(other_id[...] >= 0, other_in[...], 0.0)
        chip[...] = own.astype(BF)
        diagonal[...] = other.astype(BF)
        keep_ref[...] = own
        partner_ref[...] = other

    return launch(
        body,
        "split_grads",
        [
            (out_grad, row_spec(quarter, width, False)),
            (out_grad, row_spec(quarter, width, True)),
            (ids, row_spec(quarter, 1, False)),
            (ids, row_spec(quarter, 1, True)),
        ],
        [(shape((quarter, width), BF), None)] * 2
        + [(shape((quarter, width), F32), held(quarter, width)), (shape((quarter, width), F32), None)],
        scalar=core,
    )


def pack_attention(w_query, w_key, w_value, w_out):
    shard, width = w_out.shape
    padded = -(-shard // LANES) * LANES

    def body(q_ref, k_ref, v_ref, o_ref, out_ref):
        for i, ref in enumerate((q_ref, k_ref, v_ref, o_ref)):
            out_ref[i * padded : i * padded + shard] = ref[...].astype(BF)
            out_ref[i * padded + shard : (i + 1) * padded] = jnp.zeros((padded - shard, width), BF)

    full = pl.BlockSpec((shard, width), lambda i: (0, 0))
    return launch(
        body,
        "pack_attention",
        [(w_query.T, full), (w_key.T, full), (w_value.T, full), (w_out, full)],
        [(shape((4 * padded, width), BF), None)],
    )[0]


def pack_mlp(w_fc1, w_fc2):
    rows, columns = w_fc1.shape

    def body(up_ref, down_ref, up_out, down_out):
        at = step_rows(rows // 4)
        up_out[at] = up_ref[...].astype(BF)
        down_out[at] = down_ref[...].astype(BF)

    block = pl.BlockSpec((rows // 4, columns), lambda i: (i, 0))
    return launch(
        body,
        "pack_mlp",
        [(w_fc1, block), (w_fc2, block)],
        [(shape((rows, columns), BF), None)] * 2,
        grid=(4,),
    )


def project(activations, mine, pieces, weights, padded, core):
    _, quarter, width = activations.shape
    length = 4 * quarter
    columns = 3 * padded

    def body(core_ref, own, mine_ref, second, third, fourth, w_0, w_1, *outs):
        normed_ref, hat_ref, sides_ref, out_w, vec_ref, bias_ref, values = outs
        step = pl.program_id(0)
        pieces = (second, third, fourth)

        @pl.when(step == 0)
        def _():
            vec_ref[...] = mine_ref[0:6] + sum(
                to_float(ref[quarter : quarter + 6]) for ref in pieces
            )
            bias_ref[0:2] = mine_ref[6:8]
            bias_ref[2:4] = second[quarter + 6 : quarter + 8]
            out_w[0] = w_0[columns:]
            out_w[1] = w_1[columns:]
            values[...] = own[...]

        for i, piece in enumerate(pieces):

            @pl.when(step == i + 1)
            def _():
                values[...] = to_float(piece[:quarter])

        rows = step_rows(quarter)
        hat, _ = normalize(values[...])
        normed = (hat * vec_ref[0:1] + vec_ref[1:2]).astype(BF)
        normed_ref[...] = normed
        hat_ref[...] = hat.astype(BF)
        for side, w_ref in enumerate((w_0, w_1)):
            bias = bias_ref[2 * side : 2 * side + 1]
            sides_ref[side, rows] = (dot_nt(normed, w_ref[:columns]) + bias).astype(BF)

    return launch(
        body,
        "project",
        [(activations, row_spec(quarter, width, False))]
        + [(a, None) for a in (mine, *pieces, *weights)],
        [(shape((length, width), BF), by_step(quarter, width))] * 2
        + [(shape((2, length, columns), BF), None), (shape((2, padded, width), BF), None)]
        + [(shape((6, width), F32), None), (shape((4, width), F32), None)],
        grid=(4,),
        scratch=[pltpu.VMEM((quarter, width), F32)],
        scalar=core,
        flops=2 * length * width * 2 * columns,
    )


def lane_half():
    return lax.broadcasted_iota(jnp.int32, (1, LANES), 1) < HEAD_DIM


def head_place(head, first):
    block = slice((head // 2) * LANES, (head // 2 + 1) * LANES)
    return block, (first if head % 2 == 0 else ~first)


def attend(sides, marks, out_w, half_index, heads, dtype):
    _, length, columns = sides.shape
    padded, width = out_w.shape[1:]
    half = length // 2

    def body(sides, marks, w_ref, att_ref, inv_ref, e_ref, branch_ref, total_ref):
        side = pl.program_id(1)
        first = lane_half()
        here = step_rows()
        start = half_index * half + pl.program_id(0) * BLOCK
        rows = pl.ds(pl.multiple_of(start, BLOCK), BLOCK)
        mark_q = marks[rows, :LANES]
        mark_k = marks[:, LANES:]
        att = [jnp.zeros((BLOCK, LANES), F32)] * (padded // LANES)
        inv = list(att)
        for head in range(heads):
            block, lanes = head_place(head, first)
            scaled = to_float(sides[side, rows, block]) * (HEAD_DIM**-0.5 * LOG2_E)
            high = scaled.astype(BF)
            low = (scaled - to_float(high)).astype(BF)
            keys = sides[side, :, padded + block.start : padded + block.stop]
            left = jnp.concatenate(
                [jnp.where(lanes, high, mark_q), jnp.where(lanes, low, jnp.zeros_like(low))],
                axis=1,
            )
            right = jnp.concatenate([jnp.where(lanes, keys, mark_k), keys], axis=1)
            scores = dot_nt(left, right)
            exponent = jnp.exp2(scores - jnp.max(scores, axis=1, keepdims=True)).astype(BF)
            e_ref[head] = exponent
            values = sides[side, :, 2 * padded + block.start : 2 * padded + block.stop]
            both = dot_nn(exponent, jnp.concatenate([values, jnp.ones_like(values)], axis=1))
            inverse = 1.0 / both[:, LANES:]
            index = head // 2
            att[index] = jnp.where(lanes, both[:, :LANES] * inverse, att[index])
            inv[index] = jnp.where(lanes, inverse, inv[index])
        attended = jnp.concatenate(att, axis=1).astype(BF)
        att_ref[...] = attended
        inv_ref[...] = jnp.concatenate(inv, axis=1)
        part = dot_nn(attended, w_ref[side])

        @pl.when(side == 0)
        def _():
            total_ref[...] = part

        @pl.when(side == 1)
        def _():
            branch_ref[here] = (total_ref[...] + part).astype(dtype)

    block = pl.BlockSpec((None, BLOCK, padded), lambda i, j: (j, i, 0))
    return launch(
        body,
        f"attend_{half_index}",
        [(a, None) for a in (sides, marks, out_w)],
        [
            (shape((2, half, padded), BF), block),
            (shape((2, half, padded), F32), block),
            (
                shape((2 * heads, half, length), BF),
                pl.BlockSpec((heads, BLOCK, length), lambda i, j: (j, i, 0)),
            ),
            (shape((half, width), dtype), None),
        ],
        grid=(half // BLOCK, 2),
        scratch=[pltpu.VMEM((BLOCK, width), F32)],
        flops=8 * 2 * heads * half * length * 256,
        exps=2 * heads * half * length,
        limit=16,
    )


def second_norm(activations, core_piece, branch, received, vectors, core):
    half, width = branch.shape
    quarter = half // 2
    size = quarter // 2

    def body(core_ref, own, core_piece, branch_ref, recv_ref, vec, middle_ref, normed_ref, values):
        step = pl.program_id(0)
        here = step_rows(size)

        @pl.when(step < 2)
        def _():
            values[...] = own[...]

        @pl.when(step >= 2)
        def _():
            values[...] = core_piece[pl.ds(pl.multiple_of((step - 2) * size, size), size)]

        middle = values[...] + (branch_ref[here] + to_float(recv_ref[here]) + vec[2:3])
        middle_ref[...] = middle
        hat, _ = normalize(middle)
        normed_ref[here] = (hat * vec[3:4] + vec[4:5]).astype(BF)

    own_spec = pl.BlockSpec((None, size, width), lambda i, c: (c[0], jnp.minimum(i, 1), 0))
    return launch(
        body,
        "second_norm",
        [(activations, own_spec)] + [(a, None) for a in (core_piece, branch, received, vectors)],
        [(shape((half, width), F32), by_step(size, width)), (shape((half, width), BF), None)],
        grid=(4,),
        scratch=[pltpu.VMEM((size, width), F32)],
        scalar=core,
    )


def stack_weights(own, partner):
    def body(*refs):
        refs[4][0], refs[4][1] = refs[0][...], refs[1][...]
        refs[5][0], refs[5][1] = refs[2][...], refs[3][...]

    return launch(
        body,
        "stack_weights",
        [(a, None) for pair in zip(own, partner) for a in pair],
        [(shape((2, *a.shape), BF), None) for a in own],
    )


def mlp(normed, grad, ups, downs, bias, half_index, dtype, previous):
    rows, width = normed.shape
    hidden_size = ups.shape[2]

    def body(n_ref, g_0, g_1, up, down, bias, *rest):
        act_ref, hid_ref, out_ref, grad_ref, sum_ref, *totals = rest[len(previous) :]
        side = pl.program_id(1)
        start = half_index * rows + pl.program_id(0) * BLOCK
        shared = pl.ds(pl.multiple_of(start, BLOCK), BLOCK)

        @pl.when((pl.program_id(0) == 0) & (side == 0))
        def _():
            sum_ref[...] = jnp.zeros_like(sum_ref)

        here = step_rows()
        grad_rows = jnp.where(pl.program_id(0) == 0, g_0[...].astype(BF), g_1[...].astype(BF))
        normed_rows = n_ref[here]
        hidden = dot_nn(normed_rows, up[side]) + jnp.where(side == 0, bias[1:2], bias[3:4])
        grad_act = dot_nt(grad_rows, down[side])
        square = hidden * hidden
        th = jnp.tanh(hidden * (GELU_A + GELU_A * GELU_B * square))
        gate = 0.5 + 0.5 * th
        act = (hidden * gate).astype(BF)
        slope = gate + (0.5 * hidden) * (1.0 - th * th) * (GELU_A + 3.0 * GELU_A * GELU_B * square)
        grad_hidden = (grad_act * slope).astype(BF)
        act_ref[side, shared] = act
        hid_ref[side, shared] = grad_hidden
        sum_ref[side] += column_sum(grad_hidden)
        out = dot_nn(act, down[side])
        grad_in = dot_nt(grad_hidden, up[side])

        if dtype == F32:

            @pl.when(side == 0)
            def _():
                out_ref[...] = out
                grad_ref[...] = grad_in

            @pl.when(side == 1)
            def _():
                out_ref[...] += out
                grad_ref[...] += grad_in

        else:

            @pl.when(side == 0)
            def _():
                totals[0][...] = out
                totals[1][...] = grad_in

            @pl.when(side == 1)
            def _():
                out_ref[here] = (totals[0][...] + out).astype(dtype)
                grad_ref[here] = (totals[1][...] + grad_in).astype(dtype)

    return launch(
        body,
        f"mlp_{half_index}",
        [(a, None) for a in (normed, *grad, ups, downs, bias, *previous)],
        [(shape((2, 2 * rows, hidden_size), BF), None)] * 2
        + [(shape((rows, width), dtype), by_step(BLOCK, width) if dtype == F32 else None)] * 2
        + [(shape((2, 1, hidden_size), F32), None)],
        grid=(rows // BLOCK, 2),
        scratch=[] if dtype == F32 else [pltpu.VMEM((BLOCK, width), F32)] * 2,
        aliases={6 + i: i for i in range(len(previous))},
        flops=8 * rows * width * 2 * hidden_size,
        exps=rows * 2 * hidden_size,
        limit=12,
    )


def second_norm_back(middle, grad, received, grad_own, grad_partner, vectors):
    quarter, width = grad_own.shape
    size = quarter // 2

    def body(
        middle_ref, grad_ref, recv_ref, own, partner, vec, out_ref, first, second, sum_ref, values
    ):
        step = pl.program_id(0)
        here = step_rows(size)

        @pl.when(step < 2)
        def _():
            values[...] = own[...]

        @pl.when(step >= 2)
        def _():
            values[...] = partner[pl.ds(pl.multiple_of((step - 2) * size, size), size)]

        hat, inverse = normalize(middle_ref[...])
        incoming = grad_ref[...] + to_float(recv_ref[here])
        out = values[...] + norm_back(incoming * vec[3:4], hat, inverse)
        branch = out.astype(BF)
        out_ref[...] = out
        for i, ref in enumerate((first, second)):

            @pl.when(step // 2 == i)
            def _():
                ref[pl.ds(pl.multiple_of((step % 2) * size, size), size)] = branch

        sums = jnp.concatenate(
            [
                column_sum(incoming * hat),
                column_sum(incoming),
                column_sum(branch),
                column_sum(values[...].astype(BF)),
            ],
            axis=0,
        )

        @pl.when(step == 0)
        def _():
            sum_ref[...] = sums

        @pl.when(step > 0)
        def _():
            sum_ref[...] += sums

    dims = (2 * quarter, width)
    own_spec = pl.BlockSpec((size, width), lambda i: (jnp.minimum(i, 1), 0))
    return launch(
        body,
        "second_norm_back",
        [(middle, by_step(size, width)), (grad, by_step(size, width)), (received, None)]
        + [(grad_own, own_spec), (grad_partner, None), (vectors, None)],
        [
            (shape(dims, F32), by_step(size, width)),
            (shape((quarter, width), BF), None),
            (shape((quarter, width), BF), None),
            (shape((4, width), F32), None),
        ],
        grid=(4,),
        scratch=[pltpu.VMEM((size, width), F32)],
    )


def mlp_weight_grads(normed, grads, activated, hidden):
    rows, width = normed[0].shape
    size = hidden.shape[2]

    def body(n_0, n_1, g_0, g_1, g_2, g_3, act_ref, hid_ref, *outs):
        kept_ref, sent_refs = outs[0], outs[1:]
        side = 1 - pl.program_id(0)
        first, second = slice(0, rows), slice(rows, 2 * rows)
        up = dot_tn(n_0[...], hid_ref[side, first]) + dot_tn(n_1[...], hid_ref[side, second])
        down, at = None, rows // 2
        for i, ref in enumerate((g_0, g_1, g_2, g_3)):
            part = dot_tn(act_ref[side, i * at : (i + 1) * at], ref[...].astype(BF))
            down = part if down is None else down + part

        @pl.when(side == 0)
        def _():
            kept_ref[:width] = up.astype(BF)
            kept_ref[width:] = down.astype(BF)

        @pl.when(side == 1)
        def _():
            for i, ref in enumerate(sent_refs):
                at = (i % 2) * (width // 2)
                ref[...] = (up, down)[i // 2][at : at + width // 2].astype(BF)

    dims = (width + size, width)
    piece = (width // 2, width)
    return launch(
        body,
        "mlp_weight_grads",
        [(a, None) for a in (*normed, *grads, activated, hidden)],
        [(shape(dims, BF), None)] + [(shape(piece, BF), None)] * 4,
        grid=(2,),
        flops=16 * rows * width * size,
        limit=14,
    )


def attend_back(
    grads, out_w, attended, inverse, exponent, sides, first, block_index, heads, previous, last
):
    _, length, columns = sides.shape
    padded = columns // 3
    quarter, width = grads[0].shape
    count = len(grads)

    def body(*refs):
        grad_refs = refs[:count]
        w_ref, at_ref, inv_ref, sides, e_ref = refs[count : count + 5]
        dq_ref, dk_sum, dv_sum, *rounded = refs[count + 5 + len(previous) :]
        step, side = pl.program_id(0), pl.program_id(1)
        rows = pl.ds(pl.multiple_of((first + step) * quarter, quarter), quarter)

        if not previous:

            @pl.when(step == 0)
            def _():
                dk_sum[side] = jnp.zeros((length, padded), F32)
                dv_sum[side] = jnp.zeros((length, padded), F32)

        head_lanes = lane_half()
        lane = lax.broadcasted_iota(jnp.int32, (1, LANES), 1)
        zero = jnp.zeros((), BF)
        grad_rows = grad_refs[0][...]
        if count == 2:
            grad_rows = jnp.where(step == 0, grad_rows, grad_refs[1][...])
        grad_att = to_float(dot_nt(grad_rows, w_ref[side]).astype(BF))
        scaled = (grad_att * inv_ref[...]).astype(BF)
        product = to_float(scaled) * to_float(at_ref[...])
        dq = [None] * (padded // LANES)
        for head in range(heads):
            block, lanes = head_place(head, head_lanes)
            keys = sides[side, :, padded + block.start : padded + block.stop]
            values = sides[side, :, 2 * padded + block.start : 2 * padded + block.stop]
            grad_head = jnp.where(lanes, scaled[:, block], zero)
            centre = -jnp.sum(jnp.where(lanes, product[:, block], 0.0), axis=1, keepdims=True)
            high = centre.astype(BF)
            low = (centre - to_float(high)).astype(BF)
            extra = jnp.where(lane == 0, high, jnp.where(lane == 1, low, zero))
            grad_probs = dot_nt(
                jnp.concatenate([grad_head, extra], axis=1),
                jnp.concatenate([values, jnp.ones_like(values)], axis=1),
            )
            probs = e_ref[head]
            grad_scores = (to_float(probs) * grad_probs).astype(BF)
            part = dot_nn(grad_scores, jnp.where(lanes, keys, zero))
            index = head // 2
            dq[index] = part if dq[index] is None else dq[index] + part
            queries = jnp.where(lanes, sides[side, rows, block], zero)
            dk_sum[side, :, block] += dot_tn(grad_scores, queries)
            dv_sum[side, :, block] += dot_tn(probs, grad_head)
        at = pl.ds(pl.multiple_of(step * quarter, quarter), quarter)
        dq_ref[side, at] = (jnp.concatenate(dq, axis=1) * HEAD_DIM**-0.5).astype(BF)

        if last:

            @pl.when(step == count - 1)
            def _():
                rounded[0][side] = (dk_sum[side] * HEAD_DIM**-0.5).astype(BF)
                rounded[1][side] = dv_sum[side].astype(BF)

    block = pl.BlockSpec((None, quarter, padded), lambda i, j: (j, block_index + i, 0))
    ins = [(a, None) for a in grads]
    ins += [(out_w, None), (attended, block), (inverse, block), (sides, None)]
    ins += [
        (exponent, pl.BlockSpec((heads, quarter, length), lambda i, j: (j, block_index + i, 0)))
    ]
    ins += [(a, None) for a in previous]
    return launch(
        body,
        f"attend_back_{first}",
        ins,
        [(shape((2, count * quarter, padded), BF), None)]
        + [(shape((2, length, padded), F32), None)] * 2
        + ([(shape((2, length, padded), BF), None)] * 2 if last else []),
        grid=(count, 2),
        aliases={count + 5 + i: 1 + i for i in range(len(previous))},
        flops=16 * 2 * heads * count * quarter * length * 256,
        limit=18,
    )


def input_grad(queries, keys, values, weights, hat, half_index, dtype):
    half = hat.shape[0] // 2
    width, padded = hat.shape[1], keys.shape[2]
    count = len(queries)
    size = half // count

    def body(*refs):
        query_refs = refs[:count]
        k_ref, v_ref, w_0, w_1, hat_ref, out_ref, sum_ref = refs[count:]
        sums = None
        for i, q_ref in enumerate(query_refs):
            at = slice(i * size, (i + 1) * size)
            rows = slice(half_index * half + i * size, half_index * half + (i + 1) * size)
            total = None
            for side, w_ref in enumerate((w_0, w_1)):
                left = jnp.concatenate([q_ref[side], k_ref[side, rows], v_ref[side, rows]], axis=1)
                part = dot_nn(left, w_ref[: 3 * padded])
                total = part if total is None else total + part
            out_ref[at] = total.astype(dtype)
            part = [column_sum(total * to_float(hat_ref[at])), column_sum(total)]
            part = jnp.concatenate(part, axis=0)
            sums = part if sums is None else sums + part
        sum_ref[...] = sums

    return launch(
        body,
        f"input_grad_{half_index}",
        [(a, None) for a in (*queries, keys, values, *weights)]
        + [(hat, pl.BlockSpec((half, width), lambda i: (half_index, 0)))],
        [
            (shape((half, width), dtype), held(half, width) if dtype == F32 else None),
            (shape((2, width), F32), None),
        ],
        flops=2 * half * 6 * padded * width,
    )


def attention_weight_grad(attended, grads, queries, keys, values, normed, shard, side):
    length, width = normed.shape
    padded = keys.shape[2]
    half, quarter = length // 2, length // 4

    def body(*refs):
        at_refs, grad_refs, query_refs = refs[:2], refs[2:6], refs[6:9]
        k_ref, v_ref, n_ref, *outs = refs[9:]
        out_w = None
        for i, ref in enumerate(grad_refs):
            rows = slice((i % 2) * quarter, (i % 2 + 1) * quarter)
            part = dot_tn(at_refs[i // 2][rows], ref[...])
            out_w = part if out_w is None else out_w + part
        query, at = None, 0
        for ref in query_refs:
            rows = ref[side]
            part = dot_tn(rows, n_ref[at : at + rows.shape[0]])
            query, at = part if query is None else query + part, at + rows.shape[0]
        key = dot_tn(k_ref[side], n_ref[...])
        value = dot_tn(v_ref[side], n_ref[...])
        for i, part in enumerate((out_w, query, key, value)):
            if side:
                outs[i][...] = part[:shard].astype(BF)
            else:
                outs[0][i * shard : (i + 1) * shard] = part[:shard].astype(BF)

    at_spec = pl.BlockSpec((None, half, padded), lambda i: (side, 0, 0))
    dims = (4 * shard, width)
    return launch(
        body,
        ("attention_kept", "attention_sent")[side],
        [(a, at_spec) for a in attended]
        + [(a, None) for a in (*grads, *queries, keys, values)]
        + [(normed, held(*normed.shape))],
        [(shape((shard, width), BF), None)] * 4 if side else [(shape(dims, BF), None)],
        flops=2 * length * 4 * padded * width,
        limit=14,
    )


def small_grads(norms, lates, queries, values, up_sums):
    width = lates[0].shape[1]
    padded = values.shape[2]
    split = len(norms), len(lates), len(queries), 1, len(up_sums)

    def body(*refs):
        groups, at = [], 0
        for n in split:
            groups.append(refs[at : at + n])
            at += n
        norms, lates, queries, (v_ref,), ups = groups
        wide_ref, bias_ref = refs[at:]
        wide = [sum(ref[...] for ref in norms), sum(ref[...] for ref in lates)]
        wide_ref[...] = jnp.concatenate(wide, axis=0).astype(BF)
        for side in range(2):
            bias = [
                sum(column_sum(ref[side]) for ref in queries),
                column_sum(v_ref[side]),
                jnp.zeros((1, width - 2 * padded), F32),
            ]
            both = [jnp.concatenate(bias, axis=1), sum(ref[side] for ref in ups)]
            bias_ref[2 * side : 2 * side + 2] = jnp.concatenate(both, axis=0)

    return launch(
        body,
        "small_grads",
        [(a, None) for a in (*norms, *lates, *queries, values, *up_sums)],
        [(shape((6, width), BF), None), (shape((4, width), F32), None)],
    )


def small_chip(wide, received, bias):
    width = wide.shape[1]

    def body(wide_ref, recv_ref, bias_ref, own_ref, sent_ref):
        total = to_float(wide_ref[...]) + to_float(recv_ref[...])
        own_ref[...] = jnp.concatenate([total, bias_ref[0:2]], axis=0)
        sent_ref[...] = jnp.concatenate([total, bias_ref[2:4]], axis=0)

    return launch(
        body,
        "small_chip",
        [(wide, None), (received, None), (bias, None)],
        [(shape((8, width), F32), None)] * 2,
    )


def small_sum(own, received):
    def body(own_ref, recv_ref, out_ref):
        out_ref[...] = (own_ref[...] + recv_ref[...]).astype(BF)

    return launch(
        body, "small_sum", [(own, None), (received, None)], [(shape(own.shape, BF), None)]
    )[0]


def home_spec(quarter, width):
    return pl.BlockSpec((None, quarter, width), lambda i, c: (c[0], 0, 0))


def first_norm_back(activations, core_piece, grad_middle, grad, received, vectors, core):
    half, width = grad.shape
    quarter = half // 2

    def body(core_ref, own, core_piece, middle_ref, grad_ref, recv_ref, vec, home_ref, sent_ref):
        for i, piece in enumerate((own, core_piece)):
            rows = slice(i * quarter, (i + 1) * quarter)
            hat, inverse = normalize(piece[:quarter])
            incoming = grad_ref[rows] + to_float(recv_ref[rows])
            out = middle_ref[rows] + norm_back(incoming * vec[0:1], hat, inverse)
            (home_ref, sent_ref)[i][...] = out

    return launch(
        body,
        "first_norm_back",
        [(activations, row_spec(quarter, width, False)), (core_piece, None)]
        + [(grad_middle, held(half, width)), (grad, held(half, width))]
        + [(received, None), (vectors, None)],
        [
            (shape((2, quarter, width), F32), home_spec(quarter, width)),
            (shape((quarter, width), F32), None),
        ],
        scalar=core,
    )


def finish_output(middle, out, received, vectors, core):
    half, width = middle.shape
    quarter = half // 2

    def body(core_ref, middle_ref, out_ref, recv_ref, vec, home_ref, sent_ref):
        total = middle_ref[...] + (out_ref[...] + to_float(recv_ref[...]) + vec[5:6])
        home_ref[...] = total[:quarter]
        sent_ref[...] = total[quarter:]

    return launch(
        body,
        "finish_output",
        [(middle, held(half, width)), (out, held(half, width)), (received, None), (vectors, None)],
        [
            (shape((2, quarter, width), F32), home_spec(quarter, width)),
            (shape((quarter, width), F32), None),
        ],
        scalar=core,
    )


def swap(values, axis, size, bit):
    return lax.ppermute(values, axis, [(i, i ^ bit) for i in range(size)])


def core_swap(values):
    return swap(values, "group", 4, 1)


def chip_swap(values):
    return swap(values, "group", 4, 2)


def diagonal_swap(values):
    return swap(values, "group", 4, 3)


def divide(kept, received, mine, count):
    rows, width = kept.shape
    part = rows // count
    total = len(received)

    def body(mine_ref, kept_ref, *refs):
        recv_refs, out_refs = refs[:total], refs[total:]
        for k in range(count):
            at = pl.ds(pl.multiple_of((mine_ref[0] ^ k) * part, 8), part)
            value = to_float(kept_ref[at])
            for ref in recv_refs:
                value = value + to_float(ref[at])
            out_refs[k][...] = value.astype(BF)

    return launch(
        body,
        "divide",
        [(kept, held(rows, width))] + [(a, None) for a in received],
        [(shape((part, width), BF), held(part, width))] + [(shape((part, width), BF), None)] * (count - 1),
        scalar=mine,
    )


def divide_first(kept, pieces, mine):
    rows, width = kept.shape
    part, size = rows // 2, rows // 4

    def body(mine_ref, kept_ref, p_0, p_1, p_2, p_3, own_ref, sent_ref):
        for k, out_ref in enumerate((own_ref, sent_ref)):
            which = mine_ref[0] ^ k
            for j, (low, high) in enumerate(((p_0, p_2), (p_1, p_3))):
                at = pl.ds(pl.multiple_of(which * part + j * size, 8), size)
                got = jnp.where(which == 0, to_float(low[...]), to_float(high[...]))
                out_ref[j * size : (j + 1) * size] = (to_float(kept_ref[at]) + got).astype(BF)

    return launch(
        body,
        "divide",
        [(a, None) for a in (kept, *pieces)],
        [(shape((part, width), BF), held(part, width)), (shape((part, width), BF), None)],
        scalar=mine,
    )


def add_all(kept, received, extra):
    rows, width = kept.shape
    below = extra.shape[0] if extra is not None else 0

    def body(kept_ref, *refs):
        out_ref = refs[-1]
        value = to_float(kept_ref[...])
        for ref in refs[: len(received)]:
            value = value + to_float(ref[...])
        out_ref[:rows] = value.astype(BF)
        if below:
            out_ref[rows:] = refs[-2][...]

    return launch(
        body,
        "add_all",
        [(kept, held(rows, width))]
        + [(a, None) for a in received]
        + ([(extra, None)] if below else []),
        [(shape((rows + below, width), BF), None)],
    )[0]


def join(parts, mine, extra):
    rows, width = parts[0].shape
    part, count = rows - extra, len(parts)

    def body(mine_ref, *refs):
        out_ref = refs[-1]
        for k in range(count):
            at = pl.ds(pl.multiple_of((mine_ref[0] ^ k) * part, 8), part)
            out_ref[at] = refs[k][:part]
        if extra:
            out_ref[count * part :] = sum(to_float(ref[part:]) for ref in refs[:-1]).astype(BF)

    return launch(
        body,
        "join",
        [(a, None) for a in parts],
        [(shape((count * part + extra, width), BF), None)],
        scalar=mine,
    )[0]


def join_weights(parts, mine, shard, extra):
    rows, width = parts[0].shape
    part, count = rows - extra, len(parts)

    def body(mine_ref, *refs):
        total, outs = refs[-1], refs[count : count + 5]
        for k in range(count):
            at = pl.ds(pl.multiple_of((mine_ref[0] ^ k) * part, 8), part)
            total[at] = to_float(refs[k][:part])
        for i in range(4):
            outs[i][...] = total[i * shard : (i + 1) * shard]
        outs[4][...] = sum(to_float(ref[part:]) for ref in refs[:count])

    return launch(
        body,
        "join_weights",
        [(a, None) for a in parts],
        [(shape((shard, width), F32), held(shard, width))] * 4 + [(shape((extra, width), F32), None)],
        scratch=[pltpu.VMEM((count * part, width), F32)],
        scalar=mine,
    )


def join_mlp(parts, mine):
    def body(mine_ref, first_ref, second_ref, up_ref, down_ref):
        for ref, which in ((first_ref, mine_ref[0]), (second_ref, 1 - mine_ref[0])):
            for index, out_ref in enumerate((up_ref, down_ref)):

                @pl.when(which == index)
                def _():
                    out_ref[...] = to_float(ref[...])

    dims = parts[0].shape
    return launch(
        body,
        "join_mlp",
        [(a, None) for a in parts],
        [(shape(dims, F32), held(*dims))] * 2,
        scalar=mine,
    )


class ReplicaSum:
    def __init__(self, kept, received, size, first, others):
        self.kept, self.received, self.size = kept, received, size
        self.groups, bit, bits = [], 1, size.bit_length() - 1
        while bit < size:
            take = min(first if bit == 1 else others, bits)
            self.groups.append((bit, 1 << take))
            bit, bits = bit << take, bits - take
        self.at, self.rows = 0, None

    def mine(self):
        bit, count = self.groups[self.at]
        return (lax.axis_index("replica") // bit) % count

    def exchange(self, values, k):
        bit, _ = self.groups[self.at]
        return swap(values, "replica", self.size, k * bit)

    def divide(self):
        _, count = self.groups[self.at]
        mine = self.mine().astype(jnp.int32)
        part = self.kept.shape[0] // count
        if self.at == 0:
            parts = divide_first(self.kept, self.received, mine.reshape(1))
        elif part % 8 == 0:
            parts = divide(self.kept, self.received, mine.reshape(1), count)
        else:
            value = to_float(self.kept)
            for received in self.received:
                value = value + to_float(received)
            parts = [
                lax.dynamic_slice_in_dim(value, (mine ^ k) * part, part, 0).astype(BF)
                for k in range(count)
            ]
        self.kept, self.sent = parts[0], parts[1:]

    def send(self):
        self.received = [self.exchange(a, k + 1) for k, a in enumerate(self.sent)]
        self.at += 1

    def scatter(self):
        self.divide()
        self.send()

    def total(self, extra=None):
        while self.at < len(self.groups):
            self.scatter()
        self.extra = 0 if extra is None else extra.shape[0]
        self.rows = add_all(self.kept, self.received, extra)

    def collect(self):
        self.at -= 1
        _, count = self.groups[self.at]
        self.parts = [self.rows] + [self.exchange(self.rows, k) for k in range(1, count)]

    def combine(self, final=None):
        mine = self.mine().astype(jnp.int32)
        part = self.parts[0].shape[0] - self.extra
        if final is not None:
            self.rows = final(self.parts, mine.reshape(1))
            return
        if part % 8 == 0:
            self.rows = join(self.parts, mine.reshape(1), self.extra)
            return
        width = self.parts[0].shape[1]
        value = jnp.zeros((len(self.parts) * part, width), BF)
        for k, a in enumerate(self.parts):
            value = lax.dynamic_update_slice(value, a[:part], ((mine ^ k) * part, 0))
        below = sum(to_float(a[part:]) for a in self.parts).astype(BF)
        self.rows = jnp.concatenate([value, below], axis=0)


def per_device(
    replicas,
    activations,
    out_grad,
    picture_ids,
    ln1_gain,
    ln1_bias,
    w_query,
    q_bias,
    w_key,
    w_value,
    v_bias,
    w_out,
    out_bias,
    ln2_gain,
    ln2_bias,
    w_fc1,
    fc1_bias,
    w_fc2,
    fc2_bias,
):
    ORDER.clear()
    row_block, quarter, width = activations.shape
    assert row_block == 2
    shard = w_query.shape[1]
    heads = shard // HEAD_DIM
    padded = -(-shard // LANES) * LANES
    half = 2 * quarter
    group = lax.axis_index("group")
    core_index = group % 2
    core = core_index.astype(jnp.int32).reshape(1)

    small = jnp.concatenate(
        [ln1_gain, ln1_bias, out_bias, ln2_gain, ln2_bias, fc2_bias, q_bias, v_bias, fc1_bias]
    ).reshape(-1, shard)
    position = jnp.stack([core_index, group]).astype(jnp.int32)
    to_chip, to_diagonal, to_core, mine = split_inputs(
        activations, small, position, shard, padded
    )
    from_chip, from_diagonal = chip_swap(to_chip), diagonal_swap(to_diagonal)
    core_piece = core_swap(to_core)

    packed = pack_attention(w_query, w_key, w_value, w_out)
    w_att = packed, core_swap(packed)
    own_ids = lax.dynamic_slice_in_dim(picture_ids, group * quarter, quarter, 1)[..., None]
    grad_to_chip, grad_to_diagonal, grad_own, grad_to_core = split_grads(out_grad, own_ids, core)
    grad_core = core_swap(grad_to_core)
    grad_far = chip_swap(grad_to_chip), diagonal_swap(grad_to_diagonal)
    grad_near = grad_to_chip, grad_core
    up_own, down_own = pack_mlp(w_fc1, w_fc2)
    up_core, down_core = core_swap(up_own), core_swap(down_own)

    row_ids = lax.dynamic_index_in_dim(picture_ids, core_index, 0, keepdims=False)
    row_ids = row_ids.reshape(4, quarter)
    ids = jnp.concatenate(
        [lax.dynamic_index_in_dim(row_ids, group ^ i, 0, keepdims=False) for i in range(4)]
    )
    lane = jnp.arange(2 * LANES)
    same = ids[:, None] == (lane % HEAD_DIM - 1)[None, :]
    marks = jnp.where(
        lane[None, :] < LANES, jnp.where(same, 0.0, 1.0), jnp.where(same, MASKED, 0.0)
    ).astype(BF)

    normed_one, hat_one, sides, out_w, vectors, bias = project(
        activations, mine, (core_piece, from_chip, from_diagonal), w_att, padded, core
    )
    att_1, inv_1, exp_1, branch_1 = attend(sides, marks, out_w, 1, heads, BF)
    branch_received = chip_swap(branch_1)
    att_0, inv_0, exp_0, branch_0 = attend(sides, after(marks, *grad_far), out_w, 0, heads, F32)
    ups, downs = stack_weights((up_own, down_own), (up_core, down_core))
    middle, normed_own = second_norm(
        activations, core_piece, branch_0, branch_received, vectors, core
    )
    normed_two = normed_own, chip_swap(normed_own)

    activated, hidden, mlp_0, back_0, up_sum_0 = mlp(
        normed_two[0], grad_near, ups, downs, bias, 0, F32, ()
    )
    activated, hidden, mlp_1, back_1, up_sum_1 = mlp(
        normed_two[1], grad_far, ups, downs, bias, 1, BF, (activated, hidden)
    )
    grad_received = chip_swap(back_1)

    state = {}

    def advance(name):
        pending = state[name]
        if pending.rows is None and pending.at < len(pending.groups):
            pending.scatter()
        elif pending.rows is None:
            pending.total(state["small"] if name == "a" else None)
            pending.collect()
        elif pending.at > 0:
            pending.combine()
            pending.collect()

    def attention_grads(side):
        return attention_weight_grad(
            (att_0, att_1),
            (*state["branch"], *branches_far),
            (dq_0, *dq_1),
            state["dk"],
            state["dv"],
            normed_one,
            shard,
            side,
        )

    branches_far, dq_1 = [], []
    for token in SEQUENCE:
        if token == "W":
            kept, *sent = mlp_weight_grads(normed_two, grad_near + grad_far, activated, hidden)
            received = [core_swap(piece) for piece in sent]
            state["m"] = ReplicaSum(kept, received, replicas, *MLP_GROUPS)
        elif token == "R":
            state["out"] = chip_swap(after(mlp_1, ORDER[0]))
        elif token == "N":
            grad_middle, *branch, late_sums = second_norm_back(
                middle, back_0, grad_received, grad_own, grad_core, vectors
            )
            state["branch"] = branch
            branches_far.extend(chip_swap(piece) for piece in branch)
        elif token == "B0":
            dq_0, *key_sums = attend_back(
                state["branch"], out_w, att_0, inv_0, exp_0, sides, 0, 0, heads, (), False
            )
        elif token == "B2":
            dq, *key_sums = attend_back(
                branches_far[:1], out_w, att_1, inv_1, exp_1, sides, 2, 0, heads, key_sums, False
            )
            dq_1.append(dq)
        elif token == "B3":
            dq, _, _, state["dk"], state["dv"] = attend_back(
                branches_far[1:], out_w, att_1, inv_1, exp_1, sides, 3, 1, heads, key_sums, True
            )
            dq_1.append(dq)
        elif token == "A1":
            state["sent"] = [core_swap(piece) for piece in attention_grads(1)]
        elif token == "A0":
            state["a"] = ReplicaSum(attention_grads(0)[0], state["sent"], replicas, *ATT_GROUPS)
        elif token == "I1":
            first_1, norm_1 = input_grad(dq_1, state["dk"], state["dv"], w_att, hat_one, 1, BF)
            if RS4_EARLY:
                first_received = chip_swap(first_1)
        elif token == "I0":
            first_0, norm_0 = input_grad([dq_0], state["dk"], state["dv"], w_att, hat_one, 0, F32)
        elif token == "G":
            wide, bias_sums = small_grads(
                (norm_0, norm_1), [late_sums], (dq_0, *dq_1), state["dv"], [up_sum_0, up_sum_1]
            )
            wide_received = chip_swap(wide)
            if not RS4_EARLY:
                first_received = chip_swap(after(first_1, wide))
        elif token == "F":
            output_home, output_sent = finish_output(middle, mlp_0, state["out"], vectors, core)
            output_received = core_swap(output_sent)
        elif token == "C":
            small_own, small_sent = small_chip(wide, wide_received, bias_sums)
            small_core = core_swap(small_sent)
        elif token == "U":
            state["small"] = small_sum(small_own, small_core)
        elif token == "L":
            input_home, input_sent = first_norm_back(
                activations, core_piece, grad_middle, first_0, first_received, vectors, core
            )
            input_received = core_swap(input_sent)
        elif token == "J":
            while state["m"].rows is None or state["m"].at > 0:
                advance("m")
            state["m"].combine(join_mlp)
        else:
            advance(token)
    while state["a"].rows is None or state["a"].at > 0:
        advance("a")
    if "J" not in SEQUENCE:
        while state["m"].rows is None or state["m"].at > 0:
            advance("m")
        state["m"].combine(join_mlp)
    state["a"].combine(lambda parts, mine: join_weights(parts, mine, shard, 8))
    weights, small = state["a"].rows[:4], state["a"].rows[4]
    mlp_sum = state["m"]

    def place(home, received):
        return lax.dynamic_update_slice(home, received[None], (1 - core_index, 0, 0))

    mine = lax.dynamic_slice_in_dim(small[:6], group * shard, shard, 1)

    return (
        place(output_home, output_received),
        place(input_home, input_received),
        mine[0],
        mine[1],
        weights[1].T,
        small[6, :shard],
        weights[2].T,
        weights[3].T,
        small[6, padded : padded + shard],
        weights[0],
        mine[4],
        mine[2],
        mine[3],
        mlp_sum.rows[0],
        small[7],
        mlp_sum.rows[1],
        mine[5],
    )


def solution(mesh):
    replicas = mesh.shape["replica"]
    assert mesh.shape["group"] == 4
    patches = P("replica", "group", None)
    vector = P("group")
    columns = P(None, "group")
    rows = P("group", None)
    parameters = (vector, vector, columns, vector, columns, columns, vector, rows)
    parameters += (vector, vector, vector, columns, vector, rows, vector)

    def program(*arguments):
        return per_device(replicas, *arguments)

    return jax.shard_map(
        program,
        mesh=mesh,
        in_specs=(patches, patches, P("replica", None)) + parameters,
        out_specs=(patches, patches) + parameters,
        check_vma=False,
    )
```

```python
import jax
import jax.numpy as jnp
from jax import lax
from jax.experimental import pallas as pl
from jax.experimental.pallas import tpu as pltpu
from jax.sharding import PartitionSpec as P

HEAD_DIM = 64
EPS = 1e-06
MASKED = -1e30
BF = jnp.bfloat16
F32 = jnp.float32
LANES = 128
LOG2_E = 1.4426950408889634
GELU_A = 0.7978845608028654
GELU_B = 0.044715
BLOCK = 256


def to_float(values):
    return values.astype(F32)


def dot_nn(left, right):
    return jnp.dot(left, right, preferred_element_type=F32)


def dot_nt(left, right):
    return lax.dot_general(left, right, (((1,), (1,)), ((), ())), preferred_element_type=F32)


def dot_tn(left, right):
    return lax.dot_general(left, right, (((0,), (0,)), ((), ())), preferred_element_type=F32)


def normalize(values):
    centred = values - jnp.mean(values, axis=-1, keepdims=True)
    inverse = lax.rsqrt(jnp.mean(centred * centred, axis=-1, keepdims=True) + EPS)
    return (centred * inverse, inverse)


def norm_back(grad_hat, normed_hat, inverse):
    return inverse * (
        grad_hat
        - jnp.mean(grad_hat, axis=-1, keepdims=True)
        - normed_hat * jnp.mean(grad_hat * normed_hat, axis=-1, keepdims=True)
    )


def column_sum(values):
    return jnp.sum(to_float(values), axis=0, keepdims=True)


def shape(dims, dtype):
    return jax.ShapeDtypeStruct(dims, dtype)


def after(value, *others):
    return lax.optimization_barrier((value, *others))[0]


SEQUENCE = (
    "W", "m", "R", "N", "B0", "B2", "m", "B3", "A1", "m",
    "A0", "a", "m", "I1", "I0", "F", "a", "m", "G", "C",
    "U", "m", "a", "a", "L", "J",
)
COSTS = {
    "project": 8000000000,
    "attend_1": 8000000000,
    "attend_0": 8000000000,
    "mlp_0": 8000000000,
    "mlp_1": 8000000000,
    "attend_back_0": 14000000000,
    "attend_back_3": 8000000000,
    "input_grad_0": 4000000000,
    "finish_output": 4000000000,
}
MLP_GROUPS = (1, 1)
ATT_GROUPS = (1, 1)
RS4_EARLY = True
ORDER = []
IN_VMEM = pl.BlockSpec(memory_space=pltpu.VMEM)


def launch(body, name, ins, outs, grid=(1,), scratch=(), aliases=None, flops=0, exps=0, scalar=None, limit=12):
    ins = list(ins)
    if ORDER:
        sizes = [(a.size if spec is None else a.size * 1024, i) for i, (a, spec) in enumerate(ins)]
        at = min(sizes)[1]
        ins[at] = (after(ins[at][0], ORDER[0]), ins[at][1])
    in_specs = [IN_VMEM if spec is None else spec for _, spec in ins]
    out_specs = [IN_VMEM if spec is None else spec for _, spec in outs]
    arrays = [
        a if spec is None else pltpu.with_memory_space_constraint(a, pltpu.HBM) for a, spec in ins
    ]
    count = 0
    if scalar is not None:
        arrays, count = [scalar] + arrays, 1
    results = pl.pallas_call(
        body,
        grid_spec=pltpu.PrefetchScalarGridSpec(
            num_scalar_prefetch=count,
            grid=grid,
            in_specs=in_specs,
            out_specs=out_specs,
            scratch_shapes=list(scratch),
        ),
        input_output_aliases=aliases or {},
        out_shape=[o if spec is None else pltpu.HBM(o.shape, o.dtype) for o, spec in outs],
        cost_estimate=pl.CostEstimate(
            flops=COSTS.get(name, 1), transcendentals=0, bytes_accessed=1
        ),
        compiler_params=pltpu.CompilerParams(vmem_limit_bytes=limit << 20),
        name=name,
    )(*arrays)
    ORDER[:] = [min(results, key=lambda a: a.size)]
    return results


def step_rows(size=BLOCK):
    return pl.ds(pl.multiple_of(pl.program_id(0) * size, size), size)


def held(*dims):
    return pl.BlockSpec(dims, lambda *_: (0,) * len(dims), pipeline_mode=pl.Buffered(1))


def by_step(*dims):
    return pl.BlockSpec(dims, lambda i, *_: (i,) + (0,) * (len(dims) - 1))


def row_spec(quarter, width, other):
    return pl.BlockSpec(
        (None, quarter, width), lambda i, c: ((1 - c[0]) if other else c[0], 0, 0)
    )


def split_inputs(activations, small, position, shard, padded):
    _, quarter, width = activations.shape
    extra = 16

    def body(at_ref, own_in, other_ref, small_ref, chip_ref, diagonal_ref, partner_ref, mine_ref):
        lane = lax.broadcasted_iota(jnp.int32, (1, width), 1)
        low = at_ref[1] * shard
        inside = (lane >= low) & (lane < low + shard)
        wide = jnp.concatenate([small_ref[0:6]] * (width // shard), axis=1)
        placed = jnp.where(inside, wide, 0.0).astype(BF)
        gap = jnp.zeros((1, padded - shard), F32)
        query_value = jnp.concatenate(
            [small_ref[6:7], gap, jnp.zeros((1, padded), F32), small_ref[7:8], gap], axis=1
        )
        hidden = jnp.concatenate([small_ref[8 + i : 9 + i] for i in range(4)], axis=1)
        rest = jnp.zeros((extra - 8, width), F32)
        mine = jnp.concatenate([to_float(placed), query_value, hidden, rest], axis=0)
        mine = to_float(mine.astype(BF))
        mine_ref[...] = mine
        chip_ref[:quarter] = own_in[...].astype(BF)
        chip_ref[quarter:] = mine.astype(BF)
        diagonal_ref[:quarter] = other_ref[...].astype(BF)
        diagonal_ref[quarter:] = mine.astype(BF)
        partner_ref[:quarter] = other_ref[...]
        partner_ref[quarter:] = mine

    dims = (quarter + extra, width)
    return launch(
        body,
        "split_inputs",
        [
            (activations, row_spec(quarter, width, False)),
            (activations, row_spec(quarter, width, True)),
            (small, None),
        ],
        [(shape(dims, BF), None)] * 2
        + [(shape(dims, F32), None), (shape((extra, width), F32), None)],
        scalar=position,
    )


def split_grads(out_grad, ids, core):
    _, quarter, width = out_grad.shape

    def body(core_ref, own_in, other_in, own_id, other_id, chip, diagonal, keep_ref, partner_ref):
        own = jnp.where(own_id[...] >= 0, own_in[...], 0.0)
        other = jnp.where(other_id[...] >= 0, other_in[...], 0.0)
        chip[...] = own.astype(BF)
        diagonal[...] = other.astype(BF)
        keep_ref[...] = own
        partner_ref[...] = other

    return launch(
        body,
        "split_grads",
        [
            (out_grad, row_spec(quarter, width, False)),
            (out_grad, row_spec(quarter, width, True)),
            (ids, row_spec(quarter, 1, False)),
            (ids, row_spec(quarter, 1, True)),
        ],
        [(shape((quarter, width), BF), None)] * 2
        + [(shape((quarter, width), F32), held(quarter, width)), (shape((quarter, width), F32), None)],
        scalar=core,
    )


def pack_attention(w_query, w_key, w_value, w_out):
    shard, width = w_out.shape
    padded = -(-shard // LANES) * LANES

    def body(q_ref, k_ref, v_ref, o_ref, out_ref):
        for i, ref in enumerate((q_ref, k_ref, v_ref, o_ref)):
            out_ref[i * padded : i * padded + shard] = ref[...].astype(BF)
            out_ref[i * padded + shard : (i + 1) * padded] = jnp.zeros((padded - shard, width), BF)

    full = pl.BlockSpec((shard, width), lambda i: (0, 0))
    return launch(
        body,
        "pack_attention",
        [(w_query.T, full), (w_key.T, full), (w_value.T, full), (w_out, full)],
        [(shape((4 * padded, width), BF), None)],
    )[0]


def pack_mlp(w_fc1, w_fc2):
    rows, columns = w_fc1.shape

    def body(up_ref, down_ref, up_out, down_out):
        at = step_rows(rows // 4)
        up_out[at] = up_ref[...].astype(BF)
        down_out[at] = down_ref[...].astype(BF)

    block = pl.BlockSpec((rows // 4, columns), lambda i: (i, 0))
    return launch(
        body,
        "pack_mlp",
        [(w_fc1, block), (w_fc2, block)],
        [(shape((rows, columns), BF), None)] * 2,
        grid=(4,),
    )


def project(activations, mine, pieces, weights, padded, core):
    _, quarter, width = activations.shape
    length = 4 * quarter
    columns = 3 * padded

    def body(core_ref, own, mine_ref, second, third, fourth, w_0, w_1, *outs):
        normed_ref, hat_ref, sides_ref, out_w, vec_ref, bias_ref, values = outs
        step = pl.program_id(0)
        pieces = (second, third, fourth)

        @pl.when(step == 0)
        def _():
            vec_ref[...] = mine_ref[0:6] + sum(
                to_float(ref[quarter : quarter + 6]) for ref in pieces
            )
            bias_ref[0:2] = mine_ref[6:8]
            bias_ref[2:4] = second[quarter + 6 : quarter + 8]
            out_w[0] = w_0[columns:]
            out_w[1] = w_1[columns:]
            values[...] = own[...]

        for i, piece in enumerate(pieces):

            @pl.when(step == i + 1)
            def _():
                values[...] = to_float(piece[:quarter])

        rows = step_rows(quarter)
        hat, _ = normalize(values[...])
        normed = (hat * vec_ref[0:1] + vec_ref[1:2]).astype(BF)
        normed_ref[...] = normed
        hat_ref[...] = hat.astype(BF)
        for side, w_ref in enumerate((w_0, w_1)):
            bias = bias_ref[2 * side : 2 * side + 1]
            sides_ref[side, rows] = (dot_nt(normed, w_ref[:columns]) + bias).astype(BF)

    return launch(
        body,
        "project",
        [(activations, row_spec(quarter, width, False))]
        + [(a, None) for a in (mine, *pieces, *weights)],
        [(shape((length, width), BF), by_step(quarter, width))] * 2
        + [(shape((2, length, columns), BF), None), (shape((2, padded, width), BF), None)]
        + [(shape((6, width), F32), None), (shape((4, width), F32), None)],
        grid=(4,),
        scratch=[pltpu.VMEM((quarter, width), F32)],
        scalar=core,
        flops=2 * length * width * 2 * columns,
    )


def lane_half():
    return lax.broadcasted_iota(jnp.int32, (1, LANES), 1) < HEAD_DIM


def head_place(head, first):
    block = slice((head // 2) * LANES, (head // 2 + 1) * LANES)
    return block, (first if head % 2 == 0 else ~first)


def attend(sides, marks, out_w, half_index, heads, dtype):
    _, length, columns = sides.shape
    padded, width = out_w.shape[1:]
    half = length // 2

    def body(sides, marks, w_ref, att_ref, inv_ref, e_ref, branch_ref, total_ref):
        side = pl.program_id(1)
        first = lane_half()
        here = step_rows()
        start = half_index * half + pl.program_id(0) * BLOCK
        rows = pl.ds(pl.multiple_of(start, BLOCK), BLOCK)
        mark_q = marks[rows, :LANES]
        mark_k = marks[:, LANES:]
        att = [jnp.zeros((BLOCK, LANES), F32)] * (padded // LANES)
        inv = list(att)
        for head in range(heads):
            block, lanes = head_place(head, first)
            scaled = to_float(sides[side, rows, block]) * (HEAD_DIM**-0.5 * LOG2_E)
            high = scaled.astype(BF)
            low = (scaled - to_float(high)).astype(BF)
            keys = sides[side, :, padded + block.start : padded + block.stop]
            left = jnp.concatenate(
                [jnp.where(lanes, high, mark_q), jnp.where(lanes, low, jnp.zeros_like(low))],
                axis=1,
            )
            right = jnp.concatenate([jnp.where(lanes, keys, mark_k), keys], axis=1)
            scores = dot_nt(left, right)
            exponent = jnp.exp2(scores - jnp.max(scores, axis=1, keepdims=True)).astype(BF)
            e_ref[head] = exponent
            values = sides[side, :, 2 * padded + block.start : 2 * padded + block.stop]
            both = dot_nn(exponent, jnp.concatenate([values, jnp.ones_like(values)], axis=1))
            inverse = 1.0 / both[:, LANES:]
            index = head // 2
            att[index] = jnp.where(lanes, both[:, :LANES] * inverse, att[index])
            inv[index] = jnp.where(lanes, inverse, inv[index])
        attended = jnp.concatenate(att, axis=1).astype(BF)
        att_ref[...] = attended
        inv_ref[...] = jnp.concatenate(inv, axis=1)
        part = dot_nn(attended, w_ref[side])

        @pl.when(side == 0)
        def _():
            total_ref[...] = part

        @pl.when(side == 1)
        def _():
            branch_ref[here] = (total_ref[...] + part).astype(dtype)

    block = pl.BlockSpec((None, BLOCK, padded), lambda i, j: (j, i, 0))
    return launch(
        body,
        f"attend_{half_index}",
        [(a, None) for a in (sides, marks, out_w)],
        [
            (shape((2, half, padded), BF), block),
            (shape((2, half, padded), F32), block),
            (
                shape((2 * heads, half, length), BF),
                pl.BlockSpec((heads, BLOCK, length), lambda i, j: (j, i, 0)),
            ),
            (shape((half, width), dtype), None),
        ],
        grid=(half // BLOCK, 2),
        scratch=[pltpu.VMEM((BLOCK, width), F32)],
        flops=8 * 2 * heads * half * length * 256,
        exps=2 * heads * half * length,
        limit=16,
    )


def second_norm(activations, core_piece, branch, received, vectors, core):
    half, width = branch.shape
    quarter = half // 2
    size = quarter // 2

    def body(core_ref, own, core_piece, branch_ref, recv_ref, vec, middle_ref, normed_ref, values):
        step = pl.program_id(0)
        here = step_rows(size)

        @pl.when(step < 2)
        def _():
            values[...] = own[...]

        @pl.when(step >= 2)
        def _():
            values[...] = core_piece[pl.ds(pl.multiple_of((step - 2) * size, size), size)]

        middle = values[...] + (branch_ref[here] + to_float(recv_ref[here]) + vec[2:3])
        middle_ref[...] = middle
        hat, _ = normalize(middle)
        normed_ref[here] = (hat * vec[3:4] + vec[4:5]).astype(BF)

    own_spec = pl.BlockSpec((None, size, width), lambda i, c: (c[0], jnp.minimum(i, 1), 0))
    return launch(
        body,
        "second_norm",
        [(activations, own_spec)] + [(a, None) for a in (core_piece, branch, received, vectors)],
        [(shape((half, width), F32), by_step(size, width)), (shape((half, width), BF), None)],
        grid=(4,),
        scratch=[pltpu.VMEM((size, width), F32)],
        scalar=core,
    )


def stack_weights(own, partner):
    def body(*refs):
        refs[4][0], refs[4][1] = refs[0][...], refs[1][...]
        refs[5][0], refs[5][1] = refs[2][...], refs[3][...]

    return launch(
        body,
        "stack_weights",
        [(a, None) for pair in zip(own, partner) for a in pair],
        [(shape((2, *a.shape), BF), None) for a in own],
    )


def mlp(normed, grad, ups, downs, bias, half_index, dtype, previous):
    rows, width = normed.shape
    hidden_size = ups.shape[2]

    def body(n_ref, g_0, g_1, up, down, bias, *rest):
        act_ref, hid_ref, out_ref, grad_ref, sum_ref, *totals = rest[len(previous) :]
        side = pl.program_id(1)
        start = half_index * rows + pl.program_id(0) * BLOCK
        shared = pl.ds(pl.multiple_of(start, BLOCK), BLOCK)

        @pl.when((pl.program_id(0) == 0) & (side == 0))
        def _():
            sum_ref[...] = jnp.zeros_like(sum_ref)

        here = step_rows()
        grad_rows = jnp.where(pl.program_id(0) == 0, g_0[...].astype(BF), g_1[...].astype(BF))
        normed_rows = n_ref[here]
        hidden = dot_nn(normed_rows, up[side]) + jnp.where(side == 0, bias[1:2], bias[3:4])
        grad_act = dot_nt(grad_rows, down[side])
        square = hidden * hidden
        th = jnp.tanh(hidden * (GELU_A + GELU_A * GELU_B * square))
        gate = 0.5 + 0.5 * th
        act = (hidden * gate).astype(BF)
        slope = gate + (0.5 * hidden) * (1.0 - th * th) * (GELU_A + 3.0 * GELU_A * GELU_B * square)
        grad_hidden = (grad_act * slope).astype(BF)
        act_ref[side, shared] = act
        hid_ref[side, shared] = grad_hidden
        sum_ref[side] += column_sum(grad_hidden)
        out = dot_nn(act, down[side])
        grad_in = dot_nt(grad_hidden, up[side])

        if dtype == F32:

            @pl.when(side == 0)
            def _():
                out_ref[...] = out
                grad_ref[...] = grad_in

            @pl.when(side == 1)
            def _():
                out_ref[...] += out
                grad_ref[...] += grad_in

        else:

            @pl.when(side == 0)
            def _():
                totals[0][...] = out
                totals[1][...] = grad_in

            @pl.when(side == 1)
            def _():
                out_ref[here] = (totals[0][...] + out).astype(dtype)
                grad_ref[here] = (totals[1][...] + grad_in).astype(dtype)

    return launch(
        body,
        f"mlp_{half_index}",
        [(a, None) for a in (normed, *grad, ups, downs, bias, *previous)],
        [(shape((2, 2 * rows, hidden_size), BF), None)] * 2
        + [(shape((rows, width), dtype), by_step(BLOCK, width) if dtype == F32 else None)] * 2
        + [(shape((2, 1, hidden_size), F32), None)],
        grid=(rows // BLOCK, 2),
        scratch=[] if dtype == F32 else [pltpu.VMEM((BLOCK, width), F32)] * 2,
        aliases={6 + i: i for i in range(len(previous))},
        flops=8 * rows * width * 2 * hidden_size,
        exps=rows * 2 * hidden_size,
        limit=12,
    )


def second_norm_back(middle, grad, received, grad_own, grad_partner, vectors):
    quarter, width = grad_own.shape
    size = quarter // 2

    def body(
        middle_ref, grad_ref, recv_ref, own, partner, vec, out_ref, first, second, sum_ref, values
    ):
        step = pl.program_id(0)
        here = step_rows(size)

        @pl.when(step < 2)
        def _():
            values[...] = own[...]

        @pl.when(step >= 2)
        def _():
            values[...] = partner[pl.ds(pl.multiple_of((step - 2) * size, size), size)]

        hat, inverse = normalize(middle_ref[...])
        incoming = grad_ref[...] + to_float(recv_ref[here])
        out = values[...] + norm_back(incoming * vec[3:4], hat, inverse)
        branch = out.astype(BF)
        out_ref[...] = out
        for i, ref in enumerate((first, second)):

            @pl.when(step // 2 == i)
            def _():
                ref[pl.ds(pl.multiple_of((step % 2) * size, size), size)] = branch

        sums = jnp.concatenate(
            [
                column_sum(incoming * hat),
                column_sum(incoming),
                column_sum(branch),
                column_sum(values[...].astype(BF)),
            ],
            axis=0,
        )

        @pl.when(step == 0)
        def _():
            sum_ref[...] = sums

        @pl.when(step > 0)
        def _():
            sum_ref[...] += sums

    dims = (2 * quarter, width)
    own_spec = pl.BlockSpec((size, width), lambda i: (jnp.minimum(i, 1), 0))
    return launch(
        body,
        "second_norm_back",
        [(middle, by_step(size, width)), (grad, by_step(size, width)), (received, None)]
        + [(grad_own, own_spec), (grad_partner, None), (vectors, None)],
        [
            (shape(dims, F32), by_step(size, width)),
            (shape((quarter, width), BF), None),
            (shape((quarter, width), BF), None),
            (shape((4, width), F32), None),
        ],
        grid=(4,),
        scratch=[pltpu.VMEM((size, width), F32)],
    )


def mlp_weight_grads(normed, grads, activated, hidden):
    rows, width = normed[0].shape
    size = hidden.shape[2]

    def body(n_0, n_1, g_0, g_1, g_2, g_3, act_ref, hid_ref, *outs):
        kept_ref, sent_refs = outs[0], outs[1:]
        side = 1 - pl.program_id(0)
        first, second = slice(0, rows), slice(rows, 2 * rows)
        up = dot_tn(n_0[...], hid_ref[side, first]) + dot_tn(n_1[...], hid_ref[side, second])
        down, at = None, rows // 2
        for i, ref in enumerate((g_0, g_1, g_2, g_3)):
            part = dot_tn(act_ref[side, i * at : (i + 1) * at], ref[...].astype(BF))
            down = part if down is None else down + part

        @pl.when(side == 0)
        def _():
            kept_ref[:width] = up.astype(BF)
            kept_ref[width:] = down.astype(BF)

        @pl.when(side == 1)
        def _():
            for i, ref in enumerate(sent_refs):
                at = (i % 2) * (width // 2)
                ref[...] = (up, down)[i // 2][at : at + width // 2].astype(BF)

    dims = (width + size, width)
    piece = (width // 2, width)
    return launch(
        body,
        "mlp_weight_grads",
        [(a, None) for a in (*normed, *grads, activated, hidden)],
        [(shape(dims, BF), None)] + [(shape(piece, BF), None)] * 4,
        grid=(2,),
        flops=16 * rows * width * size,
        limit=14,
    )


def attend_back(
    grads, out_w, attended, inverse, exponent, sides, first, block_index, heads, previous, last
):
    _, length, columns = sides.shape
    padded = columns // 3
    quarter, width = grads[0].shape
    count = len(grads)

    def body(*refs):
        grad_refs = refs[:count]
        w_ref, at_ref, inv_ref, sides, e_ref = refs[count : count + 5]
        dq_ref, dk_sum, dv_sum, *rounded = refs[count + 5 + len(previous) :]
        step, side = pl.program_id(0), pl.program_id(1)
        rows = pl.ds(pl.multiple_of((first + step) * quarter, quarter), quarter)

        if not previous:

            @pl.when(step == 0)
            def _():
                dk_sum[side] = jnp.zeros((length, padded), F32)
                dv_sum[side] = jnp.zeros((length, padded), F32)

        head_lanes = lane_half()
        lane = lax.broadcasted_iota(jnp.int32, (1, LANES), 1)
        zero = jnp.zeros((), BF)
        grad_rows = grad_refs[0][...]
        if count == 2:
            grad_rows = jnp.where(step == 0, grad_rows, grad_refs[1][...])
        grad_att = to_float(dot_nt(grad_rows, w_ref[side]).astype(BF))
        scaled = (grad_att * inv_ref[...]).astype(BF)
        product = to_float(scaled) * to_float(at_ref[...])
        dq = [None] * (padded // LANES)
        for head in range(heads):
            block, lanes = head_place(head, head_lanes)
            keys = sides[side, :, padded + block.start : padded + block.stop]
            values = sides[side, :, 2 * padded + block.start : 2 * padded + block.stop]
            grad_head = jnp.where(lanes, scaled[:, block], zero)
            centre = -jnp.sum(jnp.where(lanes, product[:, block], 0.0), axis=1, keepdims=True)
            high = centre.astype(BF)
            low = (centre - to_float(high)).astype(BF)
            extra = jnp.where(lane == 0, high, jnp.where(lane == 1, low, zero))
            grad_probs = dot_nt(
                jnp.concatenate([grad_head, extra], axis=1),
                jnp.concatenate([values, jnp.ones_like(values)], axis=1),
            )
            probs = e_ref[head]
            grad_scores = (to_float(probs) * grad_probs).astype(BF)
            part = dot_nn(grad_scores, jnp.where(lanes, keys, zero))
            index = head // 2
            dq[index] = part if dq[index] is None else dq[index] + part
            queries = jnp.where(lanes, sides[side, rows, block], zero)
            dk_sum[side, :, block] += dot_tn(grad_scores, queries)
            dv_sum[side, :, block] += dot_tn(probs, grad_head)
        at = pl.ds(pl.multiple_of(step * quarter, quarter), quarter)
        dq_ref[side, at] = (jnp.concatenate(dq, axis=1) * HEAD_DIM**-0.5).astype(BF)

        if last:

            @pl.when(step == count - 1)
            def _():
                rounded[0][side] = (dk_sum[side] * HEAD_DIM**-0.5).astype(BF)
                rounded[1][side] = dv_sum[side].astype(BF)

    block = pl.BlockSpec((None, quarter, padded), lambda i, j: (j, block_index + i, 0))
    ins = [(a, None) for a in grads]
    ins += [(out_w, None), (attended, block), (inverse, block), (sides, None)]
    ins += [
        (exponent, pl.BlockSpec((heads, quarter, length), lambda i, j: (j, block_index + i, 0)))
    ]
    ins += [(a, None) for a in previous]
    return launch(
        body,
        f"attend_back_{first}",
        ins,
        [(shape((2, count * quarter, padded), BF), None)]
        + [(shape((2, length, padded), F32), None)] * 2
        + ([(shape((2, length, padded), BF), None)] * 2 if last else []),
        grid=(count, 2),
        aliases={count + 5 + i: 1 + i for i in range(len(previous))},
        flops=16 * 2 * heads * count * quarter * length * 256,
        limit=18,
    )


def input_grad(queries, keys, values, weights, hat, half_index, dtype):
    half = hat.shape[0] // 2
    width, padded = hat.shape[1], keys.shape[2]
    count = len(queries)
    size = half // count

    def body(*refs):
        query_refs = refs[:count]
        k_ref, v_ref, w_0, w_1, hat_ref, out_ref, sum_ref = refs[count:]
        sums = None
        for i, q_ref in enumerate(query_refs):
            at = slice(i * size, (i + 1) * size)
            rows = slice(half_index * half + i * size, half_index * half + (i + 1) * size)
            total = None
            for side, w_ref in enumerate((w_0, w_1)):
                left = jnp.concatenate([q_ref[side], k_ref[side, rows], v_ref[side, rows]], axis=1)
                part = dot_nn(left, w_ref[: 3 * padded])
                total = part if total is None else total + part
            out_ref[at] = total.astype(dtype)
            part = [column_sum(total * to_float(hat_ref[at])), column_sum(total)]
            part = jnp.concatenate(part, axis=0)
            sums = part if sums is None else sums + part
        sum_ref[...] = sums

    return launch(
        body,
        f"input_grad_{half_index}",
        [(a, None) for a in (*queries, keys, values, *weights)]
        + [(hat, pl.BlockSpec((half, width), lambda i: (half_index, 0)))],
        [
            (shape((half, width), dtype), held(half, width) if dtype == F32 else None),
            (shape((2, width), F32), None),
        ],
        flops=2 * half * 6 * padded * width,
    )


def attention_weight_grad(attended, grads, queries, keys, values, normed, shard, side):
    length, width = normed.shape
    padded = keys.shape[2]
    half, quarter = length // 2, length // 4

    def body(*refs):
        at_refs, grad_refs, query_refs = refs[:2], refs[2:6], refs[6:9]
        k_ref, v_ref, n_ref, *outs = refs[9:]
        out_w = None
        for i, ref in enumerate(grad_refs):
            rows = slice((i % 2) * quarter, (i % 2 + 1) * quarter)
            part = dot_tn(at_refs[i // 2][rows], ref[...])
            out_w = part if out_w is None else out_w + part
        query, at = None, 0
        for ref in query_refs:
            rows = ref[side]
            part = dot_tn(rows, n_ref[at : at + rows.shape[0]])
            query, at = part if query is None else query + part, at + rows.shape[0]
        key = dot_tn(k_ref[side], n_ref[...])
        value = dot_tn(v_ref[side], n_ref[...])
        for i, part in enumerate((out_w, query, key, value)):
            if side:
                outs[i][...] = part[:shard].astype(BF)
            else:
                outs[0][i * shard : (i + 1) * shard] = part[:shard].astype(BF)

    at_spec = pl.BlockSpec((None, half, padded), lambda i: (side, 0, 0))
    dims = (4 * shard, width)
    return launch(
        body,
        ("attention_kept", "attention_sent")[side],
        [(a, at_spec) for a in attended]
        + [(a, None) for a in (*grads, *queries, keys, values)]
        + [(normed, held(*normed.shape))],
        [(shape((shard, width), BF), None)] * 4 if side else [(shape(dims, BF), None)],
        flops=2 * length * 4 * padded * width,
        limit=14,
    )


def small_grads(norms, lates, queries, values, up_sums):
    width = lates[0].shape[1]
    padded = values.shape[2]
    split = len(norms), len(lates), len(queries), 1, len(up_sums)

    def body(*refs):
        groups, at = [], 0
        for n in split:
            groups.append(refs[at : at + n])
            at += n
        norms, lates, queries, (v_ref,), ups = groups
        wide_ref, bias_ref = refs[at:]
        wide = [sum(ref[...] for ref in norms), sum(ref[...] for ref in lates)]
        wide_ref[...] = jnp.concatenate(wide, axis=0).astype(BF)
        for side in range(2):
            bias = [
                sum(column_sum(ref[side]) for ref in queries),
                column_sum(v_ref[side]),
                jnp.zeros((1, width - 2 * padded), F32),
            ]
            both = [jnp.concatenate(bias, axis=1), sum(ref[side] for ref in ups)]
            bias_ref[2 * side : 2 * side + 2] = jnp.concatenate(both, axis=0)

    return launch(
        body,
        "small_grads",
        [(a, None) for a in (*norms, *lates, *queries, values, *up_sums)],
        [(shape((6, width), BF), None), (shape((4, width), F32), None)],
    )


def small_chip(wide, received, bias):
    width = wide.shape[1]

    def body(wide_ref, recv_ref, bias_ref, own_ref, sent_ref):
        total = to_float(wide_ref[...]) + to_float(recv_ref[...])
        own_ref[...] = jnp.concatenate([total, bias_ref[0:2]], axis=0)
        sent_ref[...] = jnp.concatenate([total, bias_ref[2:4]], axis=0)

    return launch(
        body,
        "small_chip",
        [(wide, None), (received, None), (bias, None)],
        [(shape((8, width), F32), None)] * 2,
    )


def small_sum(own, received):
    def body(own_ref, recv_ref, out_ref):
        out_ref[...] = (own_ref[...] + recv_ref[...]).astype(BF)

    return launch(
        body, "small_sum", [(own, None), (received, None)], [(shape(own.shape, BF), None)]
    )[0]


def home_spec(quarter, width):
    return pl.BlockSpec((None, quarter, width), lambda i, c: (c[0], 0, 0))


def first_norm_back(activations, core_piece, grad_middle, grad, received, vectors, core):
    half, width = grad.shape
    quarter = half // 2

    def body(core_ref, own, core_piece, middle_ref, grad_ref, recv_ref, vec, home_ref, sent_ref):
        for i, piece in enumerate((own, core_piece)):
            rows = slice(i * quarter, (i + 1) * quarter)
            hat, inverse = normalize(piece[:quarter])
            incoming = grad_ref[rows] + to_float(recv_ref[rows])
            out = middle_ref[rows] + norm_back(incoming * vec[0:1], hat, inverse)
            (home_ref, sent_ref)[i][...] = out

    return launch(
        body,
        "first_norm_back",
        [(activations, row_spec(quarter, width, False)), (core_piece, None)]
        + [(grad_middle, held(half, width)), (grad, held(half, width))]
        + [(received, None), (vectors, None)],
        [
            (shape((2, quarter, width), F32), home_spec(quarter, width)),
            (shape((quarter, width), F32), None),
        ],
        scalar=core,
    )


def finish_output(middle, out, received, vectors, core):
    half, width = middle.shape
    quarter = half // 2

    def body(core_ref, middle_ref, out_ref, recv_ref, vec, home_ref, sent_ref):
        total = middle_ref[...] + (out_ref[...] + to_float(recv_ref[...]) + vec[5:6])
        home_ref[...] = total[:quarter]
        sent_ref[...] = total[quarter:]

    return launch(
        body,
        "finish_output",
        [(middle, held(half, width)), (out, held(half, width)), (received, None), (vectors, None)],
        [
            (shape((2, quarter, width), F32), home_spec(quarter, width)),
            (shape((quarter, width), F32), None),
        ],
        scalar=core,
    )


def swap(values, axis, size, bit):
    return lax.ppermute(values, axis, [(i, i ^ bit) for i in range(size)])


def core_swap(values):
    return swap(values, "group", 4, 1)


def chip_swap(values):
    return swap(values, "group", 4, 2)


def diagonal_swap(values):
    return swap(values, "group", 4, 3)


def divide(kept, received, mine, count):
    rows, width = kept.shape
    part = rows // count
    total = len(received)

    def body(mine_ref, kept_ref, *refs):
        recv_refs, out_refs = refs[:total], refs[total:]
        for k in range(count):
            at = pl.ds(pl.multiple_of((mine_ref[0] ^ k) * part, 8), part)
            value = to_float(kept_ref[at])
            for ref in recv_refs:
                value = value + to_float(ref[at])
            out_refs[k][...] = value.astype(BF)

    return launch(
        body,
        "divide",
        [(kept, held(rows, width))] + [(a, None) for a in received],
        [(shape((part, width), BF), held(part, width))] + [(shape((part, width), BF), None)] * (count - 1),
        scalar=mine,
    )


def divide_first(kept, pieces, mine):
    rows, width = kept.shape
    part, size = rows // 2, rows // 4

    def body(mine_ref, kept_ref, p_0, p_1, p_2, p_3, own_ref, sent_ref):
        for k, out_ref in enumerate((own_ref, sent_ref)):
            which = mine_ref[0] ^ k
            for j, (low, high) in enumerate(((p_0, p_2), (p_1, p_3))):
                at = pl.ds(pl.multiple_of(which * part + j * size, 8), size)
                got = jnp.where(which == 0, to_float(low[...]), to_float(high[...]))
                out_ref[j * size : (j + 1) * size] = (to_float(kept_ref[at]) + got).astype(BF)

    return launch(
        body,
        "divide",
        [(a, None) for a in (kept, *pieces)],
        [(shape((part, width), BF), held(part, width)), (shape((part, width), BF), None)],
        scalar=mine,
    )


def add_all(kept, received, extra):
    rows, width = kept.shape
    below = extra.shape[0] if extra is not None else 0

    def body(kept_ref, *refs):
        out_ref = refs[-1]
        value = to_float(kept_ref[...])
        for ref in refs[: len(received)]:
            value = value + to_float(ref[...])
        out_ref[:rows] = value.astype(BF)
        if below:
            out_ref[rows:] = refs[-2][...]

    return launch(
        body,
        "add_all",
        [(kept, held(rows, width))]
        + [(a, None) for a in received]
        + ([(extra, None)] if below else []),
        [(shape((rows + below, width), BF), None)],
    )[0]


def join(parts, mine, extra):
    rows, width = parts[0].shape
    part, count = rows - extra, len(parts)

    def body(mine_ref, *refs):
        out_ref = refs[-1]
        for k in range(count):
            at = pl.ds(pl.multiple_of((mine_ref[0] ^ k) * part, 8), part)
            out_ref[at] = refs[k][:part]
        if extra:
            out_ref[count * part :] = sum(to_float(ref[part:]) for ref in refs[:-1]).astype(BF)

    return launch(
        body,
        "join",
        [(a, None) for a in parts],
        [(shape((count * part + extra, width), BF), None)],
        scalar=mine,
    )[0]


def join_weights(parts, mine, shard, extra):
    rows, width = parts[0].shape
    part, count = rows - extra, len(parts)

    def body(mine_ref, *refs):
        total, outs = refs[-1], refs[count : count + 5]
        for k in range(count):
            at = pl.ds(pl.multiple_of((mine_ref[0] ^ k) * part, 8), part)
            total[at] = to_float(refs[k][:part])
        for i in range(4):
            outs[i][...] = total[i * shard : (i + 1) * shard]
        outs[4][...] = sum(to_float(ref[part:]) for ref in refs[:count])

    return launch(
        body,
        "join_weights",
        [(a, None) for a in parts],
        [(shape((shard, width), F32), held(shard, width))] * 4 + [(shape((extra, width), F32), None)],
        scratch=[pltpu.VMEM((count * part, width), F32)],
        scalar=mine,
    )


def join_mlp(parts, mine):
    def body(mine_ref, first_ref, second_ref, up_ref, down_ref):
        for ref, which in ((first_ref, mine_ref[0]), (second_ref, 1 - mine_ref[0])):
            for index, out_ref in enumerate((up_ref, down_ref)):

                @pl.when(which == index)
                def _():
                    out_ref[...] = to_float(ref[...])

    dims = parts[0].shape
    return launch(
        body,
        "join_mlp",
        [(a, None) for a in parts],
        [(shape(dims, F32), held(*dims))] * 2,
        scalar=mine,
    )


class ReplicaSum:
    def __init__(self, kept, received, size, first, others):
        self.kept, self.received, self.size = kept, received, size
        self.groups, bit, bits = [], 1, size.bit_length() - 1
        while bit < size:
            take = min(first if bit == 1 else others, bits)
            self.groups.append((bit, 1 << take))
            bit, bits = bit << take, bits - take
        self.at, self.rows = 0, None

    def mine(self):
        bit, count = self.groups[self.at]
        return (lax.axis_index("replica") // bit) % count

    def exchange(self, values, k):
        bit, _ = self.groups[self.at]
        return swap(values, "replica", self.size, k * bit)

    def divide(self):
        _, count = self.groups[self.at]
        mine = self.mine().astype(jnp.int32)
        part = self.kept.shape[0] // count
        if self.at == 0:
            parts = divide_first(self.kept, self.received, mine.reshape(1))
        elif part % 8 == 0:
            parts = divide(self.kept, self.received, mine.reshape(1), count)
        else:
            value = to_float(self.kept)
            for received in self.received:
                value = value + to_float(received)
            parts = [
                lax.dynamic_slice_in_dim(value, (mine ^ k) * part, part, 0).astype(BF)
                for k in range(count)
            ]
        self.kept, self.sent = parts[0], parts[1:]

    def send(self):
        self.received = [self.exchange(a, k + 1) for k, a in enumerate(self.sent)]
        self.at += 1

    def scatter(self):
        self.divide()
        self.send()

    def total(self, extra=None):
        while self.at < len(self.groups):
            self.scatter()
        self.extra = 0 if extra is None else extra.shape[0]
        self.rows = add_all(self.kept, self.received, extra)

    def collect(self):
        self.at -= 1
        _, count = self.groups[self.at]
        self.parts = [self.rows] + [self.exchange(self.rows, k) for k in range(1, count)]

    def combine(self, final=None):
        mine = self.mine().astype(jnp.int32)
        part = self.parts[0].shape[0] - self.extra
        if final is not None:
            self.rows = final(self.parts, mine.reshape(1))
            return
        if part % 8 == 0:
            self.rows = join(self.parts, mine.reshape(1), self.extra)
            return
        width = self.parts[0].shape[1]
        value = jnp.zeros((len(self.parts) * part, width), BF)
        for k, a in enumerate(self.parts):
            value = lax.dynamic_update_slice(value, a[:part], ((mine ^ k) * part, 0))
        below = sum(to_float(a[part:]) for a in self.parts).astype(BF)
        self.rows = jnp.concatenate([value, below], axis=0)


def per_device(
    replicas,
    activations,
    out_grad,
    picture_ids,
    ln1_gain,
    ln1_bias,
    w_query,
    q_bias,
    w_key,
    w_value,
    v_bias,
    w_out,
    out_bias,
    ln2_gain,
    ln2_bias,
    w_fc1,
    fc1_bias,
    w_fc2,
    fc2_bias,
):
    ORDER.clear()
    row_block, quarter, width = activations.shape
    assert row_block == 2
    shard = w_query.shape[1]
    heads = shard // HEAD_DIM
    padded = -(-shard // LANES) * LANES
    half = 2 * quarter
    group = lax.axis_index("group")
    core_index = group % 2
    core = core_index.astype(jnp.int32).reshape(1)

    small = jnp.concatenate(
        [ln1_gain, ln1_bias, out_bias, ln2_gain, ln2_bias, fc2_bias, q_bias, v_bias, fc1_bias]
    ).reshape(-1, shard)
    position = jnp.stack([core_index, group]).astype(jnp.int32)
    to_chip, to_diagonal, to_core, mine = split_inputs(
        activations, small, position, shard, padded
    )
    from_chip, from_diagonal = chip_swap(to_chip), diagonal_swap(to_diagonal)
    core_piece = core_swap(to_core)

    packed = pack_attention(w_query, w_key, w_value, w_out)
    w_att = packed, core_swap(packed)
    own_ids = lax.dynamic_slice_in_dim(picture_ids, group * quarter, quarter, 1)[..., None]
    grad_to_chip, grad_to_diagonal, grad_own, grad_to_core = split_grads(out_grad, own_ids, core)
    grad_core = core_swap(grad_to_core)
    grad_far = chip_swap(grad_to_chip), diagonal_swap(grad_to_diagonal)
    grad_near = grad_to_chip, grad_core
    up_own, down_own = pack_mlp(w_fc1, w_fc2)
    up_core, down_core = core_swap(up_own), core_swap(down_own)

    row_ids = lax.dynamic_index_in_dim(picture_ids, core_index, 0, keepdims=False)
    row_ids = row_ids.reshape(4, quarter)
    ids = jnp.concatenate(
        [lax.dynamic_index_in_dim(row_ids, group ^ i, 0, keepdims=False) for i in range(4)]
    )
    lane = jnp.arange(2 * LANES)
    same = ids[:, None] == (lane % HEAD_DIM - 1)[None, :]
    marks = jnp.where(
        lane[None, :] < LANES, jnp.where(same, 0.0, 1.0), jnp.where(same, MASKED, 0.0)
    ).astype(BF)

    normed_one, hat_one, sides, out_w, vectors, bias = project(
        activations, mine, (core_piece, from_chip, from_diagonal), w_att, padded, core
    )
    att_1, inv_1, exp_1, branch_1 = attend(sides, marks, out_w, 1, heads, BF)
    branch_received = chip_swap(branch_1)
    att_0, inv_0, exp_0, branch_0 = attend(sides, after(marks, *grad_far), out_w, 0, heads, F32)
    ups, downs = stack_weights((up_own, down_own), (up_core, down_core))
    middle, normed_own = second_norm(
        activations, core_piece, branch_0, branch_received, vectors, core
    )
    normed_two = normed_own, chip_swap(normed_own)

    activated, hidden, mlp_0, back_0, up_sum_0 = mlp(
        normed_two[0], grad_near, ups, downs, bias, 0, F32, ()
    )
    activated, hidden, mlp_1, back_1, up_sum_1 = mlp(
        normed_two[1], grad_far, ups, downs, bias, 1, BF, (activated, hidden)
    )
    grad_received = chip_swap(back_1)

    state = {}

    def advance(name):
        pending = state[name]
        if pending.rows is None and pending.at < len(pending.groups):
            pending.scatter()
        elif pending.rows is None:
            pending.total(state["small"] if name == "a" else None)
            pending.collect()
        elif pending.at > 0:
            pending.combine()
            pending.collect()

    def attention_grads(side):
        return attention_weight_grad(
            (att_0, att_1),
            (*state["branch"], *branches_far),
            (dq_0, *dq_1),
            state["dk"],
            state["dv"],
            normed_one,
            shard,
            side,
        )

    branches_far, dq_1 = [], []
    for token in SEQUENCE:
        if token == "W":
            kept, *sent = mlp_weight_grads(normed_two, grad_near + grad_far, activated, hidden)
            received = [core_swap(piece) for piece in sent]
            state["m"] = ReplicaSum(kept, received, replicas, *MLP_GROUPS)
        elif token == "R":
            state["out"] = chip_swap(after(mlp_1, ORDER[0]))
        elif token == "N":
            grad_middle, *branch, late_sums = second_norm_back(
                middle, back_0, grad_received, grad_own, grad_core, vectors
            )
            state["branch"] = branch
            branches_far.extend(chip_swap(piece) for piece in branch)
        elif token == "B0":
            dq_0, *key_sums = attend_back(
                state["branch"], out_w, att_0, inv_0, exp_0, sides, 0, 0, heads, (), False
            )
        elif token == "B2":
            dq, *key_sums = attend_back(
                branches_far[:1], out_w, att_1, inv_1, exp_1, sides, 2, 0, heads, key_sums, False
            )
            dq_1.append(dq)
        elif token == "B3":
            dq, _, _, state["dk"], state["dv"] = attend_back(
                branches_far[1:], out_w, att_1, inv_1, exp_1, sides, 3, 1, heads, key_sums, True
            )
            dq_1.append(dq)
        elif token == "A1":
            state["sent"] = [core_swap(piece) for piece in attention_grads(1)]
        elif token == "A0":
            state["a"] = ReplicaSum(attention_grads(0)[0], state["sent"], replicas, *ATT_GROUPS)
        elif token == "I1":
            first_1, norm_1 = input_grad(dq_1, state["dk"], state["dv"], w_att, hat_one, 1, BF)
            if RS4_EARLY:
                first_received = chip_swap(first_1)
        elif token == "I0":
            first_0, norm_0 = input_grad([dq_0], state["dk"], state["dv"], w_att, hat_one, 0, F32)
        elif token == "G":
            wide, bias_sums = small_grads(
                (norm_0, norm_1), [late_sums], (dq_0, *dq_1), state["dv"], [up_sum_0, up_sum_1]
            )
            wide_received = chip_swap(wide)
            if not RS4_EARLY:
                first_received = chip_swap(after(first_1, wide))
        elif token == "F":
            output_home, output_sent = finish_output(middle, mlp_0, state["out"], vectors, core)
            output_received = core_swap(output_sent)
        elif token == "C":
            small_own, small_sent = small_chip(wide, wide_received, bias_sums)
            small_core = core_swap(small_sent)
        elif token == "U":
            state["small"] = small_sum(small_own, small_core)
        elif token == "L":
            input_home, input_sent = first_norm_back(
                activations, core_piece, grad_middle, first_0, first_received, vectors, core
            )
            input_received = core_swap(input_sent)
        elif token == "J":
            while state["m"].rows is None or state["m"].at > 0:
                advance("m")
            state["m"].combine(join_mlp)
        else:
            advance(token)
    while state["a"].rows is None or state["a"].at > 0:
        advance("a")
    if "J" not in SEQUENCE:
        while state["m"].rows is None or state["m"].at > 0:
            advance("m")
        state["m"].combine(join_mlp)
    state["a"].combine(lambda parts, mine: join_weights(parts, mine, shard, 8))
    weights, small = state["a"].rows[:4], state["a"].rows[4]
    mlp_sum = state["m"]

    def place(home, received):
        return lax.dynamic_update_slice(home, received[None], (1 - core_index, 0, 0))

    mine = lax.dynamic_slice_in_dim(small[:6], group * shard, shard, 1)

    return (
        place(output_home, output_received),
        place(input_home, input_received),
        mine[0],
        mine[1],
        weights[1].T,
        small[6, :shard],
        weights[2].T,
        weights[3].T,
        small[6, padded : padded + shard],
        weights[0],
        mine[4],
        mine[2],
        mine[3],
        mlp_sum.rows[0],
        small[7],
        mlp_sum.rows[1],
        mine[5],
    )


def solution(mesh):
    replicas = mesh.shape["replica"]
    assert mesh.shape["group"] == 4
    patches = P("replica", "group", None)
    vector = P("group")
    columns = P(None, "group")
    rows = P("group", None)
    parameters = (vector, vector, columns, vector, columns, columns, vector, rows)
    parameters += (vector, vector, vector, columns, vector, rows, vector)

    def program(*arguments):
        return per_device(replicas, *arguments)

    return jax.shard_map(
        program,
        mesh=mesh,
        in_specs=(patches, patches, P("replica", None)) + parameters,
        out_specs=(patches, patches) + parameters,
        check_vma=False,
    )
```
